32 devices in a mesh: dp: 4 (over y, x), fsdp: 8 (over z, core).
Axes of the slice: x: 2, y: 2, z: 4, core: 2. Of those that a mesh axis runs over, the one named last changes fastest.
Arguments:
- step_count: int32 [1], replicated, may hold values from 2 to 20
- token_ids: int32 [2, 32, 512], replicated, may hold values from 0 to 50303
- segment_ids: int32 [2, 32, 512], P(None, ('dp', 'fsdp')), may hold values from 0 to 3, never falling along the last dimension, each value on 1 to 256 neighbouring positions
- loss_positions: int32 [2, 32, 32], P(None, ('dp', 'fsdp')), may hold values from 0 to 511
- label_ids: int32 [2, 32, 32], replicated, may hold values from 0 to 50303
- label_mask: int32 [2, 32, 32], replicated, may hold values 0 or 1
- embed_in: float32 [768, 50304], P(('dp', 'fsdp')), may hold values from -6 to 6
- embed_in_first: float32 [768, 50304], P(('dp', 'fsdp')), may hold values from -8.940697e-08 to 8.940697e-08
- embed_in_second: float32 [768, 50304], P(('dp', 'fsdp')), may hold values from 4.741832e-16 to 3.9120115e-15
- embed_out: float32 [50304, 768], P(('dp', 'fsdp')), may hold values from -0.4375 to 0.4375
- embed_out_first: float32 [50304, 768], P(('dp', 'fsdp')), may hold values from -7.1525574e-07 to 7.1525574e-07
- embed_out_second: float32 [50304, 768], P(('dp', 'fsdp')), may hold values from 3.0821906e-14 to 2.4894618e-13
- proj_in: float32 [768, 2304], P(('dp', 'fsdp')), may hold values from -0.21875 to 0.21875
- proj_in_first: float32 [768, 2304], P(('dp', 'fsdp')), may hold values from -7.1525574e-07 to 7.1525574e-07
- proj_in_second: float32 [768, 2304], P(('dp', 'fsdp')), may hold values from 3.0821906e-14 to 2.4894618e-13
- proj_up: float32 [768, 3072], P(('dp', 'fsdp')), may hold values from -0.21875 to 0.21875
- proj_up_first: float32 [768, 3072], P(('dp', 'fsdp')), may hold values from -7.1525574e-07 to 7.1525574e-07
- proj_up_second: float32 [768, 3072], P(('dp', 'fsdp')), may hold values from 3.0821906e-14 to 2.4894618e-13
- proj_mix: float32 [3840, 768], P(('dp', 'fsdp')), may hold values from -0.21875 to 0.21875
- proj_mix_first: float32 [3840, 768], P(('dp', 'fsdp')), may hold values from -7.1525574e-07 to 7.1525574e-07
- proj_mix_second: float32 [3840, 768], P(('dp', 'fsdp')), may hold values from 3.0821906e-14 to 2.4894618e-13
- vector_params: float32 [10752], P(('dp', 'fsdp')), may hold values from -1.5 to 1.5, as said below
- vector_first: float32 [10752], P(('dp', 'fsdp')), may hold values from -2.861023e-06 to 2.861023e-06
- vector_second: float32 [10752], P(('dp', 'fsdp')), may hold values from 4.9789236e-13 to 4.030557e-12
- basis_in: bfloat16 [768, 768], replicated, may hold values from -0.21875 to 0.21875
- basis_out: bfloat16 [3072, 3072], replicated, may hold values from -0.109375 to 0.109375
Outputs:
- new_embed_in: float32 [768, 50304], P(('dp', 'fsdp'))
- next_embed_in_first: float32 [768, 50304], P(('dp', 'fsdp'))
- next_embed_in_second: float32 [768, 50304], P(('dp', 'fsdp'))
- new_embed_out: float32 [50304, 768], P(('dp', 'fsdp'))
- next_embed_out_first: float32 [50304, 768], P(('dp', 'fsdp'))
- next_embed_out_second: float32 [50304, 768], P(('dp', 'fsdp'))
- new_proj_in: float32 [768, 2304], P(('dp', 'fsdp'))
- next_proj_in_first: float32 [768, 2304], P(('dp', 'fsdp'))
- next_proj_in_second: float32 [768, 2304], P(('dp', 'fsdp'))
- new_proj_up: float32 [768, 3072], P(('dp', 'fsdp'))
- next_proj_up_first: float32 [768, 3072], P(('dp', 'fsdp'))
- next_proj_up_second: float32 [768, 3072], P(('dp', 'fsdp'))
- new_proj_mix: float32 [3840, 768], P(('dp', 'fsdp'))
- next_proj_mix_first: float32 [3840, 768], P(('dp', 'fsdp'))
- next_proj_mix_second: float32 [3840, 768], P(('dp', 'fsdp'))
- new_vector_params: float32 [10752], P(('dp', 'fsdp'))
- next_vector_first: float32 [10752], P(('dp', 'fsdp'))
- next_vector_second: float32 [10752], P(('dp', 'fsdp'))
- loss_value: float32 [], replicated
- grad_norm: float32 [], replicated
- eigen_scales: float32 [768, 3072], P(('dp', 'fsdp'))
The draws below stay inside these ranges and needn't reach their ends.
Inputs may be any that keep to these rules, and one draw needn't show every extreme that they name: `segment_ids`: within a row the ids never fall; a document has at most 256 positions. `vector_params`: the first 8448 entries are biases, the last 2304 are gains between 0.7 and 1.3.
All inputs are finite; a program needn't handle non-finite values.
Results may differ from the reference program's by a relative error of at most 0.0055.
The reference program's roundings to bfloat16 on the way count: a program that leaves them out, or rounds other values in their place, can miss the bound.
Values may be sent and summed in bfloat16 or wider, within the bound.
No kernel may reach another device: no remote copies, remote signals or barrier semaphores. Data moves between devices by JAX's collectives and lax.ppermute only.
A program may use at most 384 MiB of HBM per device.

```python
import math
import jax
import jax.numpy as jnp
import numpy as np
from jax import lax

D = 768
FF = 3072
HEADS = 12
V = 50304
ROT = 16
DOCS = 4
SEQ = 512
PICK = 32
MICRO = 2
ROWS = 32
SMALL = 10752
PARAMS = 84355584


def draw_vector_params(key, part):
    key_bias, key_gain = jax.random.split(key)
    biases = jnp.clip(0.3 * jax.random.normal(key_bias, (7 * D + FF,), jnp.float32), -1.5, 1.5)
    gains = jax.random.uniform(key_gain, (3 * D,), jnp.float32, 0.7, 1.3)
    return jnp.concatenate([biases, gains])


def with_ends(drawn, key, smallest, top_value):
    shape = drawn.shape
    index_at = [jax.random.randint(jax.random.fold_in(key, axis), (), 0, shape[axis]) for axis in range(len(shape))]
    drawn = drawn.at[tuple(index_at)].set(smallest)
    longest = shape.index(max(shape))
    index_at[longest] = (index_at[longest] + 1) % shape[longest]
    return drawn.at[tuple(index_at)].set(top_value)


def steps_of(rng, extent, cuts, low, top_value):
    loudness, own = 1.0, jax.random.fold_in(rng, 6)
    for position, shards_of in cuts:
        steps = jnp.exp(jax.random.uniform(jax.random.fold_in(own, position), (shards_of,), jnp.float32, low / len(cuts), top_value / len(cuts)))
        loudness = loudness * jnp.repeat(steps, extent[position] // shards_of).reshape([-1 if axis == position else 1 for axis in range(len(extent))])
    return loudness


def rank_table(count, lean):
    weights = [(1 << 20) // math.isqrt(rank ** lean) + 1 for rank in range(1, count + 1)]
    scale = 1 + sum(weights) // (1 << 30)
    return np.cumsum(np.array([max(1, weight // scale) for weight in weights]))


def skewed_ids(rng, extent, count, lean):
    listing = rank_table(count, lean)
    ticket = jax.random.randint(jax.random.fold_in(rng, 1), extent, 0, int(listing[count - 1]))
    rank = jnp.searchsorted(jnp.asarray(listing, jnp.int32), ticket, side="right")
    return jax.random.permutation(jax.random.fold_in(rng, 2), count)[rank].astype(jnp.int32)


def split_up(amount, total, most, slope):
    loads = [(1 << 20) // math.isqrt(rank ** slope) + 1 for rank in range(2, amount + 1)]
    rest, counts = total - most - (amount - 1), [1] * (amount - 1)
    while rest > 0:
        free = [i for i in range(amount - 1) if counts[i] < most]
        whole, remaining = sum([loads[i] for i in free]), rest
        for i in free:
            addition = min(most - counts[i], max(1, remaining * loads[i] // whole), rest)
            counts[i] = counts[i] + addition
            rest = rest - addition
    return np.array([most] + counts)


def ragged(own_key, count, total, bound, skew):
    if count == 2:
        one = jax.random.randint(own_key, (), max(1, total - bound), min(bound, total - 1) + 1)
        return jnp.stack([one, total - one])
    sizes = jnp.asarray(split_up(count, total, bound, skew), jnp.int32)
    pairs = (count - 1) // 2
    donor, taker = sizes[1:1 + 2 * pairs:2], sizes[2:2 + 2 * pairs:2]
    margin = jnp.minimum(donor - 1, bound - taker)
    passed = jax.random.randint(jax.random.fold_in(own_key, 1), (pairs,), 0, 1 << 20) % (margin + 1)
    sizes = sizes.at[1:1 + 2 * pairs:2].set(donor - passed).at[2:2 + 2 * pairs:2].set(taker + passed)
    return sizes[jax.random.permutation(jax.random.fold_in(own_key, 2), count)]


def scatter_about(stream_key, dims, scale, limit, cuts=(), kind=jnp.bfloat16):
    loudness = steps_of(stream_key, dims, cuts, -0.22, 0.18) if cuts else 1.0
    values = jax.random.normal(stream_key, dims, jnp.float32) * scale * loudness
    return jnp.minimum(jnp.maximum(values, -limit), limit).astype(kind)


def setup_inputs(seed: int = 0) -> dict:
    streams_of = jax.random.split(jax.random.key(seed), 27)
    return {
        "step_count": jax.random.randint(streams_of[0], (1,), 2, 21).astype(jnp.int32),
        "token_ids": with_ends(skewed_ids(streams_of[1], (MICRO, ROWS, SEQ), V, 2), jax.random.fold_in(streams_of[1], 3), 0, V - 1).astype(jnp.int32),
        "segment_ids": jax.vmap(lambda own: jnp.searchsorted(jnp.cumsum(ragged(own, DOCS, SEQ, SEQ // 2, 2)), jnp.arange(SEQ), side="right"))(jax.random.split(streams_of[2], MICRO * ROWS)).reshape((MICRO, ROWS, SEQ)).astype(jnp.int32),
        "loss_positions": with_ends(jax.random.randint(streams_of[3], (MICRO, ROWS, PICK), 0, SEQ), jax.random.fold_in(streams_of[3], 1), 0, SEQ - 1).astype(jnp.int32),
        "label_ids": with_ends(jax.random.randint(streams_of[4], (MICRO, ROWS, PICK), 0, V), jax.random.fold_in(streams_of[4], 1), 0, V - 1).astype(jnp.int32),
        "label_mask": with_ends((jax.random.randint(streams_of[5], (MICRO, ROWS, PICK), 0, 4) < 3).astype(jnp.int32), jax.random.fold_in(streams_of[5], 1), 0, 1),
        "embed_in": scatter_about(streams_of[6], (D, V), 1.0, 6.0, ((0, 32),), jnp.float32),
        "embed_in_first": scatter_about(streams_of[7], (D, V), (0.000139 * PARAMS ** -0.5), 8.940696716308594e-08, ((0, 32),), jnp.float32),
        "embed_in_second": jnp.clip(jnp.exp(math.log(3.912011502498619e-15) - 2.1102133 * jax.random.uniform(streams_of[8], (D, V), jnp.float32) ** steps_of(streams_of[8], (D, V), ((0, 32),), -0.2, 0.2)), 4.741831787352646e-16, 3.912011502498619e-15),
        "embed_out": scatter_about(streams_of[9], (V, D), (2.0 * D ** -0.5), 0.4375, ((0, 32),), jnp.float32),
        "embed_out_first": scatter_about(streams_of[10], (V, D), (0.00111 * PARAMS ** -0.5), 7.152557373046875e-07, ((0, 32),), jnp.float32),
        "embed_out_second": jnp.clip(jnp.exp(math.log(2.489461815944477e-13) - 2.089011 * jax.random.uniform(streams_of[11], (V, D), jnp.float32) ** steps_of(streams_of[11], (V, D), ((0, 32),), -0.2, 0.2)), 3.082190603545705e-14, 2.489461815944477e-13),
        "proj_in": scatter_about(streams_of[12], (D, 3 * D), D ** -0.5, 0.21875, ((0, 32),), jnp.float32),
        "proj_in_first": scatter_about(streams_of[13], (D, 3 * D), (0.00111 * PARAMS ** -0.5), 7.152557373046875e-07, ((0, 32),), jnp.float32),
        "proj_in_second": jnp.clip(jnp.exp(math.log(2.489461815944477e-13) - 2.089011 * jax.random.uniform(streams_of[14], (D, 3 * D), jnp.float32) ** steps_of(streams_of[14], (D, 3 * D), ((0, 32),), -0.2, 0.2)), 3.082190603545705e-14, 2.489461815944477e-13),
        "proj_up": scatter_about(streams_of[15], (D, FF), D ** -0.5, 0.21875, ((0, 32),), jnp.float32),
        "proj_up_first": scatter_about(streams_of[16], (D, FF), (0.00111 * PARAMS ** -0.5), 7.152557373046875e-07, ((0, 32),), jnp.float32),
        "proj_up_second": jnp.clip(jnp.exp(math.log(2.489461815944477e-13) - 2.089011 * jax.random.uniform(streams_of[17], (D, FF), jnp.float32) ** steps_of(streams_of[17], (D, FF), ((0, 32),), -0.2, 0.2)), 3.082190603545705e-14, 2.489461815944477e-13),
        "proj_mix": scatter_about(streams_of[18], (D + FF, D), D ** -0.5, 0.21875, ((0, 32),), jnp.float32),
        "proj_mix_first": scatter_about(streams_of[19], (D + FF, D), (0.00111 * PARAMS ** -0.5), 7.152557373046875e-07, ((0, 32),), jnp.float32),
        "proj_mix_second": jnp.clip(jnp.exp(math.log(2.489461815944477e-13) - 2.089011 * jax.random.uniform(streams_of[20], (D + FF, D), jnp.float32) ** steps_of(streams_of[20], (D + FF, D), ((0, 32),), -0.2, 0.2)), 3.082190603545705e-14, 2.489461815944477e-13),
        "vector_params": draw_vector_params(jax.random.fold_in(streams_of[26], 71), 0),
        "vector_first": scatter_about(streams_of[22], (SMALL,), (0.00444 * PARAMS ** -0.5), 2.86102294921875e-06, ((0, 32),), jnp.float32),
        "vector_second": jnp.clip(jnp.exp(math.log(4.03055713804612e-12) - 2.091276 * jax.random.uniform(streams_of[23], (SMALL,), jnp.float32) ** steps_of(streams_of[23], (SMALL,), ((0, 32),), -0.2, 0.2)), 4.978923631888954e-13, 4.03055713804612e-12),
        "basis_in": scatter_about(streams_of[24], (D, D), D ** -0.5, 0.21875),
        "basis_out": scatter_about(streams_of[25], (FF, FF), FF ** -0.5, 0.109375),
    }


@jax.custom_vjp
def low(v):
    return lax.optimization_barrier(v.astype(jnp.bfloat16)).astype(jnp.float32)

@jax.custom_vjp
def low_back(v):
    return v

def low_keep(v):
    return (low(v), None)

def low_pass(kept, grad):
    return (grad,)

def back_keep(v):
    return (v, None)

def back_low(kept, grad):
    return (low(grad),)
low.defvjp(low_keep, low_pass)
low_back.defvjp(back_keep, back_low)
highest = lax.Precision.HIGHEST
clip_limit = 0.01
decay_first = 0.9
decay_second = 0.95
adam_epsilon = 1e-08
weight_decay = 0.01
step_rates = (1.0, 0.07, 0.04, 0.04, 0.04, 0.3)

def product(left, right):
    return jnp.dot(left, right, precision=highest)

def split_vector(vector):
    lengths = (3 * D, FF, D, D, D, D, D, D, D)
    pieces = []
    offset = 0
    for length in lengths:
        pieces.append(vector[offset:offset + length])
        offset = offset + length
    return pieces

def rotary_tables(row_length):
    halfway = ROT // 2
    inverse = 10000.0 ** (-2.0 * jnp.arange(halfway, dtype=jnp.float32) / ROT)
    angles = jnp.arange(row_length, dtype=jnp.float32)[:, None] * inverse[None, :]
    return (jnp.concatenate([jnp.cos(angles)] * 2, 1), jnp.concatenate([jnp.sin(angles)] * 2, 1))

def turn(values_in, cosine_table, sine_table):
    halfway = ROT // 2
    rotated = values_in[..., :ROT]
    lower_half = rotated[..., :halfway]
    upper_half = rotated[..., halfway:]
    swapped = jnp.concatenate([-upper_half, lower_half], -1)
    moved = rotated * cosine_table[:, None, :] + swapped * sine_table[:, None, :]
    return jnp.concatenate([moved, values_in[..., ROT:]], -1)

def normalize(inputs):
    centred = inputs - lax.optimization_barrier(jnp.mean(inputs, 1, keepdims=True))
    return centred * lax.rsqrt(lax.optimization_barrier(jnp.mean(centred * centred, 1, keepdims=True)) + 1e-05)

def second_input(lowered, row_ids):
    pieces = split_vector(lowered[5])
    embedded = jnp.take(lowered[0], row_ids, axis=1).T
    return low(normalize(embedded) * pieces[7] + pieces[4])

def row_loss(lowered, item, total):
    table_in, table_out, proj_in, proj_up, proj_mix, vector = lowered
    row_ids, row_segments, row_picks, row_labels, row_mask, probe_row = item
    bias_in, bias_up, bias_mix, shift_first, shift_second, shift_last, gain_first, gain_second, gain_last = split_vector(vector)
    row_length = row_ids.shape[0]
    head_width = D // HEADS
    embedded = low_back(jnp.take(table_in, row_ids, axis=1).T)
    normed = normalize(embedded)
    first_in = low(normed * gain_first + shift_first)
    second_in = low(normed * gain_second + shift_second)
    mixed = low_back(product(first_in, proj_in) + bias_in).reshape(row_length, 3, HEADS, head_width)
    cosine_table, sine_table = rotary_tables(row_length)
    queries = low(turn(mixed[:, 0], cosine_table, sine_table))
    keys_all = low(turn(mixed[:, 1], cosine_table, sine_table))
    values_all = low(mixed[:, 2])
    scores = jnp.einsum('qhd,khd->hqk', queries, keys_all, precision=highest)
    scores = low_back(scores * (1.0 / math.sqrt(head_width)))
    places = jnp.arange(row_length)
    allowed = (places[None, :] <= places[:, None]) & (row_segments[None, :] == row_segments[:, None])
    scores = jnp.where(allowed[None], scores, -1e+30)
    weights_soft = jax.nn.softmax(scores, axis=-1)
    context = jnp.einsum('hqk,khd->qhd', low(weights_soft), values_all, precision=highest).reshape(row_length, D)
    hidden_pre = low_back(product(second_in, proj_up) + bias_up + probe_row)
    joined = jnp.concatenate([low(low_back(context)), low(jax.nn.gelu(hidden_pre, approximate=False))], 1)
    residual = embedded + low_back(product(joined, proj_mix)) + bias_mix
    final = normalize(residual) * gain_last + shift_last
    picked = low(jnp.take(final, row_picks, axis=0))
    logits = low_back(product(picked, table_out.T))
    logsum = jax.nn.logsumexp(logits, axis=-1)
    target = jnp.take_along_axis(logits, row_labels[:, None], axis=1)[:, 0]
    return jnp.sum(row_mask * (logsum - target)) / total

def adam_update(weight, gradient, moment_one, moment_two, rate, step_value):
    next_one = decay_first * moment_one + (1.0 - decay_first) * gradient
    next_two = decay_second * moment_two + (1.0 - decay_second) * gradient * gradient
    fix_one = 1.0 - decay_first ** step_value
    fix_two = 1.0 - decay_second ** step_value
    update = next_one / fix_one / (jnp.sqrt(next_two / fix_two) + adam_epsilon)
    return [weight - rate * (update + weight_decay * weight), next_one, next_two]

def reference(step_count, token_ids, segment_ids, loss_positions, label_ids, label_mask, embed_in, embed_in_first, embed_in_second, embed_out, embed_out_first, embed_out_second, proj_in, proj_in_first, proj_in_second, proj_up, proj_up_first, proj_up_second, proj_mix, proj_mix_first, proj_mix_second, vector_params, vector_first, vector_second, basis_in, basis_out):
    weights = (embed_in, embed_out, proj_in, proj_up, proj_mix, vector_params)
    total = jnp.maximum(jnp.sum(label_mask.astype(jnp.float32)), 1.0)
    flat_tokens = token_ids.reshape(MICRO * ROWS, SEQ)
    flat_segments = segment_ids.reshape(MICRO * ROWS, SEQ)
    probe = jnp.zeros((MICRO * ROWS, SEQ, FF), jnp.float32)
    row_step = jax.checkpoint(row_loss)

    def loss_of(*params):
        lowered = tuple((low(param_value) for param_value in params[:6]))
        items = (flat_tokens, flat_segments, loss_positions.reshape(MICRO * ROWS, PICK), label_ids.reshape(MICRO * ROWS, PICK), label_mask.reshape(MICRO * ROWS, PICK).astype(jnp.float32), params[6])

        def scan_step(carry, item):
            return (carry + row_step(lowered, item, total), None)
        result, unused = lax.scan(scan_step, jnp.zeros((), jnp.float32), items)
        return result
    loss_value, pull_back = jax.vjp(loss_of, *weights, probe)
    all_grads = pull_back(jnp.ones((), jnp.float32))
    grads = all_grads[:6]
    hidden_grads = all_grads[6]
    lowered_now = tuple((low(weight) for weight in weights))
    rotate_in = basis_in.astype(jnp.float32)
    rotate_out = basis_out.astype(jnp.float32)

    def scale_step(carry, item):
        row_ids, row_segments, row_grad = item
        rot_in = low(product(second_input(lowered_now, row_ids), rotate_in))
        rot_out = low(product(row_grad, rotate_out))
        docs = (row_segments[None, :] == jnp.arange(DOCS)[:, None]).astype(jnp.float32)
        masked = docs[:, :, None] * rot_in[None]
        blocks = low(total * jnp.einsum('nsa,sb->nab', masked, rot_out, precision=highest))
        return (carry + lax.optimization_barrier(jnp.sum(blocks * blocks, 0)), None)
    scale_sum, unused = lax.scan(scale_step, jnp.zeros((D, FF), jnp.float32), (flat_tokens, flat_segments, hidden_grads))
    eigen_scales = scale_sum / float(MICRO * ROWS * DOCS)
    squares = sum((jnp.sum(gradient * gradient) for gradient in grads))
    grad_norm = jnp.sqrt(squares)
    factor = jnp.minimum(1.0, clip_limit / (grad_norm + 1e-06))
    step_value = step_count[0].astype(jnp.float32)
    firsts = (embed_in_first, embed_out_first, proj_in_first, proj_up_first, proj_mix_first, vector_first)
    seconds = (embed_in_second, embed_out_second, proj_in_second, proj_up_second, proj_mix_second, vector_second)
    outputs = []
    for weight, gradient, moment_one, moment_two, rate in zip(weights, grads, firsts, seconds, step_rates):
        outputs.extend(adam_update(weight, gradient * factor, moment_one, moment_two, rate, step_value))
    return (outputs[0], outputs[1], outputs[2], outputs[3], outputs[4], outputs[5], outputs[6], outputs[7], outputs[8], outputs[9], outputs[10], outputs[11], outputs[12], outputs[13], outputs[14], outputs[15], outputs[16], outputs[17], loss_value, grad_norm, eigen_scales)
```

```python
import math

import jax
import jax.numpy as jnp
from jax import lax
from jax.experimental import pallas as pl
from jax.experimental.pallas import tpu as pltpu
from jax.sharding import PartitionSpec as P

HEADS = 12
ROT = 16
DOCS = 4


half_type = jnp.bfloat16
full_type = jnp.float32
clip_limit = 0.01
decay_first = 0.9
decay_second = 0.95
adam_epsilon = 1e-08
weight_decay = 0.01
step_rates = (1.0, 0.07, 0.04, 0.04, 0.04, 0.3)


def split_vector(vector, width, hidden):
    lengths = (3 * width, hidden, width, width, width, width, width, width, width)
    pieces = []
    offset = 0
    for length in lengths:
        pieces.append(vector[offset : offset + length])
        offset = offset + length
    return pieces


def normalize(inputs):
    centred = inputs - jnp.mean(inputs, 1, keepdims=True)
    inv_std = lax.rsqrt(jnp.mean(centred * centred, 1, keepdims=True) + 1e-05)
    return (centred * inv_std, inv_std)


def norm_back(grad_out, normed, inv_std):
    return inv_std * (
        grad_out
        - jnp.mean(grad_out, 1, keepdims=True)
        - normed * jnp.mean(grad_out * normed, 1, keepdims=True)
    )


def gelu_slope(inputs):
    return 0.5 * (1.0 + lax.erf(inputs * (1.0 / math.sqrt(2.0)))) + inputs * jnp.exp(
        -0.5 * inputs * inputs
    ) * (1.0 / math.sqrt(2.0 * math.pi))


LANES = 128


def lane_pack(width):
    pad = 8
    while pad < width:
        pad *= 2
    return (pad, LANES // pad)


def copies_matrix(width, dtype):
    pad, _ = lane_pack(width)
    feature = lax.broadcasted_iota(jnp.int32, (width, LANES), 0)
    lane = lax.broadcasted_iota(jnp.int32, (width, LANES), 1)
    return jnp.where(lane % pad == feature, 1.0, 0.0).astype(dtype)


def gather_kernel(ids_ref, table_ref, out_ref, rows_ref, stage_ref):
    width, vocab = table_ref.shape
    tokens = ids_ref.shape[2]
    pad, groups = lane_pack(width)
    stride = tokens // groups

    @pl.when(pl.program_id(0) == 0)
    def _():
        spread = copies_matrix(width, half_type)
        step = 3 * LANES if vocab % (3 * LANES) == 0 else LANES

        def build(chunk, carry):
            start = pl.multiple_of(chunk * step, LANES)
            piece = table_ref[:, pl.ds(start, step)].astype(half_type)
            rows_ref[pl.ds(start, step), :] = lax.dot_general(
                piece, spread, (((0,), (0,)), ((), ())), preferred_element_type=full_type
            )
            return carry

        lax.fori_loop(0, vocab // step, build, 0)

    lane_group = lax.broadcasted_iota(jnp.int32, (1, LANES), 1) // pad
    unroll = 8

    def pick(block, carry):
        base = block * unroll
        for inner in range(unroll):
            row = None
            for group in range(groups):
                found = rows_ref[pl.ds(ids_ref[0, 0, group * stride + base + inner], 1), :]
                row = found if row is None else jnp.where(lane_group == group, found, row)
            stage_ref[pl.ds(base + inner, 1), :] = row
        return carry

    lax.fori_loop(0, stride // unroll, pick, 0)
    turned = jnp.transpose(stage_ref[...])
    for group in range(groups):
        out_ref[0, :, group * stride : (group + 1) * stride] = turned[
            group * pad : group * pad + width, :
        ].astype(half_type)


def gather_features(table, ids):
    width, vocab = table.shape
    count, _, tokens = ids.shape
    _, groups = lane_pack(width)
    return pl.pallas_call(
        gather_kernel,
        out_shape=jax.ShapeDtypeStruct((count, width, tokens), half_type),
        grid=(count,),
        in_specs=[
            pl.BlockSpec((1, 1, tokens), lambda i: (i, 0, 0), memory_space=pltpu.SMEM),
            pl.BlockSpec((width, vocab), lambda i: (0, 0), pipeline_mode=pl.Buffered(1)),
        ],
        out_specs=pl.BlockSpec((1, width, tokens), lambda i: (i, 0, 0)),
        scratch_shapes=[
            pltpu.VMEM((vocab, LANES), full_type),
            pltpu.VMEM((tokens // groups, LANES), full_type),
        ],
        compiler_params=pltpu.CompilerParams(
            dimension_semantics=("arbitrary",), vmem_limit_bytes=44 * 1024 * 1024
        ),
    )(ids, table)


def quarter(vocab, groups):
    return -(-vocab // (groups * LANES)) * LANES


def scatter_kernel(places_ref, grad_ref, out_ref, square_ref, mask_ref, stage_ref, *sums):
    width, vocab = out_ref.shape
    runs, _, tokens = places_ref.shape
    pad, groups = lane_pack(width)
    shift = groups.bit_length() - 1
    span = quarter(vocab, groups)

    @pl.when(pl.program_id(0) == 0)
    def _():
        lane_group = lax.broadcasted_iota(jnp.int32, mask_ref.shape, 1) // pad
        mask_ref[...] = jnp.where(
            lane_group == lax.broadcasted_iota(jnp.int32, mask_ref.shape, 0), 1.0, 0.0
        )

        def clear(block, carry):
            start = pl.multiple_of(block * LANES, LANES)
            for total in sums:
                total[pl.ds(start, LANES), :] = jnp.zeros((LANES, LANES), full_type)
            return carry

        lax.fori_loop(0, span // LANES, clear, 0)

    spread = copies_matrix(width, half_type)
    for run in range(runs):
        stage_ref[run] = lax.dot_general(
            grad_ref[run], spread, (((0,), (0,)), ((), ())), preferred_element_type=full_type
        )
    unroll = 4

    def add(block, carry):
        base = block * unroll
        for inner in range(unroll):
            for run in range(runs):
                place = places_ref[run, 0, base + inner]
                row = pl.ds(place >> shift, 1)
                group = pl.ds(place & (groups - 1), 1)
                sums[run][row, :] = (
                    sums[run][row, :] + stage_ref[run, pl.ds(base + inner, 1), :] * mask_ref[group, :]
                )
        return carry

    lax.fori_loop(0, tokens // unroll, add, 0)

    @pl.when(pl.program_id(0) == pl.num_programs(0) - 1)
    def _():
        def finish(block, squares):
            start = pl.multiple_of(block * LANES, LANES)
            whole = sums[0][pl.ds(start, LANES), :]
            for total in sums[1:]:
                whole = whole + total[pl.ds(start, LANES), :]
            turned = jnp.transpose(whole)
            for group in range(groups):
                column = pl.multiple_of(group * span + start, LANES)

                @pl.when(column < vocab)
                def _():
                    out_ref[:, pl.ds(column, LANES)] = turned[group * pad : group * pad + width, :]

            return squares + jnp.sum((whole * whole).reshape(LANES // 8, 8, LANES), 0)

        square_ref[...] = lax.fori_loop(0, span // LANES, finish, jnp.zeros((8, LANES), full_type))


def scatter_features(grads, places, vocab):
    count, width, tokens = grads.shape
    pad, groups = lane_pack(width)
    runs = 4
    return pl.pallas_call(
        scatter_kernel,
        out_shape=(
            jax.ShapeDtypeStruct((width, vocab), full_type),
            jax.ShapeDtypeStruct((8, LANES), full_type),
        ),
        grid=(count // runs,),
        in_specs=[
            pl.BlockSpec((runs, 1, tokens), lambda i: (i, 0, 0), memory_space=pltpu.SMEM),
            pl.BlockSpec((runs, width, tokens), lambda i: (i, 0, 0)),
        ],
        out_specs=(
            pl.BlockSpec((width, vocab), lambda i: (0, 0)),
            pl.BlockSpec((8, LANES), lambda i: (0, 0)),
        ),
        scratch_shapes=[
            pltpu.VMEM((max(8, groups), LANES), full_type),
            pltpu.VMEM((runs, tokens, LANES), full_type),
        ]
        + [pltpu.VMEM((quarter(vocab, groups), LANES), full_type) for _ in range(runs)],
        compiler_params=pltpu.CompilerParams(
            dimension_semantics=("arbitrary",), vmem_limit_bytes=52 * 1024 * 1024
        ),
    )(places, grads)


def scatter_places(ids, width, vocab):
    _, groups = lane_pack(width)
    span = quarter(vocab, groups)
    return (ids % span) * groups + ids // span


def turn_tables(row_length, head_width):
    halfway = ROT // 2
    dims = jnp.arange(LANES) % head_width
    inverse = 10000.0 ** (-2.0 * (dims % halfway).astype(full_type) / ROT)
    angles = jnp.arange(row_length, dtype=full_type)[:, None] * inverse[None, :]
    cosine = jnp.where(dims < ROT, jnp.cos(angles), 1.0)
    above = jnp.where(dims < halfway, -jnp.sin(angles), 0.0)
    below = jnp.where((dims >= halfway) & (dims < ROT), jnp.sin(angles), 0.0)
    return jnp.stack([cosine, above, below], 0)


def turned(values_in, tables_ref, forward):
    halfway = ROT // 2
    higher = pltpu.roll(values_in, LANES - halfway, 1) * tables_ref[1]
    lower = pltpu.roll(values_in, halfway, 1) * tables_ref[2]
    straight = values_in * tables_ref[0]
    return straight + (higher + lower) if forward else straight - (higher + lower)


def dot_of(left, right, dims):
    return lax.dot_general(left, right, (dims, ((), ())), preferred_element_type=full_type)


def key_window(block, block_rows):
    return (block + 1) * block_rows


def allowed_block(row_ref, column_ref, block, block_rows):
    reach = key_window(block, block_rows)
    start = block * block_rows
    key_place = lax.broadcasted_iota(jnp.int32, (reach, block_rows), 0)
    query_place = start + lax.broadcasted_iota(jnp.int32, (reach, block_rows), 1)
    same = column_ref[0, :reach, :] == row_ref[0, :, start : start + block_rows]
    return (key_place <= query_place) & same


def forward_kernel(
    query_in, key_in, value_in, tables_ref, row_ref, column_ref, context_ref, query_ref, key_ref, value_ref, logsum_ref
):
    row_length = query_in.shape[0]
    head_width = LANES // 2
    block_rows = row_length // 2
    scale = 1.0 / math.sqrt(head_width)
    query_ref[...] = turned(query_in[...], tables_ref, True).astype(half_type)
    key_ref[...] = turned(key_in[...], tables_ref, True).astype(half_type)
    value_ref[...] = value_in[...].astype(half_type)
    for block in range(2):
        start = block * block_rows
        reach = key_window(block, block_rows)
        allowed = allowed_block(row_ref, column_ref, block, block_rows)
        for head in range(2):
            lanes = slice(head * head_width, (head + 1) * head_width)
            scores = dot_of(key_ref[:reach, lanes], query_ref[start : start + block_rows, lanes], ((1,), (1,)))
            scores = jnp.where(allowed, scores * scale, -1e30)
            peak = jnp.max(scores, 0, keepdims=True)
            powers = jnp.exp(scores - peak)
            total = jnp.sum(powers, 0, keepdims=True)
            logsum_ref[0, 0, head : head + 1, start : start + block_rows] = peak + jnp.log(total)
            weights_soft = (powers * (1.0 / total)).astype(half_type)
            context_ref[start : start + block_rows, lanes] = dot_of(
                weights_soft, value_ref[:reach, lanes], ((0,), (0,))
            ).astype(half_type)


def attention_specs(row_length, pairs):
    def part(offset):
        return pl.BlockSpec((row_length, LANES), lambda m, h: (m, offset * pairs + h))

    tables = pl.BlockSpec((3, row_length, LANES), lambda m, h: (0, 0, 0))
    row = pl.BlockSpec((1, 1, row_length), lambda m, h: (m, 0, 0))
    column = pl.BlockSpec((1, row_length, 1), lambda m, h: (m, 0, 0))
    logsum = pl.BlockSpec((1, 1, 2, row_length), lambda m, h: (m, h, 0, 0))
    return (part, tables, row, column, logsum)


def attention_forward(mixed, tables, segments):
    micro_count, row_length = segments.shape
    tokens = mixed.shape[0]
    width = mixed.shape[1] // 3
    pairs = width // LANES
    part, tables_spec, row, column, logsum = attention_specs(row_length, pairs)
    flat = jax.ShapeDtypeStruct((tokens, width), half_type)
    return pl.pallas_call(
        forward_kernel,
        out_shape=(flat, flat, flat, flat, jax.ShapeDtypeStruct((micro_count, pairs, 2, row_length), full_type)),
        grid=(micro_count, pairs),
        in_specs=[part(0), part(1), part(2), tables_spec, row, column],
        out_specs=(part(0), part(0), part(0), part(0), logsum),
        compiler_params=pltpu.CompilerParams(
            dimension_semantics=("arbitrary", "arbitrary"), vmem_limit_bytes=40 * 1024 * 1024
        ),
    )(mixed, mixed, mixed, tables, segments[:, None, :], segments[:, :, None])


def backward_kernel(
    query_ref, key_ref, value_ref, grad_ref, tables_ref, row_ref, column_ref, logsum_ref, out_ref, query_sum, key_sum, value_sum
):
    row_length = query_ref.shape[0]
    head_width = LANES // 2
    block_rows = row_length // 2
    scale = 1.0 / math.sqrt(head_width)
    for block in reversed(range(2)):
        start = block * block_rows
        reach = key_window(block, block_rows)
        rows = slice(start, start + block_rows)
        allowed = allowed_block(row_ref, column_ref, block, block_rows)
        for head in range(2):
            lanes = slice(head * head_width, (head + 1) * head_width)
            query = query_ref[rows, lanes]
            key = key_ref[:reach, lanes]
            grad = grad_ref[rows, lanes]
            scores = jnp.where(allowed, dot_of(key, query, ((1,), (1,))) * scale, -1e30)
            weights_soft = jnp.exp(scores - logsum_ref[0, 0, head : head + 1, rows])
            grad_value = dot_of(weights_soft.astype(half_type), grad, ((1,), (0,)))
            grad_weights = dot_of(value_ref[:reach, lanes], grad, ((1,), (1,)))
            leaning = jnp.sum(weights_soft * grad_weights, 0, keepdims=True)
            grad_scores = (weights_soft * (grad_weights - leaning)).astype(half_type)
            query_sum[rows, lanes] = dot_of(grad_scores, key, ((0,), (0,))) * scale
            grad_key = dot_of(grad_scores, query, ((1,), (0,))) * scale
            if block == 1:
                value_sum[:, lanes] = grad_value
                key_sum[:, lanes] = grad_key
            else:
                value_sum[:reach, lanes] = value_sum[:reach, lanes] + grad_value
                key_sum[:reach, lanes] = key_sum[:reach, lanes] + grad_key
    out_ref[0] = turned(query_sum[...], tables_ref, False).astype(half_type)
    out_ref[1] = turned(key_sum[...], tables_ref, False).astype(half_type)
    out_ref[2] = value_sum[...].astype(half_type)


def attention_backward(queries, keys_all, values_all, grad_context, logsum, tables, segments):
    micro_count, row_length = segments.shape
    tokens, width = queries.shape
    pairs = width // LANES
    part, tables_spec, row, column, logsum_spec = attention_specs(row_length, pairs)
    return pl.pallas_call(
        backward_kernel,
        out_shape=jax.ShapeDtypeStruct((3, tokens, width), half_type),
        grid=(micro_count, pairs),
        in_specs=[part(0), part(0), part(0), part(0), tables_spec, row, column, logsum_spec],
        out_specs=pl.BlockSpec((3, row_length, LANES), lambda m, h: (0, m, h)),
        scratch_shapes=[pltpu.VMEM((row_length, LANES), full_type) for _ in range(3)],
        compiler_params=pltpu.CompilerParams(
            dimension_semantics=("arbitrary", "arbitrary"), vmem_limit_bytes=40 * 1024 * 1024
        ),
    )(queries, keys_all, values_all, grad_context, tables, segments[:, None, :], segments[:, :, None], logsum)


def document_kernel(starts_ref, total_ref, in_ref, out_ref, sum_ref, turned_ref, spill_ref):
    micro_count, docs = starts_ref.shape[0], starts_ref.shape[1] - 1
    row_length = in_ref.shape[0] // micro_count
    reach = row_length // 2
    step = 16

    def bounds(micro, doc):
        start, end = starts_ref[micro, doc], starts_ref[micro, doc + 1]
        window = jnp.minimum((start // step) * step, row_length - reach)
        base = pl.multiple_of(micro * row_length + window, step)
        return (start - window, end - window, base)

    @pl.when(pl.program_id(0) == 0)
    def _():
        for micro in range(micro_count):
            for doc in range(docs):
                begin, end, base = bounds(micro, doc)
                place = lax.broadcasted_iota(jnp.int32, (reach, in_ref.shape[1]), 0)
                rows = in_ref[pl.ds(base, reach), :].astype(full_type)
                kept = jnp.where((place >= begin) & (place < end), rows, 0.0)
                turned_ref[micro * docs + doc] = jnp.transpose(kept).astype(half_type)

                @pl.when(end > reach)
                def _():
                    place = reach + lax.broadcasted_iota(jnp.int32, (step, in_ref.shape[1]), 0)
                    rows = in_ref[pl.ds(base + reach, step), :].astype(full_type)
                    spill_ref[micro * docs + doc] = jnp.where(place < end, rows, 0.0).astype(half_type)

    total = total_ref[0]
    for micro in range(micro_count):
        for doc in range(docs):
            begin, end, base = bounds(micro, doc)
            place = micro * docs + doc
            first = place == 0

            def add(block):
                block = (block * total).astype(half_type).astype(full_type)
                sum_ref[...] = block * block if first else sum_ref[...] + block * block

            block = dot_of(turned_ref[place], out_ref[pl.ds(base, reach), :], ((1,), (0,)))

            @pl.when(end <= reach)
            def _():
                add(block)

            @pl.when(end > reach)
            def _():
                more = dot_of(spill_ref[place], out_ref[pl.ds(base + reach, step), :], ((0,), (0,)))
                add(block + more)


def document_squares(rot_in, rot_out, segments, total):
    micro_count, row_length = segments.shape
    tokens, width = rot_in.shape
    hidden = rot_out.shape[1]
    tile = 2 * LANES
    slots = jnp.arange(DOCS + 1)
    starts = jnp.sum(segments[:, :, None] < slots[None, None, :], 1).astype(jnp.int32)
    return pl.pallas_call(
        document_kernel,
        out_shape=jax.ShapeDtypeStruct((width, hidden), full_type),
        grid=(hidden // tile,),
        in_specs=[
            pl.BlockSpec(memory_space=pltpu.SMEM),
            pl.BlockSpec(memory_space=pltpu.SMEM),
            pl.BlockSpec((tokens, width), lambda i: (0, 0)),
            pl.BlockSpec((tokens, tile), lambda i: (0, i)),
        ],
        out_specs=pl.BlockSpec((width, tile), lambda i: (0, i)),
        scratch_shapes=[
            pltpu.VMEM((micro_count * DOCS, width, row_length // 2), half_type),
            pltpu.VMEM((micro_count * DOCS, 16, width), half_type),
        ],
        compiler_params=pltpu.CompilerParams(
            dimension_semantics=("arbitrary",), vmem_limit_bytes=40 * 1024 * 1024
        ),
    )(starts, total.reshape(1), rot_in, rot_out)


AXES = ("dp", "fsdp")


def partner_pairs(count, bit):
    return [(place, place ^ (1 << bit)) for place in range(count)]


class Stream:
    def __init__(self, chunks, order, wire, relative=False):
        self.count = chunks.shape[0]
        bits = self.count.bit_length() - 1
        self.held = chunks.reshape((2,) * bits + chunks.shape[1:])
        self.left = list(order) if relative else list(range(bits - 1, -1, -1))
        self.relative = relative
        self.order = list(order)
        self.wire = wire
        self.sent = self.kept = self.got = None

    def land(self, arrived):
        self.held = self.kept + arrived.astype(full_type)
        self.got = None

    def split(self):
        bit = self.order[0]
        axis = self.left.index(bit)
        mine = 0 if self.relative else (lax.axis_index(AXES) >> bit) & 1
        self.sent = lax.dynamic_index_in_dim(self.held, 1 - mine, axis, keepdims=False)
        self.kept = lax.dynamic_index_in_dim(self.held, mine, axis, keepdims=False)
        if bit != 0:
            self.sent = self.sent.astype(self.wire)
        self.left.pop(axis)

    def send(self, ready):
        self.got = lax.ppermute(ready, AXES, partner_pairs(self.count, self.order.pop(0)))


def link_orders(bits):
    near = list(range(1, bits - 2))
    return ([0, bits - 2, bits - 1] + near, [0, bits - 1, bits - 2] + near)


def flipped(folded, place):
    bits = lax.axis_size(AXES).bit_length() - 1
    for axis in range(bits):
        mine = (place >> (bits - 1 - axis)) & 1
        folded = jnp.where(mine == 1, jnp.flip(folded, axis), folded)
    return folded


def by_device(stacked, order, place):
    bits = len(order)
    folded = stacked.reshape((2,) * bits + stacked.shape[1:])
    natural = [order.index(bit) for bit in range(bits - 1, -1, -1)]
    folded = jnp.transpose(folded, natural + list(range(bits, folded.ndim)))
    return flipped(folded, place).reshape(stacked.shape)


def by_partner(ordered, order, place):
    bits = len(order)
    folded = flipped(ordered.reshape((2,) * bits + ordered.shape[1:]), place)
    stacked = [bits - 1 - bit for bit in order]
    folded = jnp.transpose(folded, stacked + list(range(bits, folded.ndim)))
    return folded.reshape(ordered.shape)


def gather_trees(blocks, orders):
    held = [block[None] for block in blocks]
    for step in range(len(orders[0])):
        for m, order in enumerate(orders):
            count = 1 << len(order)
            arrived = lax.ppermute(held[m], AXES, partner_pairs(count, order[-1 - step]))
            held[m] = jnp.concatenate([held[m], arrived], 0)
    return held


def streams_of(full, count, wire=full_type):
    rows = full.shape[0] // count
    half = full.shape[1] // 2
    chunks = full.reshape(count, rows, full.shape[1])
    order_a, order_b = link_orders(count.bit_length() - 1)
    return [Stream(chunks[:, :, :half], order_a, wire), Stream(chunks[:, :, half:], order_b, wire)]


def advance(anchor, streams):
    flying = [stream for stream in streams if stream.got is not None]
    anchor, landed = lax.optimization_barrier((anchor, [stream.got for stream in flying]))
    for stream, arrived in zip(flying, landed):
        stream.land(arrived)
    going = [stream for stream in streams if stream.order]
    for stream in going:
        stream.split()
    anchor, ready = lax.optimization_barrier((anchor, [stream.sent for stream in going]))
    for stream, block in zip(going, ready):
        stream.send(block)
    return anchor


def finished(streams):
    return jnp.concatenate([stream.held for stream in streams], 1)


def run_all(anchor, streams):
    while any(stream.order or stream.got is not None for stream in streams):
        anchor = advance(anchor, streams)
    return anchor


def shared_by_all(own, count):
    return lax.all_to_all(
        jnp.broadcast_to(own[None], (count,) + own.shape), AXES, split_axis=0, concat_axis=0, tiled=True
    )


def adam_update(weight, gradient, moment_one, moment_two, rate, step_value):
    next_one = decay_first * moment_one + (1.0 - decay_first) * gradient
    next_two = decay_second * moment_two + (1.0 - decay_second) * gradient * gradient
    fix_one = 1.0 - decay_first**step_value
    fix_two = 1.0 - decay_second**step_value
    update = next_one / fix_one / (jnp.sqrt(next_two / fix_two) + adam_epsilon)
    return [weight - rate * (update + weight_decay * weight), next_one, next_two]


def per_device(
    step_count,
    token_ids,
    segment_ids,
    loss_positions,
    label_ids,
    label_mask,
    embed_in,
    embed_in_first,
    embed_in_second,
    embed_out,
    embed_out_first,
    embed_out_second,
    proj_in,
    proj_in_first,
    proj_in_second,
    proj_up,
    proj_up_first,
    proj_up_second,
    proj_mix,
    proj_mix_first,
    proj_mix_second,
    vector_params,
    vector_first,
    vector_second,
    basis_in,
    basis_out,
):
    micro_count = token_ids.shape[0]
    row_length = token_ids.shape[2]
    pick_count = loss_positions.shape[2]
    tokens = micro_count * row_length
    count = lax.axis_size(AXES)
    total = jnp.maximum(jnp.sum(label_mask.astype(full_type)), 1.0)
    vocab = embed_in.shape[1]
    own_width = embed_in.shape[0]
    width = proj_mix.shape[1]
    hidden = proj_up.shape[1]
    head_width = width // HEADS

    weight_in = lax.all_gather(proj_in.astype(half_type), AXES, axis=0, tiled=True)
    weight_up = lax.all_gather(proj_up.astype(half_type), AXES, axis=0, tiled=True)
    weight_mix = lax.all_gather(proj_mix.astype(half_type), AXES, axis=0, tiled=True)
    vector = shared_by_all(vector_params.astype(half_type), count).reshape(-1).astype(full_type)
    (
        bias_in,
        bias_up,
        bias_mix,
        shift_first,
        shift_second,
        shift_last,
        gain_first,
        gain_second,
        gain_last,
    ) = split_vector(vector, width, hidden)

    flat_ids = jnp.transpose(token_ids, (1, 0, 2)).reshape(-1)
    ids_by_run = flat_ids.reshape(count, 1, tokens)
    columns = gather_features(embed_in, ids_by_run)
    arrived = lax.all_to_all(columns, AXES, split_axis=0, concat_axis=0, tiled=True)
    embedded = arrived.reshape(width, tokens).T.astype(full_type)
    places = scatter_places(ids_by_run, own_width, vocab)
    segments = segment_ids[:, 0]
    picks = loss_positions[:, 0] + row_length * jnp.arange(micro_count)[:, None]
    picks = picks.reshape(-1)

    normed, inv_std = normalize(embedded)
    first_in = (normed * gain_first + shift_first).astype(half_type)
    second_in = (normed * gain_second + shift_second).astype(half_type)
    mixed = jnp.dot(first_in, weight_in, preferred_element_type=full_type) + bias_in
    tables = turn_tables(row_length, head_width)
    context, queries, keys_all, values_all, logsum = attention_forward(mixed, tables, segments)
    hidden_pre = jnp.dot(second_in, weight_up, preferred_element_type=full_type) + bias_up
    active = (hidden_pre * (0.5 + 0.5 * lax.erf(hidden_pre * (1.0 / math.sqrt(2.0))))).astype(half_type)
    joined = jnp.concatenate([context, active], 1)
    residual = embedded + jnp.dot(joined, weight_mix, preferred_element_type=full_type) + bias_mix
    normed_last, inv_last = normalize(residual)
    final = normed_last * gain_last + shift_last
    picked = jnp.take(final, picks, axis=0, mode="clip").astype(half_type)

    bits = count.bit_length() - 1
    orders = link_orders(bits)
    place = lax.axis_index(AXES)
    picked = picked.reshape(micro_count, pick_count, width)
    gathered = jnp.stack(gather_trees(picked, orders)).reshape(-1, width)
    table_out = embed_out.astype(half_type)
    vocab_rows = embed_out.shape[0]
    vocab_ids = place * vocab_rows + jnp.arange(vocab_rows)
    labels_flat = jnp.stack([by_partner(label_ids[m], orders[m], place) for m in range(micro_count)]).reshape(-1)
    mask_flat = jnp.stack([by_partner(label_mask[m], orders[m], place) for m in range(micro_count)]).reshape(-1)
    mask_flat = mask_flat.astype(full_type)
    logits = jnp.einsum("rd,vd->rv", gathered, table_out, preferred_element_type=full_type)
    matches = labels_flat[:, None] == vocab_ids[None, :]
    label_part = jnp.sum(jnp.where(matches, logits, 0.0), 1)
    local_max = jnp.max(logits, 1)
    local_sum = jnp.sum(jnp.exp(logits - local_max[:, None]), 1)
    parts = jnp.stack([local_max, local_sum, label_part], 0).reshape(3, micro_count, count, pick_count)
    parts = jnp.transpose(parts, (1, 2, 0, 3))
    parts = jnp.stack([by_device(parts[m], orders[m], place) for m in range(micro_count)], 1)
    parts = lax.all_to_all(
        parts.reshape(count, 1, -1), AXES, split_axis=0, concat_axis=0, tiled=True
    ).reshape(count, micro_count, 3, pick_count)
    peak = jnp.max(parts[:, :, 0], 0)
    own_logsum = peak + jnp.log(jnp.sum(parts[:, :, 1] * jnp.exp(parts[:, :, 0] - peak[None]), 0))
    own_mask = lax.dynamic_index_in_dim(label_mask, place, 1, keepdims=False).astype(full_type)
    loss_part = jnp.sum(own_mask * (own_logsum - jnp.sum(parts[:, :, 2], 0))) / total
    logsum_all = shared_by_all(own_logsum.reshape(1, -1), count).reshape(count, micro_count, pick_count)
    logsum_all = jnp.stack([by_partner(logsum_all[:, m], orders[m], place) for m in range(micro_count)]).reshape(-1)
    grad_logits = (
        (jnp.exp(logits - logsum_all[:, None]) - matches.astype(full_type))
        * (mask_flat / total)[:, None]
    ).astype(half_type)
    back = jnp.dot(grad_logits, table_out, preferred_element_type=full_type)
    back = back.reshape(micro_count, count, pick_count, width)
    pick_streams = [Stream(back[m], orders[m], full_type, relative=True) for m in range(micro_count)]
    grad_logits = advance(grad_logits, pick_streams)
    grad_out_table = jnp.einsum("rv,rd->vd", grad_logits, gathered, preferred_element_type=full_type)
    run_all(jnp.zeros((), full_type), pick_streams)
    grad_picked = jnp.concatenate([stream.held for stream in pick_streams], 0)

    grad_final = jnp.zeros((tokens, width), full_type).at[picks].add(grad_picked)
    grad_residual = norm_back(grad_final * gain_last, normed_last, inv_last)
    grad_branch = grad_residual.astype(half_type)
    grad_mix = jnp.einsum("sa,sb->ab", joined, grad_branch, preferred_element_type=full_type)
    mix_streams = streams_of(grad_mix, count)
    grad_branch = advance(grad_branch, mix_streams)
    grad_joined = jnp.einsum("sb,ab->sa", grad_branch, weight_mix, preferred_element_type=full_type)
    grad_context = (
        grad_joined[:, :width].astype(half_type)
    )
    grad_hidden = (grad_joined[:, width:] * gelu_slope(hidden_pre)).astype(half_type)
    grad_hidden = advance(grad_hidden, mix_streams)
    grad_up = jnp.einsum("sa,sb->ab", second_in, grad_hidden, preferred_element_type=full_type)
    grad_second = jnp.einsum("sb,ab->sa", grad_hidden, weight_up, preferred_element_type=full_type)
    up_streams = streams_of(grad_up, count)
    (grad_hidden, grad_second) = advance((grad_hidden, grad_second), mix_streams + up_streams)

    rot_in = jnp.dot(second_in, basis_in, preferred_element_type=full_type).astype(half_type)
    rot_out = jnp.dot(grad_hidden, basis_out, preferred_element_type=full_type).astype(half_type)
    (rot_in, rot_out) = advance((rot_in, rot_out), mix_streams + up_streams)
    scale_sum = document_squares(rot_in, rot_out, segments, total)
    scale_streams = streams_of(scale_sum, count, half_type)
    grad_context = advance(grad_context, mix_streams + up_streams + scale_streams)

    grad_parts = attention_backward(
        queries, keys_all, values_all, grad_context, logsum, tables, segments
    )
    grad_mixed = jnp.concatenate([grad_parts[0], grad_parts[1], grad_parts[2]], 1)
    grad_mixed = advance(grad_mixed, mix_streams + up_streams + scale_streams)
    grad_in = jnp.einsum("sa,sb->ab", first_in, grad_mixed, preferred_element_type=full_type)
    in_streams = streams_of(grad_in, count)
    grad_mixed = advance(grad_mixed, up_streams + scale_streams + in_streams)
    grad_first = jnp.einsum("sb,ab->sa", grad_mixed, weight_in, preferred_element_type=full_type)
    grad_embedded = grad_residual + norm_back(
        grad_first * gain_first + grad_second * gain_second, normed, inv_std
    )
    sending = grad_embedded.astype(half_type).T.reshape(count, own_width, tokens)
    returned = lax.all_to_all(sending, AXES, split_axis=0, concat_axis=0, tiled=True)
    vector_grad = jnp.concatenate(
        [
            jnp.sum(grad_mixed.astype(full_type), 0),
            jnp.sum(grad_hidden.astype(full_type), 0),
            jnp.sum(grad_residual, 0),
            jnp.sum(grad_first, 0),
            jnp.sum(grad_second, 0),
            jnp.sum(grad_final, 0),
            jnp.sum(grad_first * normed, 0),
            jnp.sum(grad_second * normed, 0),
            jnp.sum(grad_final * normed_last, 0),
        ]
    )
    vector_parts = lax.all_to_all(
        vector_grad.reshape(count, 1, -1), AXES, split_axis=0, concat_axis=0, tiled=True
    )
    own_vector = jnp.sum(vector_parts, (0, 1))
    late = mix_streams + up_streams + scale_streams + in_streams
    own_vector = advance(own_vector, late)
    own_vector = advance(own_vector, late)
    returned, own_vector = lax.optimization_barrier((returned, own_vector))
    grad_in_table, in_squares = scatter_features(returned, places, vocab)
    in_squares = run_all(in_squares, late)
    own_mix = finished(mix_streams)
    own_up = finished(up_streams)
    own_in = finished(in_streams)
    eigen_scales = finished(scale_streams) / float(micro_count * count * DOCS)
    grads = (grad_in_table, grad_out_table, own_in, own_up, own_mix, own_vector)
    squares = jnp.sum(in_squares) + sum((jnp.sum(gradient * gradient) for gradient in grads[1:]))
    both = jnp.sum(shared_by_all(jnp.stack([squares, loss_part])[None], count), (0, 1))
    grad_norm = jnp.sqrt(both[0])
    loss_value = both[1]
    factor = jnp.minimum(1.0, clip_limit / (grad_norm + 1e-06))
    step_value = step_count[0].astype(full_type)
    weights = (embed_in, embed_out, proj_in, proj_up, proj_mix, vector_params)
    firsts = (
        embed_in_first,
        embed_out_first,
        proj_in_first,
        proj_up_first,
        proj_mix_first,
        vector_first,
    )
    seconds = (
        embed_in_second,
        embed_out_second,
        proj_in_second,
        proj_up_second,
        proj_mix_second,
        vector_second,
    )
    results = []
    for weight, gradient, moment_one, moment_two, rate in zip(
        weights, grads, firsts, seconds, step_rates
    ):
        results.extend(
            adam_update(weight, gradient * factor, moment_one, moment_two, rate, step_value)
        )
    return tuple(results) + (loss_value, grad_norm, eigen_scales)


def solution(mesh):
    in_specs = (
        P(),
        P(),
        P(None, ("dp", "fsdp"), None),
        P(None, ("dp", "fsdp"), None),
        P(),
        P(),
        P(("dp", "fsdp"), None),
        P(("dp", "fsdp"), None),
        P(("dp", "fsdp"), None),
        P(("dp", "fsdp"), None),
        P(("dp", "fsdp"), None),
        P(("dp", "fsdp"), None),
        P(("dp", "fsdp"), None),
        P(("dp", "fsdp"), None),
        P(("dp", "fsdp"), None),
        P(("dp", "fsdp"), None),
        P(("dp", "fsdp"), None),
        P(("dp", "fsdp"), None),
        P(("dp", "fsdp"), None),
        P(("dp", "fsdp"), None),
        P(("dp", "fsdp"), None),
        P(("dp", "fsdp")),
        P(("dp", "fsdp")),
        P(("dp", "fsdp")),
        P(),
        P(),
    )
    out_specs = (
        P(("dp", "fsdp"), None),
        P(("dp", "fsdp"), None),
        P(("dp", "fsdp"), None),
        P(("dp", "fsdp"), None),
        P(("dp", "fsdp"), None),
        P(("dp", "fsdp"), None),
        P(("dp", "fsdp"), None),
        P(("dp", "fsdp"), None),
        P(("dp", "fsdp"), None),
        P(("dp", "fsdp"), None),
        P(("dp", "fsdp"), None),
        P(("dp", "fsdp"), None),
        P(("dp", "fsdp"), None),
        P(("dp", "fsdp"), None),
        P(("dp", "fsdp"), None),
        P(("dp", "fsdp")),
        P(("dp", "fsdp")),
        P(("dp", "fsdp")),
        P(),
        P(),
        P(("dp", "fsdp"), None),
    )
    return jax.shard_map(
        per_device, mesh=mesh, in_specs=in_specs, out_specs=out_specs, check_vma=False
    )
```

```python
import math

import jax
import jax.numpy as jnp
from jax import lax
from jax.experimental import pallas as pl
from jax.experimental.pallas import tpu as pltpu
from jax.sharding import PartitionSpec as P

HEADS = 12
ROT = 16
DOCS = 4


half_type = jnp.bfloat16
full_type = jnp.float32
clip_limit = 0.01
decay_first = 0.9
decay_second = 0.95
adam_epsilon = 1e-08
weight_decay = 0.01
step_rates = (1.0, 0.07, 0.04, 0.04, 0.04, 0.3)


def split_vector(vector, width, hidden):
    lengths = (3 * width, hidden, width, width, width, width, width, width, width)
    pieces = []
    offset = 0
    for length in lengths:
        pieces.append(vector[offset : offset + length])
        offset = offset + length
    return pieces


def normalize(inputs):
    centred = inputs - jnp.mean(inputs, 1, keepdims=True)
    inv_std = lax.rsqrt(jnp.mean(centred * centred, 1, keepdims=True) + 1e-05)
    return (centred * inv_std, inv_std)


def norm_back(grad_out, normed, inv_std):
    return inv_std * (
        grad_out
        - jnp.mean(grad_out, 1, keepdims=True)
        - normed * jnp.mean(grad_out * normed, 1, keepdims=True)
    )


def gelu_slope(inputs):
    return 0.5 * (1.0 + lax.erf(inputs * (1.0 / math.sqrt(2.0)))) + inputs * jnp.exp(
        -0.5 * inputs * inputs
    ) * (1.0 / math.sqrt(2.0 * math.pi))


LANES = 128


def lane_pack(width):
    pad = 8
    while pad < width:
        pad *= 2
    return (pad, LANES // pad)


def copies_matrix(width, dtype):
    pad, _ = lane_pack(width)
    feature = lax.broadcasted_iota(jnp.int32, (width, LANES), 0)
    lane = lax.broadcasted_iota(jnp.int32, (width, LANES), 1)
    return jnp.where(lane % pad == feature, 1.0, 0.0).astype(dtype)


def gather_kernel(ids_ref, table_ref, out_ref, rows_ref, stage_ref):
    width, vocab = table_ref.shape
    tokens = ids_ref.shape[2]
    pad, groups = lane_pack(width)
    stride = tokens // groups

    @pl.when(pl.program_id(0) == 0)
    def _():
        chunks = vocab // LANES
        many = 8
        filler = jnp.zeros((pad - width, LANES), full_type)

        def build(start):
            piece = table_ref[:, pl.ds(start, LANES)].astype(half_type).astype(full_type)
            tall = jnp.concatenate([piece, filler] * groups, 0) if pad > width else jnp.concatenate([piece] * groups, 0)
            rows_ref[pl.ds(start, LANES), :] = jnp.transpose(tall)

        def several(block, carry):
            for inner in range(many):
                build(pl.multiple_of((block * many + inner) * LANES, LANES))
            return carry

        lax.fori_loop(0, chunks // many, several, 0)
        for rest in range(chunks // many * many, chunks):
            build(rest * LANES)

    lane_group = lax.broadcasted_iota(jnp.int32, (1, LANES), 1) // pad
    unroll = 16

    def pick(block, carry):
        base = block * unroll
        for inner in range(unroll):
            row = None
            for group in range(groups):
                found = rows_ref[pl.ds(ids_ref[0, 0, group * stride + base + inner], 1), :]
                row = found if row is None else jnp.where(lane_group == group, found, row)
            stage_ref[pl.ds(base + inner, 1), :] = row
        return carry

    lax.fori_loop(0, stride // unroll, pick, 0)
    turned = jnp.transpose(stage_ref[...])
    for group in range(groups):
        out_ref[0, :, group * stride : (group + 1) * stride] = turned[
            group * pad : group * pad + width, :
        ].astype(half_type)


def gather_features(table, ids):
    width, vocab = table.shape
    count, _, tokens = ids.shape
    _, groups = lane_pack(width)
    return pl.pallas_call(
        gather_kernel,
        out_shape=jax.ShapeDtypeStruct((count, width, tokens), half_type),
        grid=(count,),
        in_specs=[
            pl.BlockSpec((1, 1, tokens), lambda i: (i, 0, 0), memory_space=pltpu.SMEM),
            pl.BlockSpec((width, vocab), lambda i: (0, 0), pipeline_mode=pl.Buffered(1)),
        ],
        out_specs=pl.BlockSpec((1, width, tokens), lambda i: (i, 0, 0)),
        scratch_shapes=[
            pltpu.VMEM((vocab, LANES), full_type),
            pltpu.VMEM((tokens // groups, LANES), full_type),
        ],
        compiler_params=pltpu.CompilerParams(
            dimension_semantics=("arbitrary",), vmem_limit_bytes=44 * 1024 * 1024
        ),
    )(ids, table)


def quarter(vocab, groups):
    return -(-vocab // (groups * LANES)) * LANES


def scatter_kernel(places_ref, groups_ref, grad_ref, out_ref, square_ref, mask_ref, stage_ref, *sums):
    width, vocab = out_ref.shape
    runs, _, tokens = places_ref.shape
    pad, groups = lane_pack(width)
    shift = groups.bit_length() - 1
    span = quarter(vocab, groups)

    @pl.when(pl.program_id(0) == 0)
    def _():
        lane_group = lax.broadcasted_iota(jnp.int32, mask_ref.shape, 1) // pad
        mask_ref[...] = jnp.where(
            lane_group == lax.broadcasted_iota(jnp.int32, mask_ref.shape, 0), 1.0, 0.0
        )

        def clear(block, carry):
            start = pl.multiple_of(block * LANES, LANES)
            for total in sums:
                total[pl.ds(start, LANES), :] = jnp.zeros((LANES, LANES), full_type)
            return carry

        lax.fori_loop(0, span // LANES, clear, 0)

    spread = copies_matrix(width, half_type)
    for run in range(runs):
        stage_ref[run] = lax.dot_general(
            grad_ref[run], spread, (((0,), (0,)), ((), ())), preferred_element_type=full_type
        )
    unroll = 32

    def add(block, carry):
        base = block * unroll
        for inner in range(unroll):
            rows = [pl.ds(places_ref[run, 0, base + inner], 1) for run in range(runs)]
            new = [
                sums[run][rows[run], :]
                + stage_ref[run, pl.ds(base + inner, 1), :] * mask_ref[pl.ds(groups_ref[run, 0, base + inner], 1), :]
                for run in range(runs)
            ]
            for run in range(runs):
                sums[run][rows[run], :] = new[run]
        return carry

    lax.fori_loop(0, tokens // unroll, add, 0)

    @pl.when(pl.program_id(0) == pl.num_programs(0) - 1)
    def _():
        def finish(block, squares):
            start = pl.multiple_of(block * LANES, LANES)
            whole = sums[0][pl.ds(start, LANES), :]
            for total in sums[1:]:
                whole = whole + total[pl.ds(start, LANES), :]
            turned = jnp.transpose(whole)
            for group in range(groups):
                column = pl.multiple_of(group * span + start, LANES)

                @pl.when(column < vocab)
                def _():
                    out_ref[:, pl.ds(column, LANES)] = turned[group * pad : group * pad + width, :]

            return squares + jnp.sum((whole * whole).reshape(LANES // 8, 8, LANES), 0)

        square_ref[...] = lax.fori_loop(0, span // LANES, finish, jnp.zeros((8, LANES), full_type))


def scatter_features(grads, places, vocab):
    count, width, tokens = grads.shape
    pad, groups = lane_pack(width)
    runs = 4
    return pl.pallas_call(
        scatter_kernel,
        out_shape=(
            jax.ShapeDtypeStruct((width, vocab), full_type),
            jax.ShapeDtypeStruct((8, LANES), full_type),
        ),
        grid=(count // runs,),
        in_specs=[
            pl.BlockSpec((runs, 1, tokens), lambda i: (i, 0, 0), memory_space=pltpu.SMEM),
            pl.BlockSpec((runs, 1, tokens), lambda i: (i, 0, 0), memory_space=pltpu.SMEM),
            pl.BlockSpec((runs, width, tokens), lambda i: (i, 0, 0)),
        ],
        out_specs=(
            pl.BlockSpec((width, vocab), lambda i: (0, 0)),
            pl.BlockSpec((8, LANES), lambda i: (0, 0)),
        ),
        scratch_shapes=[
            pltpu.VMEM((max(8, groups), LANES), full_type),
            pltpu.VMEM((runs, tokens, LANES), full_type),
        ]
        + [pltpu.VMEM((quarter(vocab, groups), LANES), full_type) for _ in range(runs)],
        compiler_params=pltpu.CompilerParams(
            dimension_semantics=("arbitrary",), vmem_limit_bytes=52 * 1024 * 1024
        ),
    )(places[0], places[1], grads)


def scatter_places(ids, width, vocab):
    _, groups = lane_pack(width)
    span = quarter(vocab, groups)
    return (ids % span, ids // span)


def turn_tables(row_length, head_width):
    halfway = ROT // 2
    dims = jnp.arange(LANES) % head_width
    inverse = 10000.0 ** (-2.0 * (dims % halfway).astype(full_type) / ROT)
    angles = jnp.arange(row_length, dtype=full_type)[:, None] * inverse[None, :]
    cosine = jnp.where(dims < ROT, jnp.cos(angles), 1.0)
    above = jnp.where(dims < halfway, -jnp.sin(angles), 0.0)
    below = jnp.where((dims >= halfway) & (dims < ROT), jnp.sin(angles), 0.0)
    return jnp.stack([cosine, above, below], 0)


def turned(values_in, tables_ref, forward):
    halfway = ROT // 2
    higher = pltpu.roll(values_in, LANES - halfway, 1) * tables_ref[1]
    lower = pltpu.roll(values_in, halfway, 1) * tables_ref[2]
    straight = values_in * tables_ref[0]
    return straight + (higher + lower) if forward else straight - (higher + lower)


def dot_of(left, right, dims):
    return lax.dot_general(left, right, (dims, ((), ())), preferred_element_type=full_type)


def key_window(block, block_rows):
    return (block + 1) * block_rows


def allowed_block(row_ref, column_ref, block, block_rows):
    reach = key_window(block, block_rows)
    start = block * block_rows
    key_place = lax.broadcasted_iota(jnp.int32, (reach, block_rows), 0)
    query_place = start + lax.broadcasted_iota(jnp.int32, (reach, block_rows), 1)
    same = column_ref[0, :reach, :] == row_ref[0, :, start : start + block_rows]
    return (key_place <= query_place) & same


def forward_kernel(
    query_in, key_in, value_in, tables_ref, row_ref, column_ref, context_ref, query_ref, key_ref, value_ref, logsum_ref
):
    row_length = query_in.shape[0]
    head_width = LANES // 2
    block_rows = row_length // 2
    scale = 1.0 / math.sqrt(head_width)
    query_ref[...] = turned(query_in[...], tables_ref, True).astype(half_type)
    key_ref[...] = turned(key_in[...], tables_ref, True).astype(half_type)
    value_ref[...] = value_in[...].astype(half_type)
    for block in range(2):
        start = block * block_rows
        reach = key_window(block, block_rows)
        allowed = allowed_block(row_ref, column_ref, block, block_rows)
        for head in range(2):
            lanes = slice(head * head_width, (head + 1) * head_width)
            scores = dot_of(key_ref[:reach, lanes], query_ref[start : start + block_rows, lanes], ((1,), (1,)))
            scores = jnp.where(allowed, scores * scale, -1e30)
            peak = jnp.max(scores, 0, keepdims=True)
            powers = jnp.exp(scores - peak)
            total = jnp.sum(powers, 0, keepdims=True)
            logsum_ref[0, 0, head : head + 1, start : start + block_rows] = peak + jnp.log(total)
            weights_soft = (powers * (1.0 / total)).astype(half_type)
            context_ref[start : start + block_rows, lanes] = dot_of(
                weights_soft, value_ref[:reach, lanes], ((0,), (0,))
            ).astype(half_type)


def attention_specs(row_length, pairs):
    def part(offset):
        return pl.BlockSpec((row_length, LANES), lambda m, h: (m, offset * pairs + h))

    tables = pl.BlockSpec((3, row_length, LANES), lambda m, h: (0, 0, 0))
    row = pl.BlockSpec((1, 1, row_length), lambda m, h: (m, 0, 0))
    column = pl.BlockSpec((1, row_length, 1), lambda m, h: (m, 0, 0))
    logsum = pl.BlockSpec((1, 1, 2, row_length), lambda m, h: (m, h, 0, 0))
    return (part, tables, row, column, logsum)


def attention_forward(mixed, tables, segments):
    micro_count, row_length = segments.shape
    tokens = mixed.shape[0]
    width = mixed.shape[1] // 3
    pairs = width // LANES
    part, tables_spec, row, column, logsum = attention_specs(row_length, pairs)
    flat = jax.ShapeDtypeStruct((tokens, width), half_type)
    return pl.pallas_call(
        forward_kernel,
        out_shape=(flat, flat, flat, flat, jax.ShapeDtypeStruct((micro_count, pairs, 2, row_length), full_type)),
        grid=(micro_count, pairs),
        in_specs=[part(0), part(1), part(2), tables_spec, row, column],
        out_specs=(part(0), part(0), part(0), part(0), logsum),
        compiler_params=pltpu.CompilerParams(
            dimension_semantics=("arbitrary", "arbitrary"), vmem_limit_bytes=40 * 1024 * 1024
        ),
    )(mixed, mixed, mixed, tables, segments[:, None, :], segments[:, :, None])


def backward_kernel(
    query_ref, key_ref, value_ref, grad_ref, tables_ref, row_ref, column_ref, logsum_ref, out_ref, query_sum, key_sum, value_sum
):
    row_length = query_ref.shape[0]
    head_width = LANES // 2
    block_rows = row_length // 2
    scale = 1.0 / math.sqrt(head_width)
    for block in reversed(range(2)):
        start = block * block_rows
        reach = key_window(block, block_rows)
        rows = slice(start, start + block_rows)
        allowed = allowed_block(row_ref, column_ref, block, block_rows)
        for head in range(2):
            lanes = slice(head * head_width, (head + 1) * head_width)
            query = query_ref[rows, lanes]
            key = key_ref[:reach, lanes]
            grad = grad_ref[rows, lanes]
            scores = jnp.where(allowed, dot_of(key, query, ((1,), (1,))) * scale, -1e30)
            weights_soft = jnp.exp(scores - logsum_ref[0, 0, head : head + 1, rows])
            grad_value = dot_of(weights_soft.astype(half_type), grad, ((1,), (0,)))
            grad_weights = dot_of(value_ref[:reach, lanes], grad, ((1,), (1,)))
            leaning = jnp.sum(weights_soft * grad_weights, 0, keepdims=True)
            grad_scores = (weights_soft * (grad_weights - leaning)).astype(half_type)
            query_sum[rows, lanes] = dot_of(grad_scores, key, ((0,), (0,))) * scale
            grad_key = dot_of(grad_scores, query, ((1,), (0,))) * scale
            if block == 1:
                value_sum[:, lanes] = grad_value
                key_sum[:, lanes] = grad_key
            else:
                value_sum[:reach, lanes] = value_sum[:reach, lanes] + grad_value
                key_sum[:reach, lanes] = key_sum[:reach, lanes] + grad_key
    out_ref[0] = turned(query_sum[...], tables_ref, False).astype(half_type)
    out_ref[1] = turned(key_sum[...], tables_ref, False).astype(half_type)
    out_ref[2] = value_sum[...].astype(half_type)


def attention_backward(queries, keys_all, values_all, grad_context, logsum, tables, segments):
    micro_count, row_length = segments.shape
    tokens, width = queries.shape
    pairs = width // LANES
    part, tables_spec, row, column, logsum_spec = attention_specs(row_length, pairs)
    return pl.pallas_call(
        backward_kernel,
        out_shape=jax.ShapeDtypeStruct((3, tokens, width), half_type),
        grid=(micro_count, pairs),
        in_specs=[part(0), part(0), part(0), part(0), tables_spec, row, column, logsum_spec],
        out_specs=pl.BlockSpec((3, row_length, LANES), lambda m, h: (0, m, h)),
        scratch_shapes=[pltpu.VMEM((row_length, LANES), full_type) for _ in range(3)],
        compiler_params=pltpu.CompilerParams(
            dimension_semantics=("arbitrary", "arbitrary"), vmem_limit_bytes=40 * 1024 * 1024
        ),
    )(queries, keys_all, values_all, grad_context, tables, segments[:, None, :], segments[:, :, None], logsum)


def document_kernel(
    starts_ref, total_ref, in_ref, out_ref, other_ref, own_ref, turned_ref, shift_ref, window_ref
):
    micro_count, docs = starts_ref.shape[0], starts_ref.shape[1] - 1
    row_length = in_ref.shape[0] // micro_count
    reach = row_length // 2
    step = 16
    half = other_ref.shape[0]
    places = [(micro, doc) for micro in range(micro_count) for doc in range(docs)]

    def bounds(micro, doc):
        start, end = starts_ref[micro, doc], starts_ref[micro, doc + 1]
        window = jnp.minimum((start // step) * step, row_length - reach)
        base = pl.multiple_of(micro * row_length + window, step)
        return (start - window, end - window, base)

    @pl.when(pl.program_id(0) == 0)
    def _():
        row = lax.broadcasted_iota(jnp.int32, (reach, in_ref.shape[1]), 0)
        for place, (micro, doc) in enumerate(places):
            begin, end, base = bounds(micro, doc)

            @pl.when(end <= reach)
            def _():
                rows = in_ref[pl.ds(base, reach), :].astype(full_type)
                kept = jnp.where((row >= begin) & (row < end), rows, 0.0)
                turned_ref[place] = jnp.transpose(kept).astype(half_type)

            @pl.when(end > reach)
            def _():
                to = lax.broadcasted_iota(jnp.int32, (reach, reach + step), 0)
                source = lax.broadcasted_iota(jnp.int32, (reach, reach + step), 1)
                shift_ref[place] = jnp.where(to + begin == source, 1.0, 0.0).astype(half_type)
                rows = dot_of(shift_ref[place], in_ref[pl.ds(base, reach + step), :], ((1,), (0,)))
                kept = jnp.where(row < end - begin, rows, 0.0)
                turned_ref[place] = jnp.transpose(kept).astype(half_type)

    for place, (micro, doc) in enumerate(places):
        begin, end, base = bounds(micro, doc)

        @pl.when(end <= reach)
        def _():
            window_ref[place] = out_ref[pl.ds(base, reach), :]

        @pl.when(end > reach)
        def _():
            window_ref[place] = dot_of(
                shift_ref[place], out_ref[pl.ds(base, reach + step), :], ((1,), (0,))
            ).astype(half_type)

    total = total_ref[0]
    parts = 2
    rows = half // parts
    for part in range(2 * parts):
        found = None
        for place in range(len(places)):
            block = dot_of(
                turned_ref[place, part * rows : (part + 1) * rows, :], window_ref[place], ((1,), (0,))
            )
            block = (block * total).astype(half_type).astype(full_type)
            found = block * block if found is None else found + block * block
        target = other_ref if part < parts else own_ref
        start = (part % parts) * rows
        target[start : start + rows, :] = found


def document_squares(rot_in, rot_out, segments, total):
    micro_count, row_length = segments.shape
    tokens, width = rot_in.shape
    hidden = rot_out.shape[1]
    tile = 2 * LANES
    slots = jnp.arange(DOCS + 1)
    starts = jnp.sum(segments[:, :, None] < slots[None, None, :], 1).astype(jnp.int32)
    return pl.pallas_call(
        document_kernel,
        out_shape=(jax.ShapeDtypeStruct((width // 2, hidden), full_type),) * 2,
        grid=(hidden // tile,),
        in_specs=[
            pl.BlockSpec(memory_space=pltpu.SMEM),
            pl.BlockSpec(memory_space=pltpu.SMEM),
            pl.BlockSpec((tokens, width), lambda i: (0, 0)),
            pl.BlockSpec((tokens, tile), lambda i: (0, i)),
        ],
        out_specs=(pl.BlockSpec((width // 2, tile), lambda i: (0, i)),) * 2,
        scratch_shapes=[
            pltpu.VMEM((micro_count * DOCS, width, row_length // 2), half_type),
            pltpu.VMEM((micro_count * DOCS, row_length // 2, row_length // 2 + 16), half_type),
            pltpu.VMEM((micro_count * DOCS, row_length // 2, tile), half_type),
        ],
        compiler_params=pltpu.CompilerParams(
            dimension_semantics=("arbitrary",), vmem_limit_bytes=40 * 1024 * 1024
        ),
    )(starts, total.reshape(1), rot_in, rot_out)


AXES = ("dp", "fsdp")


def partner_pairs(count, bit):
    return [(place, place ^ (1 << bit)) for place in range(count)]


class Stream:
    def __init__(self, chunks, order, left, wire, relative=False):
        self.held = chunks.reshape((2,) * len(order) + chunks.shape[1:])
        self.left = list(left)
        self.order = list(order)
        self.wire = wire
        self.relative = relative
        self.sent = self.kept = self.got = None

    def land(self, arrived):
        self.held = self.kept + arrived.astype(full_type)
        self.got = None
        return [self]

    def split(self):
        bit = self.order[0]
        axis = self.left.index(bit)
        mine = 0 if self.relative else (lax.axis_index(AXES) >> bit) & 1
        self.sent = lax.dynamic_index_in_dim(self.held, 1 - mine, axis, keepdims=False).astype(self.wire)
        self.kept = lax.dynamic_index_in_dim(self.held, mine, axis, keepdims=False)
        self.left.pop(axis)

    def send(self, ready):
        self.got = lax.ppermute(ready, AXES, partner_pairs(lax.axis_size(AXES), self.order.pop(0)))


class FirstStep:
    def __init__(self, other, own, rows, wire):
        self.sent, self.kept, self.rows, self.wire = other, own, rows, wire
        self.order = [0]
        self.got = None
        self.streams = None

    def land(self, arrived):
        held = (self.kept + arrived).reshape(-1, self.rows, self.kept.shape[1])
        half = held.shape[2] // 2
        bits = lax.axis_size(AXES).bit_length() - 1
        order_a, order_b = link_orders(bits)
        left = range(bits - 1, 0, -1)
        self.got = None
        self.streams = [
            Stream(held[:, :, :half], order_a[1:], left, self.wire),
            Stream(held[:, :, half:], order_b[1:], left, self.wire),
        ]
        return self.streams

    def split(self):
        pass

    def send(self, ready):
        self.order = []
        self.got = lax.ppermute(ready, AXES, partner_pairs(lax.axis_size(AXES), 0))

    def finished(self):
        return jnp.concatenate([stream.held for stream in self.streams], 1)


def advance(anchor, live):
    flying = [stream for stream in live if stream.got is not None]
    anchor, landed = lax.optimization_barrier((anchor, [stream.got for stream in flying]))
    going = [stream for stream in live if stream.got is None]
    for stream, arrived in zip(flying, landed):
        going.extend(stream.land(arrived))
    going = [stream for stream in going if stream.order]
    for stream in going:
        stream.split()
    anchor, ready = lax.optimization_barrier((anchor, [stream.sent for stream in going]))
    for stream, block in zip(going, ready):
        stream.send(block)
    live[:] = going
    return anchor


def run_all(anchor, live):
    while live:
        anchor = advance(anchor, live)
    return anchor


def pair_first(width, rows, place):
    to = lax.broadcasted_iota(jnp.int32, (width, width), 1)
    source = lax.broadcasted_iota(jnp.int32, (width, width), 0)
    core = jnp.where(to < width // 2, 1 - (place & 1), place & 1)
    inside = to % (width // 2)
    wanted = (inside // rows) * (2 * rows) + core * rows + inside % rows
    return (source == wanted).astype(half_type)


def link_orders(bits):
    near = list(range(1, bits - 2))
    return ([0, bits - 2, bits - 1] + near, [0, bits - 1, bits - 2] + near)


def flipped(folded, place):
    bits = lax.axis_size(AXES).bit_length() - 1
    for axis in range(bits):
        mine = (place >> (bits - 1 - axis)) & 1
        folded = jnp.where(mine == 1, jnp.flip(folded, axis), folded)
    return folded


def by_device(stacked, order, place):
    bits = len(order)
    folded = stacked.reshape((2,) * bits + stacked.shape[1:])
    natural = [order.index(bit) for bit in range(bits - 1, -1, -1)]
    folded = jnp.transpose(folded, natural + list(range(bits, folded.ndim)))
    return flipped(folded, place).reshape(stacked.shape)


def by_partner(ordered, order, place):
    bits = len(order)
    folded = flipped(ordered.reshape((2,) * bits + ordered.shape[1:]), place)
    stacked = [bits - 1 - bit for bit in order]
    folded = jnp.transpose(folded, stacked + list(range(bits, folded.ndim)))
    return folded.reshape(ordered.shape)


def gather_trees(blocks, orders):
    held = [block[None] for block in blocks]
    for step in range(len(orders[0])):
        for m, order in enumerate(orders):
            count = 1 << len(order)
            arrived = lax.ppermute(held[m], AXES, partner_pairs(count, order[-1 - step]))
            held[m] = jnp.concatenate([held[m], arrived], 0)
    return held


def shared_by_all(own, count):
    return lax.all_to_all(
        jnp.broadcast_to(own[None], (count,) + own.shape), AXES, split_axis=0, concat_axis=0, tiled=True
    )


def adam_update(weight, gradient, moment_one, moment_two, rate, step_value):
    next_one = decay_first * moment_one + (1.0 - decay_first) * gradient
    next_two = decay_second * moment_two + (1.0 - decay_second) * gradient * gradient
    fix_one = 1.0 - decay_first**step_value
    fix_two = 1.0 - decay_second**step_value
    update = next_one / fix_one / (jnp.sqrt(next_two / fix_two) + adam_epsilon)
    return [weight - rate * (update + weight_decay * weight), next_one, next_two]


def per_device(
    step_count,
    token_ids,
    segment_ids,
    loss_positions,
    label_ids,
    label_mask,
    embed_in,
    embed_in_first,
    embed_in_second,
    embed_out,
    embed_out_first,
    embed_out_second,
    proj_in,
    proj_in_first,
    proj_in_second,
    proj_up,
    proj_up_first,
    proj_up_second,
    proj_mix,
    proj_mix_first,
    proj_mix_second,
    vector_params,
    vector_first,
    vector_second,
    basis_in,
    basis_out,
):
    micro_count = token_ids.shape[0]
    row_length = token_ids.shape[2]
    pick_count = loss_positions.shape[2]
    tokens = micro_count * row_length
    count = lax.axis_size(AXES)
    total = jnp.maximum(jnp.sum(label_mask.astype(full_type)), 1.0)
    vocab = embed_in.shape[1]
    own_width = embed_in.shape[0]
    width = proj_mix.shape[1]
    hidden = proj_up.shape[1]
    head_width = width // HEADS

    place = lax.axis_index(AXES)
    flat_ids = jnp.transpose(token_ids, (1, 0, 2)).reshape(-1)
    ids_by_run = flat_ids.reshape(count, 1, tokens)
    columns = gather_features(embed_in, ids_by_run)
    columns, vector_half = lax.optimization_barrier((columns, vector_params.astype(half_type)))
    arrived = lax.all_to_all(columns, AXES, split_axis=0, concat_axis=0, tiled=True)
    embedded = arrived.reshape(width, tokens).T.astype(full_type)
    places = scatter_places(ids_by_run, own_width, vocab)

    both = jnp.concatenate([proj_in.astype(half_type), proj_up.astype(half_type)], 1)
    both = lax.all_gather(both, AXES, axis=0, tiled=True)
    weight_in, weight_up = both[:, : 3 * width], both[:, 3 * width :]
    weight_mix = lax.all_gather(proj_mix.astype(half_type), AXES, axis=0, tiled=True)
    vector = shared_by_all(vector_half, count).reshape(-1).astype(full_type)
    pairing = pair_first(width, own_width, place)
    basis_paired = jnp.dot(basis_in, pairing, preferred_element_type=full_type).astype(half_type)
    (
        bias_in,
        bias_up,
        bias_mix,
        shift_first,
        shift_second,
        shift_last,
        gain_first,
        gain_second,
        gain_last,
    ) = split_vector(vector, width, hidden)

    segments = segment_ids[:, 0]
    picks = loss_positions[:, 0] + row_length * jnp.arange(micro_count)[:, None]
    picks = picks.reshape(-1)

    normed, inv_std = normalize(embedded)
    first_in = (normed * gain_first + shift_first).astype(half_type)
    second_in = (normed * gain_second + shift_second).astype(half_type)
    mixed = jnp.dot(first_in, weight_in, preferred_element_type=full_type) + bias_in
    tables = turn_tables(row_length, head_width)
    context, queries, keys_all, values_all, logsum = attention_forward(mixed, tables, segments)
    hidden_pre = jnp.dot(second_in, weight_up, preferred_element_type=full_type) + bias_up
    active = (hidden_pre * (0.5 + 0.5 * lax.erf(hidden_pre * (1.0 / math.sqrt(2.0))))).astype(half_type)
    joined = jnp.concatenate([context, active], 1)
    residual = embedded + jnp.dot(joined, weight_mix, preferred_element_type=full_type) + bias_mix
    normed_last, inv_last = normalize(residual)
    final = normed_last * gain_last + shift_last
    picked = jnp.take(final, picks, axis=0, mode="clip").astype(half_type)

    bits = count.bit_length() - 1
    orders = link_orders(bits)
    picked = picked.reshape(micro_count, pick_count, width)
    gathered = jnp.stack(gather_trees(picked, orders)).reshape(-1, width)
    table_out = embed_out.astype(half_type)
    vocab_rows = embed_out.shape[0]
    vocab_ids = place * vocab_rows + jnp.arange(vocab_rows)
    labels_flat = jnp.stack([by_partner(label_ids[m], orders[m], place) for m in range(micro_count)]).reshape(-1)
    mask_flat = jnp.stack([by_partner(label_mask[m], orders[m], place) for m in range(micro_count)]).reshape(-1)
    mask_flat = mask_flat.astype(full_type)
    logits = jnp.einsum("rd,vd->rv", gathered, table_out, preferred_element_type=full_type)
    matches = labels_flat[:, None] == vocab_ids[None, :]
    label_part = jnp.sum(jnp.where(matches, logits, 0.0), 1)
    local_max = jnp.max(logits, 1)
    local_sum = jnp.sum(jnp.exp(logits - local_max[:, None]), 1)
    parts = jnp.stack([local_max, local_sum, label_part], 0).reshape(3, micro_count, count, pick_count)
    parts = jnp.transpose(parts, (1, 2, 0, 3))
    parts = jnp.stack([by_device(parts[m], orders[m], place) for m in range(micro_count)], 1)
    parts = lax.all_to_all(
        parts.reshape(count, 1, -1), AXES, split_axis=0, concat_axis=0, tiled=True
    ).reshape(count, micro_count, 3, pick_count)
    peak = jnp.max(parts[:, :, 0], 0)
    own_logsum = peak + jnp.log(jnp.sum(parts[:, :, 1] * jnp.exp(parts[:, :, 0] - peak[None]), 0))
    own_mask = lax.dynamic_index_in_dim(label_mask, place, 1, keepdims=False).astype(full_type)
    loss_part = jnp.sum(own_mask * (own_logsum - jnp.sum(parts[:, :, 2], 0))) / total
    logsum_all = shared_by_all(own_logsum.reshape(1, -1), count).reshape(count, micro_count, pick_count)
    logsum_all = jnp.stack([by_partner(logsum_all[:, m], orders[m], place) for m in range(micro_count)]).reshape(-1)
    grad_logits = (
        (jnp.exp(logits - logsum_all[:, None]) - matches.astype(full_type))
        * (mask_flat / total)[:, None]
    ).astype(half_type)
    back = jnp.dot(grad_logits, table_out, preferred_element_type=full_type)
    back = back.reshape(micro_count, count, pick_count, width)
    pick_streams = [
        Stream(back[m], orders[m], orders[m], full_type, relative=True) for m in range(micro_count)
    ]
    live = list(pick_streams)
    grad_logits = advance(grad_logits, live)
    grad_out_table = jnp.einsum("rv,rd->vd", grad_logits, gathered, preferred_element_type=full_type)
    out_squares = jnp.sum(grad_out_table * grad_out_table)
    second_paired, out_squares = advance((second_in, out_squares), live)
    rot_in = jnp.dot(second_paired, basis_paired, preferred_element_type=full_type).astype(half_type)
    first_turned = lax.dot_general(
        pairing, first_in, (((0,), (1,)), ((), ())), preferred_element_type=full_type
    ).astype(half_type)
    rot_in, first_turned = advance((rot_in, first_turned), live)
    run_all(jnp.zeros((), full_type), live)
    grad_picked = jnp.concatenate([stream.held for stream in pick_streams], 0)

    grad_final = jnp.zeros((tokens, width), full_type).at[picks].add(grad_picked)
    grad_residual = norm_back(grad_final * gain_last, normed_last, inv_last)
    grad_branch = grad_residual.astype(half_type)
    grad_mix = jnp.einsum("sa,sb->ab", joined, grad_branch, preferred_element_type=full_type)
    own_mix = lax.psum_scatter(grad_mix, AXES, scatter_dimension=0, tiled=True)
    grad_joined = jnp.einsum("sb,ab->sa", grad_branch, weight_mix, preferred_element_type=full_type)
    grad_context = (
        grad_joined[:, :width].astype(half_type)
    )
    grad_hidden = (grad_joined[:, width:] * gelu_slope(hidden_pre)).astype(half_type)
    grad_up = jnp.einsum("sa,sb->ab", second_in, grad_hidden, preferred_element_type=full_type)
    grad_second = jnp.einsum("sb,ab->sa", grad_hidden, weight_up, preferred_element_type=full_type)
    own_up = lax.psum_scatter(grad_up, AXES, scatter_dimension=0, tiled=True)

    rot_out = jnp.dot(grad_hidden, basis_out, preferred_element_type=full_type).astype(half_type)
    scale_other, scale_own = document_squares(rot_in, rot_out, segments, total)
    scale_step = FirstStep(scale_other, scale_own, own_width, half_type)
    live = [scale_step]
    grad_context = advance(grad_context, live)
    grad_parts = attention_backward(
        queries, keys_all, values_all, grad_context, logsum, tables, segments
    )
    grad_mixed = jnp.concatenate([grad_parts[0], grad_parts[1], grad_parts[2]], 1)
    grad_mixed = advance(grad_mixed, live)
    in_other = jnp.dot(first_turned[: width // 2], grad_mixed, preferred_element_type=full_type)
    in_own = jnp.dot(first_turned[width // 2 :], grad_mixed, preferred_element_type=full_type)
    in_step = FirstStep(in_other, in_own, own_width, full_type)
    live.append(in_step)
    grad_mixed = advance(grad_mixed, live)
    grad_first = jnp.einsum("sb,ab->sa", grad_mixed, weight_in, preferred_element_type=full_type)
    grad_embedded = grad_residual + norm_back(
        grad_first * gain_first + grad_second * gain_second, normed, inv_std
    )
    sending = grad_embedded.astype(half_type).T.reshape(count, own_width, tokens)
    returned = lax.all_to_all(sending, AXES, split_axis=0, concat_axis=0, tiled=True)
    vector_grad = jnp.concatenate(
        [
            jnp.sum(grad_mixed.astype(full_type), 0),
            jnp.sum(grad_hidden.astype(full_type), 0),
            jnp.sum(grad_residual, 0),
            jnp.sum(grad_first, 0),
            jnp.sum(grad_second, 0),
            jnp.sum(grad_final, 0),
            jnp.sum(grad_first * normed, 0),
            jnp.sum(grad_second * normed, 0),
            jnp.sum(grad_final * normed_last, 0),
        ]
    )
    vector_grad = advance(vector_grad, live)
    vector_grad = advance(vector_grad, live)
    returned, vector_grad = lax.optimization_barrier((returned, vector_grad))
    own_vector = jnp.sum(
        lax.all_to_all(
            vector_grad.reshape(count, 1, -1), AXES, split_axis=0, concat_axis=0, tiled=True
        ),
        (0, 1),
    )
    grad_in_table, in_squares = scatter_features(returned, places, vocab)
    in_squares = run_all(in_squares, live)
    own_in = in_step.finished()
    eigen_scales = scale_step.finished() / float(micro_count * count * DOCS)
    grads = (grad_in_table, grad_out_table, own_in, own_up, own_mix, own_vector)
    squares = jnp.sum(in_squares) + out_squares
    squares = squares + sum((jnp.sum(gradient * gradient) for gradient in grads[2:]))
    both = jnp.sum(shared_by_all(jnp.stack([squares, loss_part])[None], count), (0, 1))
    grad_norm = jnp.sqrt(both[0])
    loss_value = both[1]
    factor = jnp.minimum(1.0, clip_limit / (grad_norm + 1e-06))
    step_value = step_count[0].astype(full_type)
    weights = (embed_in, embed_out, proj_in, proj_up, proj_mix, vector_params)
    firsts = (
        embed_in_first,
        embed_out_first,
        proj_in_first,
        proj_up_first,
        proj_mix_first,
        vector_first,
    )
    seconds = (
        embed_in_second,
        embed_out_second,
        proj_in_second,
        proj_up_second,
        proj_mix_second,
        vector_second,
    )
    results = []
    for weight, gradient, moment_one, moment_two, rate in zip(
        weights, grads, firsts, seconds, step_rates
    ):
        results.extend(
            adam_update(weight, gradient * factor, moment_one, moment_two, rate, step_value)
        )
    return tuple(results) + (loss_value, grad_norm, eigen_scales)


def solution(mesh):
    in_specs = (
        P(),
        P(),
        P(None, ("dp", "fsdp"), None),
        P(None, ("dp", "fsdp"), None),
        P(),
        P(),
        P(("dp", "fsdp"), None),
        P(("dp", "fsdp"), None),
        P(("dp", "fsdp"), None),
        P(("dp", "fsdp"), None),
        P(("dp", "fsdp"), None),
        P(("dp", "fsdp"), None),
        P(("dp", "fsdp"), None),
        P(("dp", "fsdp"), None),
        P(("dp", "fsdp"), None),
        P(("dp", "fsdp"), None),
        P(("dp", "fsdp"), None),
        P(("dp", "fsdp"), None),
        P(("dp", "fsdp"), None),
        P(("dp", "fsdp"), None),
        P(("dp", "fsdp"), None),
        P(("dp", "fsdp")),
        P(("dp", "fsdp")),
        P(("dp", "fsdp")),
        P(),
        P(),
    )
    out_specs = (
        P(("dp", "fsdp"), None),
        P(("dp", "fsdp"), None),
        P(("dp", "fsdp"), None),
        P(("dp", "fsdp"), None),
        P(("dp", "fsdp"), None),
        P(("dp", "fsdp"), None),
        P(("dp", "fsdp"), None),
        P(("dp", "fsdp"), None),
        P(("dp", "fsdp"), None),
        P(("dp", "fsdp"), None),
        P(("dp", "fsdp"), None),
        P(("dp", "fsdp"), None),
        P(("dp", "fsdp"), None),
        P(("dp", "fsdp"), None),
        P(("dp", "fsdp"), None),
        P(("dp", "fsdp")),
        P(("dp", "fsdp")),
        P(("dp", "fsdp")),
        P(),
        P(),
        P(("dp", "fsdp"), None),
    )
    return jax.shard_map(
        per_device, mesh=mesh, in_specs=in_specs, out_specs=out_specs, check_vma=False
    )
```

```python
import math

import jax
import jax.numpy as jnp
from jax import lax
from jax.experimental import pallas as pl
from jax.experimental.pallas import tpu as pltpu
from jax.sharding import PartitionSpec as P

HEADS = 12
ROT = 16
DOCS = 4


half_type = jnp.bfloat16
full_type = jnp.float32
clip_limit = 0.01
decay_first = 0.9
decay_second = 0.95
adam_epsilon = 1e-08
weight_decay = 0.01
step_rates = (1.0, 0.07, 0.04, 0.04, 0.04, 0.3)


def split_vector(vector, width, hidden):
    lengths = (3 * width, hidden, width, width, width, width, width, width, width)
    pieces = []
    offset = 0
    for length in lengths:
        pieces.append(vector[offset : offset + length])
        offset = offset + length
    return pieces


def normalize(inputs):
    centred = inputs - jnp.mean(inputs, 1, keepdims=True)
    inv_std = lax.rsqrt(jnp.mean(centred * centred, 1, keepdims=True) + 1e-05)
    return (centred * inv_std, inv_std)


def norm_back(grad_out, normed, inv_std):
    return inv_std * (
        grad_out
        - jnp.mean(grad_out, 1, keepdims=True)
        - normed * jnp.mean(grad_out * normed, 1, keepdims=True)
    )


def gelu_slope(inputs):
    return 0.5 * (1.0 + lax.erf(inputs * (1.0 / math.sqrt(2.0)))) + inputs * jnp.exp(
        -0.5 * inputs * inputs
    ) * (1.0 / math.sqrt(2.0 * math.pi))


LANES = 128


def lane_pack(width):
    pad = 8
    while pad < width:
        pad *= 2
    return (pad, LANES // pad)


def copies_matrix(width, dtype):
    pad, _ = lane_pack(width)
    feature = lax.broadcasted_iota(jnp.int32, (width, LANES), 0)
    lane = lax.broadcasted_iota(jnp.int32, (width, LANES), 1)
    return jnp.where(lane % pad == feature, 1.0, 0.0).astype(dtype)


def gather_kernel(ids_ref, table_ref, out_ref, rows_ref, stage_ref):
    width, vocab = table_ref.shape
    tokens = ids_ref.shape[2]
    pad, groups = lane_pack(width)
    stride = tokens // groups

    @pl.when(pl.program_id(0) == 0)
    def _():
        chunks = vocab // LANES
        many = 8
        filler = jnp.zeros((pad - width, LANES), full_type)

        def build(start):
            piece = table_ref[:, pl.ds(start, LANES)].astype(half_type).astype(full_type)
            tall = jnp.concatenate([piece, filler] * groups, 0) if pad > width else jnp.concatenate([piece] * groups, 0)
            rows_ref[pl.ds(start, LANES), :] = jnp.transpose(tall)

        def several(block, carry):
            for inner in range(many):
                build(pl.multiple_of((block * many + inner) * LANES, LANES))
            return carry

        lax.fori_loop(0, chunks // many, several, 0)
        for rest in range(chunks // many * many, chunks):
            build(rest * LANES)

    lane_group = lax.broadcasted_iota(jnp.int32, (1, LANES), 1) // pad
    unroll = 16

    def pick(block, carry):
        base = block * unroll
        for inner in range(unroll):
            row = None
            for group in range(groups):
                found = rows_ref[pl.ds(ids_ref[0, 0, group * stride + base + inner], 1), :]
                row = found if row is None else jnp.where(lane_group == group, found, row)
            stage_ref[pl.ds(base + inner, 1), :] = row
        return carry

    lax.fori_loop(0, stride // unroll, pick, 0)
    turned = jnp.transpose(stage_ref[...])
    for group in range(groups):
        out_ref[0, :, group * stride : (group + 1) * stride] = turned[
            group * pad : group * pad + width, :
        ].astype(half_type)


def gather_features(table, ids):
    width, vocab = table.shape
    count, _, tokens = ids.shape
    _, groups = lane_pack(width)
    return pl.pallas_call(
        gather_kernel,
        out_shape=jax.ShapeDtypeStruct((count, width, tokens), half_type),
        grid=(count,),
        in_specs=[
            pl.BlockSpec((1, 1, tokens), lambda i: (i, 0, 0), memory_space=pltpu.SMEM),
            pl.BlockSpec((width, vocab), lambda i: (0, 0), pipeline_mode=pl.Buffered(1)),
        ],
        out_specs=pl.BlockSpec((1, width, tokens), lambda i: (i, 0, 0)),
        scratch_shapes=[
            pltpu.VMEM((vocab, LANES), full_type),
            pltpu.VMEM((tokens // groups, LANES), full_type),
        ],
        compiler_params=pltpu.CompilerParams(
            dimension_semantics=("arbitrary",), vmem_limit_bytes=44 * 1024 * 1024
        ),
    )(ids, table)


def quarter(vocab, groups):
    return -(-vocab // (groups * LANES)) * LANES


def scatter_kernel(places_ref, groups_ref, grad_ref, out_ref, square_ref, mask_ref, stage_ref, *sums):
    width, vocab = out_ref.shape
    runs, _, tokens = places_ref.shape
    pad, groups = lane_pack(width)
    shift = groups.bit_length() - 1
    span = quarter(vocab, groups)

    @pl.when(pl.program_id(0) == 0)
    def _():
        lane_group = lax.broadcasted_iota(jnp.int32, mask_ref.shape, 1) // pad
        mask_ref[...] = jnp.where(
            lane_group == lax.broadcasted_iota(jnp.int32, mask_ref.shape, 0), 1.0, 0.0
        )

        def clear(block, carry):
            start = pl.multiple_of(block * LANES, LANES)
            for total in sums:
                total[pl.ds(start, LANES), :] = jnp.zeros((LANES, LANES), full_type)
            return carry

        lax.fori_loop(0, span // LANES, clear, 0)

    spread = copies_matrix(width, half_type)
    for run in range(runs):
        stage_ref[run] = lax.dot_general(
            grad_ref[run], spread, (((0,), (0,)), ((), ())), preferred_element_type=full_type
        )
    unroll = 32

    def add(block, carry):
        base = block * unroll
        for inner in range(unroll):
            rows = [pl.ds(places_ref[run, 0, base + inner], 1) for run in range(runs)]
            new = [
                sums[run][rows[run], :]
                + stage_ref[run, pl.ds(base + inner, 1), :] * mask_ref[pl.ds(groups_ref[run, 0, base + inner], 1), :]
                for run in range(runs)
            ]
            for run in range(runs):
                sums[run][rows[run], :] = new[run]
        return carry

    lax.fori_loop(0, tokens // unroll, add, 0)

    @pl.when(pl.program_id(0) == pl.num_programs(0) - 1)
    def _():
        def finish(block, squares):
            start = pl.multiple_of(block * LANES, LANES)
            whole = sums[0][pl.ds(start, LANES), :]
            for total in sums[1:]:
                whole = whole + total[pl.ds(start, LANES), :]
            turned = jnp.transpose(whole)
            for group in range(groups):
                column = pl.multiple_of(group * span + start, LANES)

                @pl.when(column < vocab)
                def _():
                    out_ref[:, pl.ds(column, LANES)] = turned[group * pad : group * pad + width, :]

            return squares + jnp.sum((whole * whole).reshape(LANES // 8, 8, LANES), 0)

        square_ref[...] = lax.fori_loop(0, span // LANES, finish, jnp.zeros((8, LANES), full_type))


def scatter_features(grads, places, vocab):
    count, width, tokens = grads.shape
    pad, groups = lane_pack(width)
    runs = 4
    return pl.pallas_call(
        scatter_kernel,
        out_shape=(
            jax.ShapeDtypeStruct((width, vocab), full_type),
            jax.ShapeDtypeStruct((8, LANES), full_type),
        ),
        grid=(count // runs,),
        in_specs=[
            pl.BlockSpec((runs, 1, tokens), lambda i: (i, 0, 0), memory_space=pltpu.SMEM),
            pl.BlockSpec((runs, 1, tokens), lambda i: (i, 0, 0), memory_space=pltpu.SMEM),
            pl.BlockSpec((runs, width, tokens), lambda i: (i, 0, 0)),
        ],
        out_specs=(
            pl.BlockSpec((width, vocab), lambda i: (0, 0)),
            pl.BlockSpec((8, LANES), lambda i: (0, 0)),
        ),
        scratch_shapes=[
            pltpu.VMEM((max(8, groups), LANES), full_type),
            pltpu.VMEM((runs, tokens, LANES), full_type),
        ]
        + [pltpu.VMEM((quarter(vocab, groups), LANES), full_type) for _ in range(runs)],
        compiler_params=pltpu.CompilerParams(
            dimension_semantics=("arbitrary",), vmem_limit_bytes=52 * 1024 * 1024
        ),
    )(places[0], places[1], grads)


def scatter_places(ids, width, vocab):
    _, groups = lane_pack(width)
    span = quarter(vocab, groups)
    return (ids % span, ids // span)


def turn_tables(row_length, head_width):
    halfway = ROT // 2
    dims = jnp.arange(LANES) % head_width
    inverse = 10000.0 ** (-2.0 * (dims % halfway).astype(full_type) / ROT)
    angles = jnp.arange(row_length, dtype=full_type)[:, None] * inverse[None, :]
    cosine = jnp.where(dims < ROT, jnp.cos(angles), 1.0)
    above = jnp.where(dims < halfway, -jnp.sin(angles), 0.0)
    below = jnp.where((dims >= halfway) & (dims < ROT), jnp.sin(angles), 0.0)
    return jnp.stack([cosine, above, below], 0)


def turned(values_in, tables_ref, forward):
    halfway = ROT // 2
    higher = pltpu.roll(values_in, LANES - halfway, 1) * tables_ref[1]
    lower = pltpu.roll(values_in, halfway, 1) * tables_ref[2]
    straight = values_in * tables_ref[0]
    return straight + (higher + lower) if forward else straight - (higher + lower)


def dot_of(left, right, dims):
    return lax.dot_general(left, right, (dims, ((), ())), preferred_element_type=full_type)


def key_window(block, block_rows):
    return (block + 1) * block_rows


def allowed_block(row_ref, column_ref, block, block_rows):
    reach = key_window(block, block_rows)
    start = block * block_rows
    key_place = lax.broadcasted_iota(jnp.int32, (reach, block_rows), 0)
    query_place = start + lax.broadcasted_iota(jnp.int32, (reach, block_rows), 1)
    same = column_ref[0, :reach, :] == row_ref[0, :, start : start + block_rows]
    return (key_place <= query_place) & same


def forward_kernel(
    query_in, key_in, value_in, tables_ref, row_ref, column_ref, context_ref, query_ref, key_ref, value_ref, logsum_ref
):
    row_length = query_in.shape[0]
    head_width = LANES // 2
    block_rows = row_length // 2
    scale = 1.0 / math.sqrt(head_width)
    query_ref[...] = turned(query_in[...], tables_ref, True).astype(half_type)
    key_ref[...] = turned(key_in[...], tables_ref, True).astype(half_type)
    value_ref[...] = value_in[...].astype(half_type)
    for block in range(2):
        start = block * block_rows
        reach = key_window(block, block_rows)
        allowed = allowed_block(row_ref, column_ref, block, block_rows)
        for head in range(2):
            lanes = slice(head * head_width, (head + 1) * head_width)
            scores = dot_of(key_ref[:reach, lanes], query_ref[start : start + block_rows, lanes], ((1,), (1,)))
            scores = jnp.where(allowed, scores * scale, -1e30)
            peak = jnp.max(scores, 0, keepdims=True)
            powers = jnp.exp(scores - peak)
            total = jnp.sum(powers, 0, keepdims=True)
            logsum_ref[0, 0, head : head + 1, start : start + block_rows] = peak + jnp.log(total)
            weights_soft = (powers * (1.0 / total)).astype(half_type)
            context_ref[start : start + block_rows, lanes] = dot_of(
                weights_soft, value_ref[:reach, lanes], ((0,), (0,))
            ).astype(half_type)


def attention_specs(row_length, pairs):
    def part(offset):
        return pl.BlockSpec((row_length, LANES), lambda m, h: (m, offset * pairs + h))

    tables = pl.BlockSpec((3, row_length, LANES), lambda m, h: (0, 0, 0))
    row = pl.BlockSpec((1, 1, row_length), lambda m, h: (m, 0, 0))
    column = pl.BlockSpec((1, row_length, 1), lambda m, h: (m, 0, 0))
    logsum = pl.BlockSpec((1, 1, 2, row_length), lambda m, h: (m, h, 0, 0))
    return (part, tables, row, column, logsum)


def attention_forward(mixed, tables, segments):
    micro_count, row_length = segments.shape
    tokens = mixed.shape[0]
    width = mixed.shape[1] // 3
    pairs = width // LANES
    part, tables_spec, row, column, logsum = attention_specs(row_length, pairs)
    flat = jax.ShapeDtypeStruct((tokens, width), half_type)
    return pl.pallas_call(
        forward_kernel,
        out_shape=(flat, flat, flat, flat, jax.ShapeDtypeStruct((micro_count, pairs, 2, row_length), full_type)),
        grid=(micro_count, pairs),
        in_specs=[part(0), part(1), part(2), tables_spec, row, column],
        out_specs=(part(0), part(0), part(0), part(0), logsum),
        compiler_params=pltpu.CompilerParams(
            dimension_semantics=("arbitrary", "arbitrary"), vmem_limit_bytes=40 * 1024 * 1024
        ),
    )(mixed, mixed, mixed, tables, segments[:, None, :], segments[:, :, None])


def backward_kernel(
    query_ref, key_ref, value_ref, grad_ref, tables_ref, row_ref, column_ref, logsum_ref, out_ref, query_sum, key_sum, value_sum
):
    row_length = query_ref.shape[0]
    head_width = LANES // 2
    block_rows = row_length // 2
    scale = 1.0 / math.sqrt(head_width)
    for block in reversed(range(2)):
        start = block * block_rows
        reach = key_window(block, block_rows)
        rows = slice(start, start + block_rows)
        allowed = allowed_block(row_ref, column_ref, block, block_rows)
        for head in range(2):
            lanes = slice(head * head_width, (head + 1) * head_width)
            query = query_ref[rows, lanes]
            key = key_ref[:reach, lanes]
            grad = grad_ref[rows, lanes]
            scores = jnp.where(allowed, dot_of(key, query, ((1,), (1,))) * scale, -1e30)
            weights_soft = jnp.exp(scores - logsum_ref[0, 0, head : head + 1, rows])
            grad_value = dot_of(weights_soft.astype(half_type), grad, ((1,), (0,)))
            grad_weights = dot_of(value_ref[:reach, lanes], grad, ((1,), (1,)))
            leaning = jnp.sum(weights_soft * grad_weights, 0, keepdims=True)
            grad_scores = (weights_soft * (grad_weights - leaning)).astype(half_type)
            query_sum[rows, lanes] = dot_of(grad_scores, key, ((0,), (0,))) * scale
            grad_key = dot_of(grad_scores, query, ((1,), (0,))) * scale
            if block == 1:
                value_sum[:, lanes] = grad_value
                key_sum[:, lanes] = grad_key
            else:
                value_sum[:reach, lanes] = value_sum[:reach, lanes] + grad_value
                key_sum[:reach, lanes] = key_sum[:reach, lanes] + grad_key
    out_ref[0] = turned(query_sum[...], tables_ref, False).astype(half_type)
    out_ref[1] = turned(key_sum[...], tables_ref, False).astype(half_type)
    out_ref[2] = value_sum[...].astype(half_type)


def attention_backward(queries, keys_all, values_all, grad_context, logsum, tables, segments):
    micro_count, row_length = segments.shape
    tokens, width = queries.shape
    pairs = width // LANES
    part, tables_spec, row, column, logsum_spec = attention_specs(row_length, pairs)
    return pl.pallas_call(
        backward_kernel,
        out_shape=jax.ShapeDtypeStruct((3, tokens, width), half_type),
        grid=(micro_count, pairs),
        in_specs=[part(0), part(0), part(0), part(0), tables_spec, row, column, logsum_spec],
        out_specs=pl.BlockSpec((3, row_length, LANES), lambda m, h: (0, m, h)),
        scratch_shapes=[pltpu.VMEM((row_length, LANES), full_type) for _ in range(3)],
        compiler_params=pltpu.CompilerParams(
            dimension_semantics=("arbitrary", "arbitrary"), vmem_limit_bytes=40 * 1024 * 1024
        ),
    )(queries, keys_all, values_all, grad_context, tables, segments[:, None, :], segments[:, :, None], logsum)


def document_kernel(
    starts_ref, total_ref, in_ref, out_ref, other_ref, own_ref, turned_ref, shift_ref, window_ref
):
    micro_count, docs = starts_ref.shape[0], starts_ref.shape[1] - 1
    row_length = in_ref.shape[0] // micro_count
    reach = row_length // 2
    step = 16
    half = other_ref.shape[0]
    places = [(micro, doc) for micro in range(micro_count) for doc in range(docs)]

    def bounds(micro, doc):
        start, end = starts_ref[micro, doc], starts_ref[micro, doc + 1]
        window = jnp.minimum((start // step) * step, row_length - reach)
        base = pl.multiple_of(micro * row_length + window, step)
        return (start - window, end - window, base)

    @pl.when(pl.program_id(0) == 0)
    def _():
        row = lax.broadcasted_iota(jnp.int32, (reach, in_ref.shape[1]), 0)
        for place, (micro, doc) in enumerate(places):
            begin, end, base = bounds(micro, doc)

            @pl.when(end <= reach)
            def _():
                rows = in_ref[pl.ds(base, reach), :].astype(full_type)
                kept = jnp.where((row >= begin) & (row < end), rows, 0.0)
                turned_ref[place] = jnp.transpose(kept).astype(half_type)

            @pl.when(end > reach)
            def _():
                to = lax.broadcasted_iota(jnp.int32, (reach, reach + step), 0)
                source = lax.broadcasted_iota(jnp.int32, (reach, reach + step), 1)
                shift_ref[place] = jnp.where(to + begin == source, 1.0, 0.0).astype(half_type)
                rows = dot_of(shift_ref[place], in_ref[pl.ds(base, reach + step), :], ((1,), (0,)))
                kept = jnp.where(row < end - begin, rows, 0.0)
                turned_ref[place] = jnp.transpose(kept).astype(half_type)

    for place, (micro, doc) in enumerate(places):
        begin, end, base = bounds(micro, doc)

        @pl.when(end <= reach)
        def _():
            window_ref[place] = out_ref[pl.ds(base, reach), :]

        @pl.when(end > reach)
        def _():
            window_ref[place] = dot_of(
                shift_ref[place], out_ref[pl.ds(base, reach + step), :], ((1,), (0,))
            ).astype(half_type)

    total = total_ref[0]
    parts = 2
    rows = half // parts
    for part in range(2 * parts):
        found = None
        for place in range(len(places)):
            block = dot_of(
                turned_ref[place, part * rows : (part + 1) * rows, :], window_ref[place], ((1,), (0,))
            )
            block = (block * total).astype(half_type).astype(full_type)
            found = block * block if found is None else found + block * block
        target = other_ref if part < parts else own_ref
        start = (part % parts) * rows
        target[start : start + rows, :] = found


def document_squares(rot_in, rot_out, segments, total):
    micro_count, row_length = segments.shape
    tokens, width = rot_in.shape
    hidden = rot_out.shape[1]
    tile = 2 * LANES
    slots = jnp.arange(DOCS + 1)
    starts = jnp.sum(segments[:, :, None] < slots[None, None, :], 1).astype(jnp.int32)
    return pl.pallas_call(
        document_kernel,
        out_shape=(jax.ShapeDtypeStruct((width // 2, hidden), full_type),) * 2,
        grid=(hidden // tile,),
        in_specs=[
            pl.BlockSpec(memory_space=pltpu.SMEM),
            pl.BlockSpec(memory_space=pltpu.SMEM),
            pl.BlockSpec((tokens, width), lambda i: (0, 0)),
            pl.BlockSpec((tokens, tile), lambda i: (0, i)),
        ],
        out_specs=(pl.BlockSpec((width // 2, tile), lambda i: (0, i)),) * 2,
        scratch_shapes=[
            pltpu.VMEM((micro_count * DOCS, width, row_length // 2), half_type),
            pltpu.VMEM((micro_count * DOCS, row_length // 2, row_length // 2 + 16), half_type),
            pltpu.VMEM((micro_count * DOCS, row_length // 2, tile), half_type),
        ],
        compiler_params=pltpu.CompilerParams(
            dimension_semantics=("arbitrary",), vmem_limit_bytes=40 * 1024 * 1024
        ),
    )(starts, total.reshape(1), rot_in, rot_out)


AXES = ("dp", "fsdp")


def partner_pairs(count, bit):
    return [(place, place ^ (1 << bit)) for place in range(count)]


class Stream:
    def __init__(self, chunks, order, left, wire, relative=False):
        self.held = chunks.reshape((2,) * len(order) + chunks.shape[1:])
        self.left = list(left)
        self.order = list(order)
        self.wire = wire
        self.relative = relative
        self.sent = self.kept = self.got = None

    def land(self, arrived):
        self.held = self.kept + arrived.astype(full_type)
        self.got = None
        return [self]

    def split(self):
        bit = self.order[0]
        axis = self.left.index(bit)
        mine = 0 if self.relative else (lax.axis_index(AXES) >> bit) & 1
        self.sent = lax.dynamic_index_in_dim(self.held, 1 - mine, axis, keepdims=False).astype(self.wire)
        self.kept = lax.dynamic_index_in_dim(self.held, mine, axis, keepdims=False)
        self.left.pop(axis)

    def send(self, ready):
        self.got = lax.ppermute(ready, AXES, partner_pairs(lax.axis_size(AXES), self.order.pop(0)))


class FirstStep:
    def __init__(self, other, own, rows, wire):
        self.sent, self.kept, self.rows, self.wire = other, own, rows, wire
        self.order = [0]
        self.got = None
        self.streams = None

    def land(self, arrived):
        held = (self.kept + arrived).reshape(-1, self.rows, self.kept.shape[1])
        half = held.shape[2] // 2
        bits = lax.axis_size(AXES).bit_length() - 1
        order_a, order_b = link_orders(bits)
        left = range(bits - 1, 0, -1)
        self.got = None
        self.streams = [
            Stream(held[:, :, :half], order_a[1:], left, self.wire),
            Stream(held[:, :, half:], order_b[1:], left, self.wire),
        ]
        return self.streams

    def split(self):
        pass

    def send(self, ready):
        self.order = []
        self.got = lax.ppermute(ready, AXES, partner_pairs(lax.axis_size(AXES), 0))

    def finished(self):
        return jnp.concatenate([stream.held for stream in self.streams], 1)


def advance(anchor, live):
    flying = [stream for stream in live if stream.got is not None]
    anchor, landed = lax.optimization_barrier((anchor, [stream.got for stream in flying]))
    going = [stream for stream in live if stream.got is None]
    for stream, arrived in zip(flying, landed):
        going.extend(stream.land(arrived))
    going = [stream for stream in going if stream.order]
    for stream in going:
        stream.split()
    anchor, ready = lax.optimization_barrier((anchor, [stream.sent for stream in going]))
    for stream, block in zip(going, ready):
        stream.send(block)
    live[:] = going
    return anchor


def run_all(anchor, live):
    while live:
        anchor = advance(anchor, live)
    return anchor


def pair_first(width, rows, place):
    to = lax.broadcasted_iota(jnp.int32, (width, width), 1)
    source = lax.broadcasted_iota(jnp.int32, (width, width), 0)
    core = jnp.where(to < width // 2, 1 - (place & 1), place & 1)
    inside = to % (width // 2)
    wanted = (inside // rows) * (2 * rows) + core * rows + inside % rows
    return (source == wanted).astype(half_type)


def link_orders(bits):
    near = list(range(1, bits - 2))
    return ([0, bits - 2, bits - 1] + near, [0, bits - 1, bits - 2] + near)


def flipped(folded, place):
    bits = lax.axis_size(AXES).bit_length() - 1
    for axis in range(bits):
        mine = (place >> (bits - 1 - axis)) & 1
        folded = jnp.where(mine == 1, jnp.flip(folded, axis), folded)
    return folded


def by_device(stacked, order, place):
    bits = len(order)
    folded = stacked.reshape((2,) * bits + stacked.shape[1:])
    natural = [order.index(bit) for bit in range(bits - 1, -1, -1)]
    folded = jnp.transpose(folded, natural + list(range(bits, folded.ndim)))
    return flipped(folded, place).reshape(stacked.shape)


def by_partner(ordered, order, place):
    bits = len(order)
    folded = flipped(ordered.reshape((2,) * bits + ordered.shape[1:]), place)
    stacked = [bits - 1 - bit for bit in order]
    folded = jnp.transpose(folded, stacked + list(range(bits, folded.ndim)))
    return folded.reshape(ordered.shape)


def gather_trees(blocks, orders):
    held = [block[None] for block in blocks]
    for step in range(len(orders[0])):
        for m, order in enumerate(orders):
            count = 1 << len(order)
            arrived = lax.ppermute(held[m], AXES, partner_pairs(count, order[-1 - step]))
            held[m] = jnp.concatenate([held[m], arrived], 0)
    return held


def shared_by_all(own, count):
    return lax.all_to_all(
        jnp.broadcast_to(own[None], (count,) + own.shape), AXES, split_axis=0, concat_axis=0, tiled=True
    )


def adam_update(weight, gradient, moment_one, moment_two, rate, step_value):
    next_one = decay_first * moment_one + (1.0 - decay_first) * gradient
    next_two = decay_second * moment_two + (1.0 - decay_second) * gradient * gradient
    fix_one = 1.0 - decay_first**step_value
    fix_two = 1.0 - decay_second**step_value
    update = next_one / fix_one / (jnp.sqrt(next_two / fix_two) + adam_epsilon)
    return [weight - rate * (update + weight_decay * weight), next_one, next_two]


def per_device(
    step_count,
    token_ids,
    segment_ids,
    loss_positions,
    label_ids,
    label_mask,
    embed_in,
    embed_in_first,
    embed_in_second,
    embed_out,
    embed_out_first,
    embed_out_second,
    proj_in,
    proj_in_first,
    proj_in_second,
    proj_up,
    proj_up_first,
    proj_up_second,
    proj_mix,
    proj_mix_first,
    proj_mix_second,
    vector_params,
    vector_first,
    vector_second,
    basis_in,
    basis_out,
):
    micro_count = token_ids.shape[0]
    row_length = token_ids.shape[2]
    pick_count = loss_positions.shape[2]
    tokens = micro_count * row_length
    count = lax.axis_size(AXES)
    total = jnp.maximum(jnp.sum(label_mask.astype(full_type)), 1.0)
    vocab = embed_in.shape[1]
    own_width = embed_in.shape[0]
    width = proj_mix.shape[1]
    hidden = proj_up.shape[1]
    head_width = width // HEADS

    place = lax.axis_index(AXES)
    flat_ids = jnp.transpose(token_ids, (1, 0, 2)).reshape(-1)
    ids_by_run = flat_ids.reshape(count, 1, tokens)
    columns = gather_features(embed_in, ids_by_run)
    arrived = lax.all_to_all(columns, AXES, split_axis=0, concat_axis=0, tiled=True)
    embedded = arrived.reshape(width, tokens).T.astype(full_type)
    places = scatter_places(ids_by_run, own_width, vocab)

    small = vector_params.astype(half_type).reshape(own_width, -1)
    each = small.shape[1]
    small = jnp.pad(small, ((0, 0), (0, -each % LANES)))
    both = jnp.concatenate([proj_in.astype(half_type), proj_up.astype(half_type), small], 1)
    both = lax.all_gather(both, AXES, axis=0, tiled=True)
    weight_in, weight_up = both[:, : 3 * width], both[:, 3 * width : 3 * width + hidden]
    weight_mix = lax.all_gather(proj_mix.astype(half_type), AXES, axis=0, tiled=True)
    vector = both[:, 3 * width + hidden : 3 * width + hidden + each].reshape(-1).astype(full_type)
    pairing = pair_first(width, own_width, place)
    basis_paired = jnp.dot(basis_in, pairing, preferred_element_type=full_type).astype(half_type)
    (
        bias_in,
        bias_up,
        bias_mix,
        shift_first,
        shift_second,
        shift_last,
        gain_first,
        gain_second,
        gain_last,
    ) = split_vector(vector, width, hidden)

    segments = segment_ids[:, 0]
    picks = loss_positions[:, 0] + row_length * jnp.arange(micro_count)[:, None]
    picks = picks.reshape(-1)

    normed, inv_std = normalize(embedded)
    first_in = (normed * gain_first + shift_first).astype(half_type)
    second_in = (normed * gain_second + shift_second).astype(half_type)
    mixed = jnp.dot(first_in, weight_in, preferred_element_type=full_type) + bias_in
    tables = turn_tables(row_length, head_width)
    context, queries, keys_all, values_all, logsum = attention_forward(mixed, tables, segments)
    hidden_pre = jnp.dot(second_in, weight_up, preferred_element_type=full_type) + bias_up
    active = (hidden_pre * (0.5 + 0.5 * lax.erf(hidden_pre * (1.0 / math.sqrt(2.0))))).astype(half_type)
    joined = jnp.concatenate([context, active], 1)
    residual = embedded + jnp.dot(joined, weight_mix, preferred_element_type=full_type) + bias_mix
    normed_last, inv_last = normalize(residual)
    final = normed_last * gain_last + shift_last
    picked = jnp.take(final, picks, axis=0, mode="clip").astype(half_type)

    bits = count.bit_length() - 1
    orders = link_orders(bits)
    picked = picked.reshape(micro_count, pick_count, width)
    gathered = jnp.stack(gather_trees(picked, orders)).reshape(-1, width)
    table_out = embed_out.astype(half_type)
    vocab_rows = embed_out.shape[0]
    vocab_ids = place * vocab_rows + jnp.arange(vocab_rows)
    labels_flat = jnp.stack([by_partner(label_ids[m], orders[m], place) for m in range(micro_count)]).reshape(-1)
    mask_flat = jnp.stack([by_partner(label_mask[m], orders[m], place) for m in range(micro_count)]).reshape(-1)
    mask_flat = mask_flat.astype(full_type)
    logits = jnp.einsum("rd,vd->rv", gathered, table_out, preferred_element_type=full_type)
    matches = labels_flat[:, None] == vocab_ids[None, :]
    label_part = jnp.sum(jnp.where(matches, logits, 0.0), 1)
    local_max = jnp.max(logits, 1)
    local_sum = jnp.sum(jnp.exp(logits - local_max[:, None]), 1)
    parts = jnp.stack([local_max, local_sum, label_part], 0).reshape(3, micro_count, count, pick_count)
    parts = jnp.transpose(parts, (1, 2, 0, 3))
    parts = jnp.stack([by_device(parts[m], orders[m], place) for m in range(micro_count)], 1)
    parts = lax.all_to_all(
        parts.reshape(count, 1, -1), AXES, split_axis=0, concat_axis=0, tiled=True
    ).reshape(count, micro_count, 3, pick_count)
    peak = jnp.max(parts[:, :, 0], 0)
    own_logsum = peak + jnp.log(jnp.sum(parts[:, :, 1] * jnp.exp(parts[:, :, 0] - peak[None]), 0))
    own_mask = lax.dynamic_index_in_dim(label_mask, place, 1, keepdims=False).astype(full_type)
    loss_part = jnp.sum(own_mask * (own_logsum - jnp.sum(parts[:, :, 2], 0))) / total
    logsum_all = shared_by_all(own_logsum.reshape(1, -1), count).reshape(count, micro_count, pick_count)
    logsum_all = jnp.stack([by_partner(logsum_all[:, m], orders[m], place) for m in range(micro_count)]).reshape(-1)
    grad_logits = (
        (jnp.exp(logits - logsum_all[:, None]) - matches.astype(full_type))
        * (mask_flat / total)[:, None]
    ).astype(half_type)
    back = jnp.dot(grad_logits, table_out, preferred_element_type=full_type)
    back = back.reshape(micro_count, count, pick_count, width)
    pick_streams = [
        Stream(back[m], orders[m], orders[m], full_type, relative=True) for m in range(micro_count)
    ]
    live = list(pick_streams)
    grad_logits = advance(grad_logits, live)
    grad_out_table = jnp.einsum("rv,rd->vd", grad_logits, gathered, preferred_element_type=full_type)
    out_squares = jnp.sum(grad_out_table * grad_out_table)
    second_paired, out_squares = advance((second_in, out_squares), live)
    rot_in = jnp.dot(second_paired, basis_paired, preferred_element_type=full_type).astype(half_type)
    first_turned = lax.dot_general(
        pairing, first_in, (((0,), (1,)), ((), ())), preferred_element_type=full_type
    ).astype(half_type)
    rot_in, first_turned = advance((rot_in, first_turned), live)
    run_all(jnp.zeros((), full_type), live)
    grad_picked = jnp.concatenate([stream.held for stream in pick_streams], 0)

    grad_final = jnp.zeros((tokens, width), full_type).at[picks].add(grad_picked)
    grad_residual = norm_back(grad_final * gain_last, normed_last, inv_last)
    grad_branch = grad_residual.astype(half_type)
    grad_mix = jnp.einsum("sa,sb->ab", joined, grad_branch, preferred_element_type=full_type)
    grad_branch, grad_mix = lax.optimization_barrier((grad_branch, grad_mix))
    own_mix = lax.psum_scatter(grad_mix, AXES, scatter_dimension=0, tiled=True)
    grad_joined = jnp.einsum("sb,ab->sa", grad_branch, weight_mix, preferred_element_type=full_type)
    grad_context = grad_joined[:, :width].astype(half_type)
    grad_parts = attention_backward(
        queries, keys_all, values_all, grad_context, logsum, tables, segments
    )
    grad_mixed = jnp.concatenate([grad_parts[0], grad_parts[1], grad_parts[2]], 1)
    in_other = jnp.dot(first_turned[: width // 2], grad_mixed, preferred_element_type=full_type)
    in_own = jnp.dot(first_turned[width // 2 :], grad_mixed, preferred_element_type=full_type)
    in_step = FirstStep(in_other, in_own, own_width, full_type)
    live = [in_step]
    grad_joined = advance(grad_joined, live)
    grad_hidden = (grad_joined[:, width:] * gelu_slope(hidden_pre)).astype(half_type)
    grad_hidden = advance(grad_hidden, live)
    grad_up = jnp.einsum("sa,sb->ab", second_in, grad_hidden, preferred_element_type=full_type)
    grad_second = jnp.einsum("sb,ab->sa", grad_hidden, weight_up, preferred_element_type=full_type)
    grad_up, grad_second, grad_mixed = advance((grad_up, grad_second, grad_mixed), live)
    own_up = lax.psum_scatter(grad_up, AXES, scatter_dimension=0, tiled=True)
    grad_first = jnp.einsum("sb,ab->sa", grad_mixed, weight_in, preferred_element_type=full_type)
    grad_embedded = grad_residual + norm_back(
        grad_first * gain_first + grad_second * gain_second, normed, inv_std
    )
    sending = grad_embedded.astype(half_type).T.reshape(count, own_width, tokens)
    sending, grad_hidden_late = advance((sending, grad_hidden), live)
    returned = lax.all_to_all(sending, AXES, split_axis=0, concat_axis=0, tiled=True)

    rot_out = jnp.dot(grad_hidden_late, basis_out, preferred_element_type=full_type).astype(half_type)
    scale_other, scale_own = document_squares(rot_in, rot_out, segments, total)
    scale_step = FirstStep(scale_other, scale_own, own_width, half_type)
    scale_live = [scale_step]
    vector_grad = jnp.concatenate(
        [
            jnp.sum(grad_mixed.astype(full_type), 0),
            jnp.sum(grad_hidden.astype(full_type), 0),
            jnp.sum(grad_residual, 0),
            jnp.sum(grad_first, 0),
            jnp.sum(grad_second, 0),
            jnp.sum(grad_final, 0),
            jnp.sum(grad_first * normed, 0),
            jnp.sum(grad_second * normed, 0),
            jnp.sum(grad_final * normed_last, 0),
        ]
    )
    returned, vector_grad = advance((returned, vector_grad), live)
    returned, vector_grad = advance((returned, vector_grad), scale_live)
    own_vector = jnp.sum(
        lax.all_to_all(
            vector_grad.reshape(count, 1, -1), AXES, split_axis=0, concat_axis=0, tiled=True
        ),
        (0, 1),
    )
    grad_in_table, in_squares = scatter_features(returned, places, vocab)
    in_squares = run_all(in_squares, live)
    own_in = in_step.finished()
    grads = (grad_in_table, grad_out_table, own_in, own_up, own_mix, own_vector)
    squares = jnp.sum(in_squares) + out_squares
    squares = squares + sum((jnp.sum(gradient * gradient) for gradient in grads[2:]))
    both = jnp.sum(shared_by_all(jnp.stack([squares, loss_part])[None], count), (0, 1))
    advance(jnp.zeros((), full_type), scale_live)
    grad_norm = jnp.sqrt(both[0])
    loss_value = both[1]
    factor = jnp.minimum(1.0, clip_limit / (grad_norm + 1e-06))
    step_value = step_count[0].astype(full_type)
    weights = (embed_in, embed_out, proj_in, proj_up, proj_mix, vector_params)
    firsts = (
        embed_in_first,
        embed_out_first,
        proj_in_first,
        proj_up_first,
        proj_mix_first,
        vector_first,
    )
    seconds = (
        embed_in_second,
        embed_out_second,
        proj_in_second,
        proj_up_second,
        proj_mix_second,
        vector_second,
    )
    updates = []
    for index, (weight, moment_one, moment_two, rate) in enumerate(zip(weights, firsts, seconds, step_rates)):
        gradient = grads[index]
        if index in (1, 2):
            updates[-1], gradient = advance((updates[-1], gradient), scale_live)
        updates.append(adam_update(weight, gradient * factor, moment_one, moment_two, rate, step_value))
    run_all(loss_value, scale_live)
    eigen_scales = scale_step.finished() / float(micro_count * count * DOCS)
    results = [value for update in updates for value in update]
    return tuple(results) + (loss_value, grad_norm, eigen_scales)


def solution(mesh):
    in_specs = (
        P(),
        P(),
        P(None, ("dp", "fsdp"), None),
        P(None, ("dp", "fsdp"), None),
        P(),
        P(),
        P(("dp", "fsdp"), None),
        P(("dp", "fsdp"), None),
        P(("dp", "fsdp"), None),
        P(("dp", "fsdp"), None),
        P(("dp", "fsdp"), None),
        P(("dp", "fsdp"), None),
        P(("dp", "fsdp"), None),
        P(("dp", "fsdp"), None),
        P(("dp", "fsdp"), None),
        P(("dp", "fsdp"), None),
        P(("dp", "fsdp"), None),
        P(("dp", "fsdp"), None),
        P(("dp", "fsdp"), None),
        P(("dp", "fsdp"), None),
        P(("dp", "fsdp"), None),
        P(("dp", "fsdp")),
        P(("dp", "fsdp")),
        P(("dp", "fsdp")),
        P(),
        P(),
    )
    out_specs = (
        P(("dp", "fsdp"), None),
        P(("dp", "fsdp"), None),
        P(("dp", "fsdp"), None),
        P(("dp", "fsdp"), None),
        P(("dp", "fsdp"), None),
        P(("dp", "fsdp"), None),
        P(("dp", "fsdp"), None),
        P(("dp", "fsdp"), None),
        P(("dp", "fsdp"), None),
        P(("dp", "fsdp"), None),
        P(("dp", "fsdp"), None),
        P(("dp", "fsdp"), None),
        P(("dp", "fsdp"), None),
        P(("dp", "fsdp"), None),
        P(("dp", "fsdp"), None),
        P(("dp", "fsdp")),
        P(("dp", "fsdp")),
        P(("dp", "fsdp")),
        P(),
        P(),
        P(("dp", "fsdp"), None),
    )
    return jax.shard_map(
        per_device, mesh=mesh, in_specs=in_specs, out_specs=out_specs, check_vma=False
    )
```

```python
import math

import jax
import jax.numpy as jnp
from jax import lax
from jax.experimental import pallas as pl
from jax.experimental.pallas import tpu as pltpu
from jax.sharding import PartitionSpec as P

HEADS = 12
ROT = 16
DOCS = 4


half_type = jnp.bfloat16
full_type = jnp.float32
clip_limit = 0.01
decay_first = 0.9
decay_second = 0.95
adam_epsilon = 1e-08
weight_decay = 0.01
step_rates = (1.0, 0.07, 0.04, 0.04, 0.04, 0.3)


def split_vector(vector, width, hidden):
    lengths = (3 * width, hidden, width, width, width, width, width, width, width)
    pieces = []
    offset = 0
    for length in lengths:
        pieces.append(vector[offset : offset + length])
        offset = offset + length
    return pieces


def normalize(inputs):
    centred = inputs - jnp.mean(inputs, 1, keepdims=True)
    inv_std = lax.rsqrt(jnp.mean(centred * centred, 1, keepdims=True) + 1e-05)
    return (centred * inv_std, inv_std)


def norm_back(grad_out, normed, inv_std):
    return inv_std * (
        grad_out
        - jnp.mean(grad_out, 1, keepdims=True)
        - normed * jnp.mean(grad_out * normed, 1, keepdims=True)
    )


def gelu_slope(inputs):
    return 0.5 * (1.0 + lax.erf(inputs * (1.0 / math.sqrt(2.0)))) + inputs * jnp.exp(
        -0.5 * inputs * inputs
    ) * (1.0 / math.sqrt(2.0 * math.pi))


LANES = 128


def lane_pack(width):
    pad = 8
    while pad < width:
        pad *= 2
    return (pad, LANES // pad)


def copies_matrix(width, dtype):
    pad, _ = lane_pack(width)
    feature = lax.broadcasted_iota(jnp.int32, (width, LANES), 0)
    lane = lax.broadcasted_iota(jnp.int32, (width, LANES), 1)
    return jnp.where(lane % pad == feature, 1.0, 0.0).astype(dtype)


def gather_kernel(ids_ref, table_ref, out_ref, rows_ref, stage_ref):
    width, vocab = table_ref.shape
    tokens = ids_ref.shape[2]
    pad, groups = lane_pack(width)
    stride = tokens // groups

    @pl.when(pl.program_id(0) == 0)
    def _():
        chunks = vocab // LANES
        many = 16
        filler = jnp.zeros((pad - width, LANES), full_type)

        def build(start):
            piece = table_ref[:, pl.ds(start, LANES)].astype(half_type).astype(full_type)
            tall = jnp.concatenate([piece, filler] * groups, 0) if pad > width else jnp.concatenate([piece] * groups, 0)
            rows_ref[pl.ds(start, LANES), :] = jnp.transpose(tall)

        def several(block, carry):
            for inner in range(many):
                build(pl.multiple_of((block * many + inner) * LANES, LANES))
            return carry

        lax.fori_loop(0, chunks // many, several, 0)
        for rest in range(chunks // many * many, chunks):
            build(rest * LANES)

    lane_group = lax.broadcasted_iota(jnp.int32, (1, LANES), 1) // pad
    unroll = 16

    def pick(block, carry):
        base = block * unroll
        for inner in range(unroll):
            row = None
            for group in range(groups):
                found = rows_ref[pl.ds(ids_ref[0, 0, group * stride + base + inner], 1), :]
                row = found if row is None else jnp.where(lane_group == group, found, row)
            stage_ref[pl.ds(base + inner, 1), :] = row
        return carry

    lax.fori_loop(0, stride // unroll, pick, 0)
    turned = jnp.transpose(stage_ref[...])
    for group in range(groups):
        out_ref[0, :, group * stride : (group + 1) * stride] = turned[
            group * pad : group * pad + width, :
        ].astype(half_type)


def gather_features(table, ids):
    width, vocab = table.shape
    count, _, tokens = ids.shape
    _, groups = lane_pack(width)
    return pl.pallas_call(
        gather_kernel,
        out_shape=jax.ShapeDtypeStruct((count, width, tokens), half_type),
        grid=(count,),
        in_specs=[
            pl.BlockSpec((1, 1, tokens), lambda i: (i, 0, 0), memory_space=pltpu.SMEM),
            pl.BlockSpec((width, vocab), lambda i: (0, 0), pipeline_mode=pl.Buffered(1)),
        ],
        out_specs=pl.BlockSpec((1, width, tokens), lambda i: (i, 0, 0)),
        scratch_shapes=[
            pltpu.VMEM((vocab, LANES), full_type),
            pltpu.VMEM((tokens // groups, LANES), full_type),
        ],
        compiler_params=pltpu.CompilerParams(
            dimension_semantics=("arbitrary",), vmem_limit_bytes=44 * 1024 * 1024
        ),
    )(ids, table)


def quarter(vocab, groups):
    return -(-vocab // (groups * LANES)) * LANES


def scatter_kernel(places_ref, groups_ref, grad_ref, out_ref, square_ref, mask_ref, stage_ref, *sums):
    width, vocab = out_ref.shape
    runs, _, tokens = places_ref.shape
    pad, groups = lane_pack(width)
    shift = groups.bit_length() - 1
    span = quarter(vocab, groups)

    @pl.when(pl.program_id(0) == 0)
    def _():
        lane_group = lax.broadcasted_iota(jnp.int32, mask_ref.shape, 1) // pad
        mask_ref[...] = jnp.where(
            lane_group == lax.broadcasted_iota(jnp.int32, mask_ref.shape, 0), 1.0, 0.0
        )

        def clear(block, carry):
            start = pl.multiple_of(block * LANES, LANES)
            for total in sums:
                total[pl.ds(start, LANES), :] = jnp.zeros((LANES, LANES), full_type)
            return carry

        lax.fori_loop(0, span // LANES, clear, 0)

    spread = copies_matrix(width, half_type)
    for run in range(runs):
        stage_ref[run] = lax.dot_general(
            grad_ref[run], spread, (((0,), (0,)), ((), ())), preferred_element_type=full_type
        )
    unroll = 32

    def add(block, carry):
        base = block * unroll
        for inner in range(unroll):
            rows = [pl.ds(places_ref[run, 0, base + inner], 1) for run in range(runs)]
            new = [
                sums[run][rows[run], :]
                + stage_ref[run, pl.ds(base + inner, 1), :] * mask_ref[pl.ds(groups_ref[run, 0, base + inner], 1), :]
                for run in range(runs)
            ]
            for run in range(runs):
                sums[run][rows[run], :] = new[run]
        return carry

    lax.fori_loop(0, tokens // unroll, add, 0)

    @pl.when(pl.program_id(0) == pl.num_programs(0) - 1)
    def _():
        def finish(block, squares):
            start = pl.multiple_of(block * LANES, LANES)
            whole = sums[0][pl.ds(start, LANES), :]
            for total in sums[1:]:
                whole = whole + total[pl.ds(start, LANES), :]
            turned = jnp.transpose(whole)
            for group in range(groups):
                column = pl.multiple_of(group * span + start, LANES)

                @pl.when(column < vocab)
                def _():
                    out_ref[:, pl.ds(column, LANES)] = turned[group * pad : group * pad + width, :]

            return squares + jnp.sum((whole * whole).reshape(LANES // 8, 8, LANES), 0)

        square_ref[...] = lax.fori_loop(0, span // LANES, finish, jnp.zeros((8, LANES), full_type))


def scatter_features(grads, places, vocab):
    count, width, tokens = grads.shape
    pad, groups = lane_pack(width)
    runs = 4
    return pl.pallas_call(
        scatter_kernel,
        out_shape=(
            jax.ShapeDtypeStruct((width, vocab), full_type),
            jax.ShapeDtypeStruct((8, LANES), full_type),
        ),
        grid=(count // runs,),
        in_specs=[
            pl.BlockSpec((runs, 1, tokens), lambda i: (i, 0, 0), memory_space=pltpu.SMEM),
            pl.BlockSpec((runs, 1, tokens), lambda i: (i, 0, 0), memory_space=pltpu.SMEM),
            pl.BlockSpec((runs, width, tokens), lambda i: (i, 0, 0)),
        ],
        out_specs=(
            pl.BlockSpec((width, vocab), lambda i: (0, 0)),
            pl.BlockSpec((8, LANES), lambda i: (0, 0)),
        ),
        scratch_shapes=[
            pltpu.VMEM((max(8, groups), LANES), full_type),
            pltpu.VMEM((runs, tokens, LANES), full_type),
        ]
        + [pltpu.VMEM((quarter(vocab, groups), LANES), full_type) for _ in range(runs)],
        compiler_params=pltpu.CompilerParams(
            dimension_semantics=("arbitrary",), vmem_limit_bytes=52 * 1024 * 1024
        ),
    )(places[0], places[1], grads)


def scatter_places(ids, width, vocab):
    _, groups = lane_pack(width)
    span = quarter(vocab, groups)
    return (ids % span, ids // span)


def turn_tables(row_length, head_width):
    halfway = ROT // 2
    dims = jnp.arange(LANES) % head_width
    inverse = 10000.0 ** (-2.0 * (dims % halfway).astype(full_type) / ROT)
    angles = jnp.arange(row_length, dtype=full_type)[:, None] * inverse[None, :]
    cosine = jnp.where(dims < ROT, jnp.cos(angles), 1.0)
    above = jnp.where(dims < halfway, -jnp.sin(angles), 0.0)
    below = jnp.where((dims >= halfway) & (dims < ROT), jnp.sin(angles), 0.0)
    return jnp.stack([cosine, above, below], 0)


def turned(values_in, tables_ref, forward):
    halfway = ROT // 2
    higher = pltpu.roll(values_in, LANES - halfway, 1) * tables_ref[1]
    lower = pltpu.roll(values_in, halfway, 1) * tables_ref[2]
    straight = values_in * tables_ref[0]
    return straight + (higher + lower) if forward else straight - (higher + lower)


def dot_of(left, right, dims):
    return lax.dot_general(left, right, (dims, ((), ())), preferred_element_type=full_type)


def key_window(block, block_rows):
    return (block + 1) * block_rows


def allowed_block(row_ref, column_ref, block, block_rows):
    reach = key_window(block, block_rows)
    start = block * block_rows
    key_place = lax.broadcasted_iota(jnp.int32, (reach, block_rows), 0)
    query_place = start + lax.broadcasted_iota(jnp.int32, (reach, block_rows), 1)
    same = column_ref[0, :reach, :] == row_ref[0, :, start : start + block_rows]
    return (key_place <= query_place) & same


def forward_kernel(
    query_in, key_in, value_in, tables_ref, row_ref, column_ref, context_ref, query_ref, key_ref, value_ref, logsum_ref
):
    row_length = query_in.shape[0]
    head_width = LANES // 2
    block_rows = row_length // 2
    scale = 1.0 / math.sqrt(head_width)
    query_ref[...] = turned(query_in[...], tables_ref, True).astype(half_type)
    key_ref[...] = turned(key_in[...], tables_ref, True).astype(half_type)
    value_ref[...] = value_in[...].astype(half_type)
    for block in range(2):
        start = block * block_rows
        reach = key_window(block, block_rows)
        allowed = allowed_block(row_ref, column_ref, block, block_rows)
        for head in range(2):
            lanes = slice(head * head_width, (head + 1) * head_width)
            scores = dot_of(key_ref[:reach, lanes], query_ref[start : start + block_rows, lanes], ((1,), (1,)))
            scores = jnp.where(allowed, scores * scale, -1e30)
            peak = jnp.max(scores, 0, keepdims=True)
            powers = jnp.exp(scores - peak)
            total = jnp.sum(powers, 0, keepdims=True)
            logsum_ref[0, 0, head : head + 1, start : start + block_rows] = peak + jnp.log(total)
            weights_soft = (powers * (1.0 / total)).astype(half_type)
            context_ref[start : start + block_rows, lanes] = dot_of(
                weights_soft, value_ref[:reach, lanes], ((0,), (0,))
            ).astype(half_type)


def attention_specs(row_length, pairs):
    def part(offset):
        return pl.BlockSpec((row_length, LANES), lambda m, h: (m, offset * pairs + h))

    tables = pl.BlockSpec((3, row_length, LANES), lambda m, h: (0, 0, 0))
    row = pl.BlockSpec((1, 1, row_length), lambda m, h: (m, 0, 0))
    column = pl.BlockSpec((1, row_length, 1), lambda m, h: (m, 0, 0))
    logsum = pl.BlockSpec((1, 1, 2, row_length), lambda m, h: (m, h, 0, 0))
    return (part, tables, row, column, logsum)


def attention_forward(mixed, tables, segments):
    micro_count, row_length = segments.shape
    tokens = mixed.shape[0]
    width = mixed.shape[1] // 3
    pairs = width // LANES
    part, tables_spec, row, column, logsum = attention_specs(row_length, pairs)
    flat = jax.ShapeDtypeStruct((tokens, width), half_type)
    return pl.pallas_call(
        forward_kernel,
        out_shape=(flat, flat, flat, flat, jax.ShapeDtypeStruct((micro_count, pairs, 2, row_length), full_type)),
        grid=(micro_count, pairs),
        in_specs=[part(0), part(1), part(2), tables_spec, row, column],
        out_specs=(part(0), part(0), part(0), part(0), logsum),
        compiler_params=pltpu.CompilerParams(
            dimension_semantics=("arbitrary", "arbitrary"), vmem_limit_bytes=40 * 1024 * 1024
        ),
    )(mixed, mixed, mixed, tables, segments[:, None, :], segments[:, :, None])


def backward_kernel(
    query_ref, key_ref, value_ref, grad_ref, tables_ref, row_ref, column_ref, logsum_ref, out_ref, query_sum, key_sum, value_sum
):
    row_length = query_ref.shape[0]
    head_width = LANES // 2
    block_rows = row_length // 2
    scale = 1.0 / math.sqrt(head_width)
    for block in reversed(range(2)):
        start = block * block_rows
        reach = key_window(block, block_rows)
        rows = slice(start, start + block_rows)
        allowed = allowed_block(row_ref, column_ref, block, block_rows)
        for head in range(2):
            lanes = slice(head * head_width, (head + 1) * head_width)
            query = query_ref[rows, lanes]
            key = key_ref[:reach, lanes]
            grad = grad_ref[rows, lanes]
            scores = jnp.where(allowed, dot_of(key, query, ((1,), (1,))) * scale, -1e30)
            weights_soft = jnp.exp(scores - logsum_ref[0, 0, head : head + 1, rows])
            grad_value = dot_of(weights_soft.astype(half_type), grad, ((1,), (0,)))
            grad_weights = dot_of(value_ref[:reach, lanes], grad, ((1,), (1,)))
            leaning = jnp.sum(weights_soft * grad_weights, 0, keepdims=True)
            grad_scores = (weights_soft * (grad_weights - leaning)).astype(half_type)
            query_sum[rows, lanes] = dot_of(grad_scores, key, ((0,), (0,))) * scale
            grad_key = dot_of(grad_scores, query, ((1,), (0,))) * scale
            if block == 1:
                value_sum[:, lanes] = grad_value
                key_sum[:, lanes] = grad_key
            else:
                value_sum[:reach, lanes] = value_sum[:reach, lanes] + grad_value
                key_sum[:reach, lanes] = key_sum[:reach, lanes] + grad_key
    out_ref[0] = turned(query_sum[...], tables_ref, False).astype(half_type)
    out_ref[1] = turned(key_sum[...], tables_ref, False).astype(half_type)
    out_ref[2] = value_sum[...].astype(half_type)


def attention_backward(queries, keys_all, values_all, grad_context, logsum, tables, segments):
    micro_count, row_length = segments.shape
    tokens, width = queries.shape
    pairs = width // LANES
    part, tables_spec, row, column, logsum_spec = attention_specs(row_length, pairs)
    return pl.pallas_call(
        backward_kernel,
        out_shape=jax.ShapeDtypeStruct((3, tokens, width), half_type),
        grid=(micro_count, pairs),
        in_specs=[part(0), part(0), part(0), part(0), tables_spec, row, column, logsum_spec],
        out_specs=pl.BlockSpec((3, row_length, LANES), lambda m, h: (0, m, h)),
        scratch_shapes=[pltpu.VMEM((row_length, LANES), full_type) for _ in range(3)],
        compiler_params=pltpu.CompilerParams(
            dimension_semantics=("arbitrary", "arbitrary"), vmem_limit_bytes=40 * 1024 * 1024
        ),
    )(queries, keys_all, values_all, grad_context, tables, segments[:, None, :], segments[:, :, None], logsum)


def document_kernel(
    starts_ref, total_ref, in_ref, out_ref, other_ref, own_ref, turned_ref, shift_ref, window_ref
):
    micro_count, docs = starts_ref.shape[0], starts_ref.shape[1] - 1
    row_length = in_ref.shape[0] // micro_count
    reach = row_length // 2
    step = 16
    half = other_ref.shape[0]
    places = [(micro, doc) for micro in range(micro_count) for doc in range(docs)]

    def bounds(micro, doc):
        start, end = starts_ref[micro, doc], starts_ref[micro, doc + 1]
        window = jnp.minimum((start // step) * step, row_length - reach)
        base = pl.multiple_of(micro * row_length + window, step)
        return (start - window, end - window, base)

    @pl.when(pl.program_id(0) == 0)
    def _():
        row = lax.broadcasted_iota(jnp.int32, (reach, in_ref.shape[1]), 0)
        for place, (micro, doc) in enumerate(places):
            begin, end, base = bounds(micro, doc)

            @pl.when(end <= reach)
            def _():
                rows = in_ref[pl.ds(base, reach), :].astype(full_type)
                kept = jnp.where((row >= begin) & (row < end), rows, 0.0)
                turned_ref[place] = jnp.transpose(kept).astype(half_type)

            @pl.when(end > reach)
            def _():
                to = lax.broadcasted_iota(jnp.int32, (reach, reach + step), 0)
                source = lax.broadcasted_iota(jnp.int32, (reach, reach + step), 1)
                shift_ref[place] = jnp.where(to + begin == source, 1.0, 0.0).astype(half_type)
                rows = dot_of(shift_ref[place], in_ref[pl.ds(base, reach + step), :], ((1,), (0,)))
                kept = jnp.where(row < end - begin, rows, 0.0)
                turned_ref[place] = jnp.transpose(kept).astype(half_type)

    for place, (micro, doc) in enumerate(places):
        begin, end, base = bounds(micro, doc)

        @pl.when(end <= reach)
        def _():
            window_ref[place] = out_ref[pl.ds(base, reach), :]

        @pl.when(end > reach)
        def _():
            window_ref[place] = dot_of(
                shift_ref[place], out_ref[pl.ds(base, reach + step), :], ((1,), (0,))
            ).astype(half_type)

    total = total_ref[0]
    parts = 2
    rows = half // parts
    for part in range(2 * parts):
        found = None
        for place in range(len(places)):
            block = dot_of(
                turned_ref[place, part * rows : (part + 1) * rows, :], window_ref[place], ((1,), (0,))
            )
            block = (block * total).astype(half_type).astype(full_type)
            found = block * block if found is None else found + block * block
        target = other_ref if part < parts else own_ref
        start = (part % parts) * rows
        target[start : start + rows, :] = found


def document_squares(rot_in, rot_out, segments, total):
    micro_count, row_length = segments.shape
    tokens, width = rot_in.shape
    hidden = rot_out.shape[1]
    tile = 2 * LANES
    slots = jnp.arange(DOCS + 1)
    starts = jnp.sum(segments[:, :, None] < slots[None, None, :], 1).astype(jnp.int32)
    return pl.pallas_call(
        document_kernel,
        out_shape=(jax.ShapeDtypeStruct((width // 2, hidden), full_type),) * 2,
        grid=(hidden // tile,),
        in_specs=[
            pl.BlockSpec(memory_space=pltpu.SMEM),
            pl.BlockSpec(memory_space=pltpu.SMEM),
            pl.BlockSpec((tokens, width), lambda i: (0, 0)),
            pl.BlockSpec((tokens, tile), lambda i: (0, i)),
        ],
        out_specs=(pl.BlockSpec((width // 2, tile), lambda i: (0, i)),) * 2,
        scratch_shapes=[
            pltpu.VMEM((micro_count * DOCS, width, row_length // 2), half_type),
            pltpu.VMEM((micro_count * DOCS, row_length // 2, row_length // 2 + 16), half_type),
            pltpu.VMEM((micro_count * DOCS, row_length // 2, tile), half_type),
        ],
        compiler_params=pltpu.CompilerParams(
            dimension_semantics=("arbitrary",), vmem_limit_bytes=40 * 1024 * 1024
        ),
    )(starts, total.reshape(1), rot_in, rot_out)


AXES = ("dp", "fsdp")


def partner_pairs(count, bit):
    return [(place, place ^ (1 << bit)) for place in range(count)]


class Stream:
    def __init__(self, chunks, order, left, wire, relative=False):
        self.held = chunks.reshape((2,) * len(order) + chunks.shape[1:])
        self.left = list(left)
        self.order = list(order)
        self.wire = wire
        self.relative = relative
        self.sent = self.kept = self.got = None

    def land(self, arrived):
        self.held = self.kept + arrived.astype(full_type)
        self.got = None
        return [self]

    def split(self):
        bit = self.order[0]
        axis = self.left.index(bit)
        mine = 0 if self.relative else (lax.axis_index(AXES) >> bit) & 1
        self.sent = lax.dynamic_index_in_dim(self.held, 1 - mine, axis, keepdims=False).astype(self.wire)
        self.kept = lax.dynamic_index_in_dim(self.held, mine, axis, keepdims=False)
        self.left.pop(axis)

    def send(self, ready):
        self.got = lax.ppermute(ready, AXES, partner_pairs(lax.axis_size(AXES), self.order.pop(0)))


class FirstStep:
    def __init__(self, other, own, rows, wire):
        self.sent, self.kept, self.rows, self.wire = other, own, rows, wire
        self.order = [0]
        self.got = None
        self.streams = None

    def land(self, arrived):
        held = (self.kept + arrived).reshape(-1, self.rows, self.kept.shape[1])
        half = held.shape[2] // 2
        bits = lax.axis_size(AXES).bit_length() - 1
        order_a, order_b = link_orders(bits)
        left = range(bits - 1, 0, -1)
        self.got = None
        self.streams = [
            Stream(held[:, :, :half], order_a[1:], left, self.wire),
            Stream(held[:, :, half:], order_b[1:], left, self.wire),
        ]
        return self.streams

    def split(self):
        pass

    def send(self, ready):
        self.order = []
        self.got = lax.ppermute(ready, AXES, partner_pairs(lax.axis_size(AXES), 0))

    def finished(self):
        return jnp.concatenate([stream.held for stream in self.streams], 1)


def advance(anchor, live):
    flying = [stream for stream in live if stream.got is not None]
    anchor, landed = lax.optimization_barrier((anchor, [stream.got for stream in flying]))
    going = [stream for stream in live if stream.got is None]
    for stream, arrived in zip(flying, landed):
        going.extend(stream.land(arrived))
    going = [stream for stream in going if stream.order]
    for stream in going:
        stream.split()
    anchor, ready = lax.optimization_barrier((anchor, [stream.sent for stream in going]))
    for stream, block in zip(going, ready):
        stream.send(block)
    live[:] = going
    return anchor


def run_all(anchor, live):
    while live:
        anchor = advance(anchor, live)
    return anchor


def pair_first(width, rows, place):
    to = lax.broadcasted_iota(jnp.int32, (width, width), 1)
    source = lax.broadcasted_iota(jnp.int32, (width, width), 0)
    core = jnp.where(to < width // 2, 1 - (place & 1), place & 1)
    inside = to % (width // 2)
    wanted = (inside // rows) * (2 * rows) + core * rows + inside % rows
    return (source == wanted).astype(half_type)


def link_orders(bits):
    near = list(range(1, bits - 2))
    return ([0, bits - 2, bits - 1] + near, [0, bits - 1, bits - 2] + near)


def flipped(folded, place):
    bits = lax.axis_size(AXES).bit_length() - 1
    for axis in range(bits):
        mine = (place >> (bits - 1 - axis)) & 1
        folded = jnp.where(mine == 1, jnp.flip(folded, axis), folded)
    return folded


def by_device(stacked, order, place):
    bits = len(order)
    folded = stacked.reshape((2,) * bits + stacked.shape[1:])
    natural = [order.index(bit) for bit in range(bits - 1, -1, -1)]
    folded = jnp.transpose(folded, natural + list(range(bits, folded.ndim)))
    return flipped(folded, place).reshape(stacked.shape)


def by_partner(ordered, order, place):
    bits = len(order)
    folded = flipped(ordered.reshape((2,) * bits + ordered.shape[1:]), place)
    stacked = [bits - 1 - bit for bit in order]
    folded = jnp.transpose(folded, stacked + list(range(bits, folded.ndim)))
    return folded.reshape(ordered.shape)


def gather_trees(blocks, orders):
    held = [block[None] for block in blocks]
    for step in range(len(orders[0])):
        for m, order in enumerate(orders):
            count = 1 << len(order)
            arrived = lax.ppermute(held[m], AXES, partner_pairs(count, order[-1 - step]))
            held[m] = jnp.concatenate([held[m], arrived], 0)
    return held


def shared_by_all(own, count):
    return lax.all_to_all(
        jnp.broadcast_to(own[None], (count,) + own.shape), AXES, split_axis=0, concat_axis=0, tiled=True
    )


def adam_update(weight, gradient, moment_one, moment_two, rate, step_value):
    next_one = decay_first * moment_one + (1.0 - decay_first) * gradient
    next_two = decay_second * moment_two + (1.0 - decay_second) * gradient * gradient
    fix_one = 1.0 - decay_first**step_value
    fix_two = 1.0 - decay_second**step_value
    update = next_one / fix_one / (jnp.sqrt(next_two / fix_two) + adam_epsilon)
    return [weight - rate * (update + weight_decay * weight), next_one, next_two]


def per_device(
    step_count,
    token_ids,
    segment_ids,
    loss_positions,
    label_ids,
    label_mask,
    embed_in,
    embed_in_first,
    embed_in_second,
    embed_out,
    embed_out_first,
    embed_out_second,
    proj_in,
    proj_in_first,
    proj_in_second,
    proj_up,
    proj_up_first,
    proj_up_second,
    proj_mix,
    proj_mix_first,
    proj_mix_second,
    vector_params,
    vector_first,
    vector_second,
    basis_in,
    basis_out,
):
    micro_count = token_ids.shape[0]
    row_length = token_ids.shape[2]
    pick_count = loss_positions.shape[2]
    tokens = micro_count * row_length
    count = lax.axis_size(AXES)
    total = jnp.maximum(jnp.sum(label_mask.astype(full_type)), 1.0)
    vocab = embed_in.shape[1]
    own_width = embed_in.shape[0]
    width = proj_mix.shape[1]
    hidden = proj_up.shape[1]
    head_width = width // HEADS

    place = lax.axis_index(AXES)
    flat_ids = jnp.transpose(token_ids, (1, 0, 2)).reshape(-1)
    ids_by_run = flat_ids.reshape(count, 1, tokens)
    columns = gather_features(embed_in, ids_by_run)
    arrived = lax.all_to_all(columns, AXES, split_axis=0, concat_axis=0, tiled=True)
    embedded = arrived.reshape(width, tokens).T.astype(full_type)
    places = scatter_places(ids_by_run, own_width, vocab)

    small = vector_params.astype(half_type).reshape(own_width, -1)
    each = small.shape[1]
    small = jnp.pad(small, ((0, 0), (0, -each % LANES)))
    both = jnp.concatenate([proj_in.astype(half_type), proj_up.astype(half_type), small], 1)
    both = lax.all_gather(both, AXES, axis=0, tiled=True)
    weight_in, weight_up = both[:, : 3 * width], both[:, 3 * width : 3 * width + hidden]
    weight_mix = lax.all_gather(proj_mix.astype(half_type), AXES, axis=0, tiled=True)
    vector = both[:, 3 * width + hidden : 3 * width + hidden + each].reshape(-1).astype(full_type)
    pairing = pair_first(width, own_width, place)
    basis_paired = jnp.dot(basis_in, pairing, preferred_element_type=full_type).astype(half_type)
    (
        bias_in,
        bias_up,
        bias_mix,
        shift_first,
        shift_second,
        shift_last,
        gain_first,
        gain_second,
        gain_last,
    ) = split_vector(vector, width, hidden)

    segments = segment_ids[:, 0]
    picks = loss_positions[:, 0] + row_length * jnp.arange(micro_count)[:, None]
    picks = picks.reshape(-1)

    normed, inv_std = normalize(embedded)
    first_in = (normed * gain_first + shift_first).astype(half_type)
    second_in = (normed * gain_second + shift_second).astype(half_type)
    mixed = jnp.dot(first_in, weight_in, preferred_element_type=full_type) + bias_in
    tables = turn_tables(row_length, head_width)
    context, queries, keys_all, values_all, logsum = attention_forward(mixed, tables, segments)
    hidden_pre = jnp.dot(second_in, weight_up, preferred_element_type=full_type) + bias_up
    active = (hidden_pre * (0.5 + 0.5 * lax.erf(hidden_pre * (1.0 / math.sqrt(2.0))))).astype(half_type)
    joined = jnp.concatenate([context, active], 1)
    residual = embedded + jnp.dot(joined, weight_mix, preferred_element_type=full_type) + bias_mix
    normed_last, inv_last = normalize(residual)
    final = normed_last * gain_last + shift_last
    picked = jnp.take(final, picks, axis=0, mode="clip").astype(half_type)

    bits = count.bit_length() - 1
    orders = link_orders(bits)
    picked = picked.reshape(micro_count, pick_count, width)
    gathered = jnp.stack(gather_trees(picked, orders)).reshape(-1, width)
    table_out = embed_out.astype(half_type)
    vocab_rows = embed_out.shape[0]
    vocab_ids = place * vocab_rows + jnp.arange(vocab_rows)
    labels_flat = jnp.stack([by_partner(label_ids[m], orders[m], place) for m in range(micro_count)]).reshape(-1)
    mask_flat = jnp.stack([by_partner(label_mask[m], orders[m], place) for m in range(micro_count)]).reshape(-1)
    mask_flat = mask_flat.astype(full_type)
    logits = jnp.einsum("rd,vd->rv", gathered, table_out, preferred_element_type=full_type)
    matches = labels_flat[:, None] == vocab_ids[None, :]
    label_part = jnp.sum(jnp.where(matches, logits, 0.0), 1)
    local_max = jnp.max(logits, 1)
    local_sum = jnp.sum(jnp.exp(logits - local_max[:, None]), 1)
    parts = jnp.stack([local_max, local_sum, label_part], 0).reshape(3, micro_count, count, pick_count)
    parts = jnp.transpose(parts, (1, 2, 0, 3))
    parts = jnp.stack([by_device(parts[m], orders[m], place) for m in range(micro_count)], 1)
    parts = lax.all_to_all(
        parts.reshape(count, 1, -1), AXES, split_axis=0, concat_axis=0, tiled=True
    ).reshape(count, micro_count, 3, pick_count)
    peak = jnp.max(parts[:, :, 0], 0)
    own_logsum = peak + jnp.log(jnp.sum(parts[:, :, 1] * jnp.exp(parts[:, :, 0] - peak[None]), 0))
    own_mask = lax.dynamic_index_in_dim(label_mask, place, 1, keepdims=False).astype(full_type)
    loss_part = jnp.sum(own_mask * (own_logsum - jnp.sum(parts[:, :, 2], 0))) / total
    logsum_all = shared_by_all(own_logsum.reshape(1, -1), count).reshape(count, micro_count, pick_count)
    logsum_all = jnp.stack([by_partner(logsum_all[:, m], orders[m], place) for m in range(micro_count)]).reshape(-1)
    grad_logits = (
        (jnp.exp(logits - logsum_all[:, None]) - matches.astype(full_type))
        * (mask_flat / total)[:, None]
    ).astype(half_type)
    back = jnp.dot(grad_logits, table_out, preferred_element_type=full_type)
    back = back.reshape(micro_count, count, pick_count, width)
    pick_streams = [
        Stream(back[m], orders[m], orders[m], full_type, relative=True) for m in range(micro_count)
    ]
    live = list(pick_streams)
    grad_logits = advance(grad_logits, live)
    grad_out_table = jnp.einsum("rv,rd->vd", grad_logits, gathered, preferred_element_type=full_type)
    out_squares = jnp.sum(grad_out_table * grad_out_table)
    second_paired, out_squares = advance((second_in, out_squares), live)
    rot_in = jnp.dot(second_paired, basis_paired, preferred_element_type=full_type).astype(half_type)
    first_turned = lax.dot_general(
        pairing, first_in, (((0,), (1,)), ((), ())), preferred_element_type=full_type
    ).astype(half_type)
    rot_in, first_turned = advance((rot_in, first_turned), live)
    run_all(jnp.zeros((), full_type), live)
    grad_picked = jnp.concatenate([stream.held for stream in pick_streams], 0)

    grad_final = jnp.zeros((tokens, width), full_type).at[picks].add(grad_picked)
    grad_residual = norm_back(grad_final * gain_last, normed_last, inv_last)
    grad_branch = grad_residual.astype(half_type)
    grad_mix = jnp.einsum("sa,sb->ab", joined, grad_branch, preferred_element_type=full_type)
    grad_branch, grad_mix = lax.optimization_barrier((grad_branch, grad_mix))
    own_mix = lax.psum_scatter(grad_mix, AXES, scatter_dimension=0, tiled=True)
    grad_joined = jnp.einsum("sb,ab->sa", grad_branch, weight_mix, preferred_element_type=full_type)
    grad_context = grad_joined[:, :width].astype(half_type)
    grad_parts = attention_backward(
        queries, keys_all, values_all, grad_context, logsum, tables, segments
    )
    grad_mixed = jnp.concatenate([grad_parts[0], grad_parts[1], grad_parts[2]], 1)
    in_other = jnp.dot(first_turned[: width // 2], grad_mixed, preferred_element_type=full_type)
    in_own = jnp.dot(first_turned[width // 2 :], grad_mixed, preferred_element_type=full_type)
    in_step = FirstStep(in_other, in_own, own_width, full_type)
    live = [in_step]
    grad_joined = advance(grad_joined, live)
    grad_hidden = (grad_joined[:, width:] * gelu_slope(hidden_pre)).astype(half_type)
    grad_hidden = advance(grad_hidden, live)
    grad_up = jnp.einsum("sa,sb->ab", second_in, grad_hidden, preferred_element_type=full_type)
    grad_second = jnp.einsum("sb,ab->sa", grad_hidden, weight_up, preferred_element_type=full_type)
    grad_up, grad_second, grad_mixed = advance((grad_up, grad_second, grad_mixed), live)
    own_up = lax.psum_scatter(grad_up, AXES, scatter_dimension=0, tiled=True)
    grad_first = jnp.einsum("sb,ab->sa", grad_mixed, weight_in, preferred_element_type=full_type)
    grad_embedded = grad_residual + norm_back(
        grad_first * gain_first + grad_second * gain_second, normed, inv_std
    )
    vector_grad = jnp.concatenate(
        [
            jnp.sum(grad_mixed.astype(full_type), 0),
            jnp.sum(grad_hidden.astype(full_type), 0),
            jnp.sum(grad_residual, 0),
            jnp.sum(grad_first, 0),
            jnp.sum(grad_second, 0),
            jnp.sum(grad_final, 0),
            jnp.sum(grad_first * normed, 0),
            jnp.sum(grad_second * normed, 0),
            jnp.sum(grad_final * normed_last, 0),
        ]
    )
    sending = grad_embedded.astype(half_type).T.reshape(count, own_width, tokens)
    sending, grad_hidden_late, vector_grad = advance((sending, grad_hidden, vector_grad), live)
    returned = lax.all_to_all(sending, AXES, split_axis=0, concat_axis=0, tiled=True)
    rot_out = jnp.dot(grad_hidden_late, basis_out, preferred_element_type=full_type).astype(half_type)
    rot_out, vector_grad = lax.optimization_barrier((rot_out, vector_grad))
    vector_parts = lax.all_to_all(
        vector_grad.reshape(count, 1, -1), AXES, split_axis=0, concat_axis=0, tiled=True
    )
    scale_other, scale_own = document_squares(rot_in, rot_out, segments, total)
    scale_step = FirstStep(scale_other, scale_own, own_width, half_type)
    scale_live = [scale_step]
    returned, vector_parts = advance((returned, vector_parts), live)
    returned = advance(returned, scale_live)
    own_vector = jnp.sum(vector_parts, (0, 1))
    grad_in_table, in_squares = scatter_features(returned, places, vocab)
    in_squares = run_all(in_squares, live)
    own_in = in_step.finished()
    grads = (grad_in_table, grad_out_table, own_in, own_up, own_mix, own_vector)
    squares = jnp.sum(in_squares) + out_squares
    squares = squares + sum((jnp.sum(gradient * gradient) for gradient in grads[2:]))
    norm_parts = jnp.stack([squares, loss_part])
    both = jnp.sum(shared_by_all(norm_parts[None], count), (0, 1))
    advance(norm_parts, scale_live)
    both = advance(both, scale_live)
    grad_norm = jnp.sqrt(both[0])
    loss_value = both[1]
    factor = jnp.minimum(1.0, clip_limit / (grad_norm + 1e-06))
    step_value = step_count[0].astype(full_type)
    weights = (embed_in, embed_out, proj_in, proj_up, proj_mix, vector_params)
    firsts = (
        embed_in_first,
        embed_out_first,
        proj_in_first,
        proj_up_first,
        proj_mix_first,
        vector_first,
    )
    seconds = (
        embed_in_second,
        embed_out_second,
        proj_in_second,
        proj_up_second,
        proj_mix_second,
        vector_second,
    )
    updates = []
    for index, (weight, moment_one, moment_two, rate) in enumerate(zip(weights, firsts, seconds, step_rates)):
        gradient = grads[index]
        if index in (1, 2):
            updates[-1], gradient = advance((updates[-1], gradient), scale_live)
        updates.append(adam_update(weight, gradient * factor, moment_one, moment_two, rate, step_value))
    run_all(loss_value, scale_live)
    eigen_scales = scale_step.finished() / float(micro_count * count * DOCS)
    results = [value for update in updates for value in update]
    return tuple(results) + (loss_value, grad_norm, eigen_scales)


def solution(mesh):
    in_specs = (
        P(),
        P(),
        P(None, ("dp", "fsdp"), None),
        P(None, ("dp", "fsdp"), None),
        P(),
        P(),
        P(("dp", "fsdp"), None),
        P(("dp", "fsdp"), None),
        P(("dp", "fsdp"), None),
        P(("dp", "fsdp"), None),
        P(("dp", "fsdp"), None),
        P(("dp", "fsdp"), None),
        P(("dp", "fsdp"), None),
        P(("dp", "fsdp"), None),
        P(("dp", "fsdp"), None),
        P(("dp", "fsdp"), None),
        P(("dp", "fsdp"), None),
        P(("dp", "fsdp"), None),
        P(("dp", "fsdp"), None),
        P(("dp", "fsdp"), None),
        P(("dp", "fsdp"), None),
        P(("dp", "fsdp")),
        P(("dp", "fsdp")),
        P(("dp", "fsdp")),
        P(),
        P(),
    )
    out_specs = (
        P(("dp", "fsdp"), None),
        P(("dp", "fsdp"), None),
        P(("dp", "fsdp"), None),
        P(("dp", "fsdp"), None),
        P(("dp", "fsdp"), None),
        P(("dp", "fsdp"), None),
        P(("dp", "fsdp"), None),
        P(("dp", "fsdp"), None),
        P(("dp", "fsdp"), None),
        P(("dp", "fsdp"), None),
        P(("dp", "fsdp"), None),
        P(("dp", "fsdp"), None),
        P(("dp", "fsdp"), None),
        P(("dp", "fsdp"), None),
        P(("dp", "fsdp"), None),
        P(("dp", "fsdp")),
        P(("dp", "fsdp")),
        P(("dp", "fsdp")),
        P(),
        P(),
        P(("dp", "fsdp"), None),
    )
    return jax.shard_map(
        per_device, mesh=mesh, in_specs=in_specs, out_specs=out_specs, check_vma=False
    )
```

```python
import math

import jax
import jax.numpy as jnp
from jax import lax
from jax.experimental import pallas as pl
from jax.experimental.pallas import tpu as pltpu
from jax.sharding import PartitionSpec as P

HEADS = 12
ROT = 16
DOCS = 4


half_type = jnp.bfloat16
full_type = jnp.float32
clip_limit = 0.01
decay_first = 0.9
decay_second = 0.95
adam_epsilon = 1e-08
weight_decay = 0.01
step_rates = (1.0, 0.07, 0.04, 0.04, 0.04, 0.3)


def split_vector(vector, width, hidden):
    lengths = (3 * width, hidden, width, width, width, width, width, width, width)
    pieces = []
    offset = 0
    for length in lengths:
        pieces.append(vector[offset : offset + length])
        offset = offset + length
    return pieces


def normalize(inputs):
    centred = inputs - jnp.mean(inputs, 1, keepdims=True)
    inv_std = lax.rsqrt(jnp.mean(centred * centred, 1, keepdims=True) + 1e-05)
    return (centred * inv_std, inv_std)


def norm_back(grad_out, normed, inv_std):
    return inv_std * (
        grad_out
        - jnp.mean(grad_out, 1, keepdims=True)
        - normed * jnp.mean(grad_out * normed, 1, keepdims=True)
    )


def gelu_slope(inputs):
    return 0.5 * (1.0 + lax.erf(inputs * (1.0 / math.sqrt(2.0)))) + inputs * jnp.exp(
        -0.5 * inputs * inputs
    ) * (1.0 / math.sqrt(2.0 * math.pi))


LANES = 128


def lane_pack(width):
    pad = 8
    while pad < width:
        pad *= 2
    return (pad, LANES // pad)


def copies_matrix(width, dtype):
    pad, _ = lane_pack(width)
    feature = lax.broadcasted_iota(jnp.int32, (width, LANES), 0)
    lane = lax.broadcasted_iota(jnp.int32, (width, LANES), 1)
    return jnp.where(lane % pad == feature, 1.0, 0.0).astype(dtype)


def gather_kernel(ids_ref, table_ref, out_ref, rows_ref, stage_ref):
    width, vocab = table_ref.shape
    tokens = ids_ref.shape[2]
    pad, groups = lane_pack(width)
    stride = tokens // groups

    @pl.when(pl.program_id(0) == 0)
    def _():
        chunks = vocab // LANES
        many = 16
        filler = jnp.zeros((pad - width, LANES), full_type)

        def build(start):
            piece = table_ref[:, pl.ds(start, LANES)].astype(half_type).astype(full_type)
            tall = jnp.concatenate([piece, filler] * groups, 0) if pad > width else jnp.concatenate([piece] * groups, 0)
            rows_ref[pl.ds(start, LANES), :] = jnp.transpose(tall)

        def several(block, carry):
            for inner in range(many):
                build(pl.multiple_of((block * many + inner) * LANES, LANES))
            return carry

        lax.fori_loop(0, chunks // many, several, 0)
        for rest in range(chunks // many * many, chunks):
            build(rest * LANES)

    lane_group = lax.broadcasted_iota(jnp.int32, (1, LANES), 1) // pad
    unroll = 16

    def pick(block, carry):
        base = block * unroll
        for inner in range(unroll):
            row = None
            for group in range(groups):
                found = rows_ref[pl.ds(ids_ref[0, 0, group * stride + base + inner], 1), :]
                row = found if row is None else jnp.where(lane_group == group, found, row)
            stage_ref[pl.ds(base + inner, 1), :] = row
        return carry

    lax.fori_loop(0, stride // unroll, pick, 0)
    turned = jnp.transpose(stage_ref[...])
    for group in range(groups):
        out_ref[0, :, group * stride : (group + 1) * stride] = turned[
            group * pad : group * pad + width, :
        ].astype(half_type)


def gather_features(table, ids):
    width, vocab = table.shape
    count, _, tokens = ids.shape
    _, groups = lane_pack(width)
    return pl.pallas_call(
        gather_kernel,
        out_shape=jax.ShapeDtypeStruct((count, width, tokens), half_type),
        grid=(count,),
        in_specs=[
            pl.BlockSpec((1, 1, tokens), lambda i: (i, 0, 0), memory_space=pltpu.SMEM),
            pl.BlockSpec((width, vocab), lambda i: (0, 0), pipeline_mode=pl.Buffered(1)),
        ],
        out_specs=pl.BlockSpec((1, width, tokens), lambda i: (i, 0, 0)),
        scratch_shapes=[
            pltpu.VMEM((vocab, LANES), full_type),
            pltpu.VMEM((tokens // groups, LANES), full_type),
        ],
        compiler_params=pltpu.CompilerParams(
            dimension_semantics=("arbitrary",), vmem_limit_bytes=44 * 1024 * 1024
        ),
    )(ids, table)


def quarter(vocab, groups):
    return -(-vocab // (groups * LANES)) * LANES


def scatter_kernel(places_ref, groups_ref, grad_ref, out_ref, square_ref, mask_ref, stage_ref, *sums):
    width, vocab = out_ref.shape
    runs, _, tokens = places_ref.shape
    pad, groups = lane_pack(width)
    shift = groups.bit_length() - 1
    span = quarter(vocab, groups)

    @pl.when(pl.program_id(0) == 0)
    def _():
        lane_group = lax.broadcasted_iota(jnp.int32, mask_ref.shape, 1) // pad
        mask_ref[...] = jnp.where(
            lane_group == lax.broadcasted_iota(jnp.int32, mask_ref.shape, 0), 1.0, 0.0
        )

        def clear(block, carry):
            start = pl.multiple_of(block * LANES, LANES)
            for total in sums:
                total[pl.ds(start, LANES), :] = jnp.zeros((LANES, LANES), full_type)
            return carry

        lax.fori_loop(0, span // LANES, clear, 0)

    spread = copies_matrix(width, half_type)
    for run in range(runs):
        stage_ref[run] = lax.dot_general(
            grad_ref[run], spread, (((0,), (0,)), ((), ())), preferred_element_type=full_type
        )
    unroll = 32

    def add(block, carry):
        base = block * unroll
        for inner in range(unroll):
            rows = [pl.ds(places_ref[run, 0, base + inner], 1) for run in range(runs)]
            new = [
                sums[run][rows[run], :]
                + stage_ref[run, pl.ds(base + inner, 1), :] * mask_ref[pl.ds(groups_ref[run, 0, base + inner], 1), :]
                for run in range(runs)
            ]
            for run in range(runs):
                sums[run][rows[run], :] = new[run]
        return carry

    lax.fori_loop(0, tokens // unroll, add, 0)

    @pl.when(pl.program_id(0) == pl.num_programs(0) - 1)
    def _():
        def finish(block, squares):
            start = pl.multiple_of(block * LANES, LANES)
            whole = sums[0][pl.ds(start, LANES), :]
            for total in sums[1:]:
                whole = whole + total[pl.ds(start, LANES), :]
            turned = jnp.transpose(whole)
            for group in range(groups):
                column = pl.multiple_of(group * span + start, LANES)

                @pl.when(column < vocab)
                def _():
                    out_ref[:, pl.ds(column, LANES)] = turned[group * pad : group * pad + width, :]

            return squares + jnp.sum((whole * whole).reshape(LANES // 8, 8, LANES), 0)

        square_ref[...] = lax.fori_loop(0, span // LANES, finish, jnp.zeros((8, LANES), full_type))


def scatter_features(grads, places, vocab):
    count, width, tokens = grads.shape
    pad, groups = lane_pack(width)
    runs = 4
    return pl.pallas_call(
        scatter_kernel,
        out_shape=(
            jax.ShapeDtypeStruct((width, vocab), full_type),
            jax.ShapeDtypeStruct((8, LANES), full_type),
        ),
        grid=(count // runs,),
        in_specs=[
            pl.BlockSpec((runs, 1, tokens), lambda i: (i, 0, 0), memory_space=pltpu.SMEM),
            pl.BlockSpec((runs, 1, tokens), lambda i: (i, 0, 0), memory_space=pltpu.SMEM),
            pl.BlockSpec((runs, width, tokens), lambda i: (i, 0, 0)),
        ],
        out_specs=(
            pl.BlockSpec((width, vocab), lambda i: (0, 0)),
            pl.BlockSpec((8, LANES), lambda i: (0, 0)),
        ),
        scratch_shapes=[
            pltpu.VMEM((max(8, groups), LANES), full_type),
            pltpu.VMEM((runs, tokens, LANES), full_type),
        ]
        + [pltpu.VMEM((quarter(vocab, groups), LANES), full_type) for _ in range(runs)],
        compiler_params=pltpu.CompilerParams(
            dimension_semantics=("arbitrary",), vmem_limit_bytes=52 * 1024 * 1024
        ),
    )(places[0], places[1], grads)


def scatter_places(ids, width, vocab):
    _, groups = lane_pack(width)
    span = quarter(vocab, groups)
    return (ids % span, ids // span)


def turn_tables(row_length, head_width):
    halfway = ROT // 2
    dims = jnp.arange(LANES) % head_width
    inverse = 10000.0 ** (-2.0 * (dims % halfway).astype(full_type) / ROT)
    angles = jnp.arange(row_length, dtype=full_type)[:, None] * inverse[None, :]
    cosine = jnp.where(dims < ROT, jnp.cos(angles), 1.0)
    above = jnp.where(dims < halfway, -jnp.sin(angles), 0.0)
    below = jnp.where((dims >= halfway) & (dims < ROT), jnp.sin(angles), 0.0)
    return jnp.stack([cosine, above, below], 0)


def turned(values_in, tables_ref, forward):
    halfway = ROT // 2
    higher = pltpu.roll(values_in, LANES - halfway, 1) * tables_ref[1]
    lower = pltpu.roll(values_in, halfway, 1) * tables_ref[2]
    straight = values_in * tables_ref[0]
    return straight + (higher + lower) if forward else straight - (higher + lower)


def dot_of(left, right, dims):
    return lax.dot_general(left, right, (dims, ((), ())), preferred_element_type=full_type)


def key_window(block, block_rows):
    return (block + 1) * block_rows


def allowed_block(row_ref, column_ref, block, block_rows):
    reach = key_window(block, block_rows)
    start = block * block_rows
    key_place = lax.broadcasted_iota(jnp.int32, (reach, block_rows), 0)
    query_place = start + lax.broadcasted_iota(jnp.int32, (reach, block_rows), 1)
    same = column_ref[0, :reach, :] == row_ref[0, :, start : start + block_rows]
    return (key_place <= query_place) & same


def forward_kernel(
    query_in, key_in, value_in, tables_ref, row_ref, column_ref, context_ref, query_ref, key_ref, value_ref, logsum_ref
):
    row_length = query_in.shape[0]
    head_width = LANES // 2
    block_rows = row_length // 2
    scale = 1.0 / math.sqrt(head_width)
    query_ref[...] = turned(query_in[...], tables_ref, True).astype(half_type)
    key_ref[...] = turned(key_in[...], tables_ref, True).astype(half_type)
    value_ref[...] = value_in[...].astype(half_type)
    for block in range(2):
        start = block * block_rows
        reach = key_window(block, block_rows)
        allowed = allowed_block(row_ref, column_ref, block, block_rows)
        for head in range(2):
            lanes = slice(head * head_width, (head + 1) * head_width)
            scores = dot_of(key_ref[:reach, lanes], query_ref[start : start + block_rows, lanes], ((1,), (1,)))
            scores = jnp.where(allowed, scores * scale, -1e30)
            peak = jnp.max(scores, 0, keepdims=True)
            powers = jnp.exp(scores - peak)
            total = jnp.sum(powers, 0, keepdims=True)
            logsum_ref[0, 0, head : head + 1, start : start + block_rows] = peak + jnp.log(total)
            weights_soft = (powers * (1.0 / total)).astype(half_type)
            context_ref[start : start + block_rows, lanes] = dot_of(
                weights_soft, value_ref[:reach, lanes], ((0,), (0,))
            ).astype(half_type)


def attention_specs(row_length, pairs):
    def part(offset):
        return pl.BlockSpec((row_length, LANES), lambda m, h: (m, offset * pairs + h))

    tables = pl.BlockSpec((3, row_length, LANES), lambda m, h: (0, 0, 0))
    row = pl.BlockSpec((1, 1, row_length), lambda m, h: (m, 0, 0))
    column = pl.BlockSpec((1, row_length, 1), lambda m, h: (m, 0, 0))
    logsum = pl.BlockSpec((1, 1, 2, row_length), lambda m, h: (m, h, 0, 0))
    return (part, tables, row, column, logsum)


def attention_forward(mixed, tables, segments):
    micro_count, row_length = segments.shape
    tokens = mixed.shape[0]
    width = mixed.shape[1] // 3
    pairs = width // LANES
    part, tables_spec, row, column, logsum = attention_specs(row_length, pairs)
    flat = jax.ShapeDtypeStruct((tokens, width), half_type)
    return pl.pallas_call(
        forward_kernel,
        out_shape=(flat, flat, flat, flat, jax.ShapeDtypeStruct((micro_count, pairs, 2, row_length), full_type)),
        grid=(micro_count, pairs),
        in_specs=[part(0), part(1), part(2), tables_spec, row, column],
        out_specs=(part(0), part(0), part(0), part(0), logsum),
        compiler_params=pltpu.CompilerParams(
            dimension_semantics=("arbitrary", "arbitrary"), vmem_limit_bytes=40 * 1024 * 1024
        ),
    )(mixed, mixed, mixed, tables, segments[:, None, :], segments[:, :, None])


def backward_kernel(
    query_ref, key_ref, value_ref, grad_ref, tables_ref, row_ref, column_ref, logsum_ref, out_ref, query_sum, key_sum, value_sum
):
    row_length = query_ref.shape[0]
    head_width = LANES // 2
    block_rows = row_length // 2
    scale = 1.0 / math.sqrt(head_width)
    for block in reversed(range(2)):
        start = block * block_rows
        reach = key_window(block, block_rows)
        rows = slice(start, start + block_rows)
        allowed = allowed_block(row_ref, column_ref, block, block_rows)
        for head in range(2):
            lanes = slice(head * head_width, (head + 1) * head_width)
            query = query_ref[rows, lanes]
            key = key_ref[:reach, lanes]
            grad = grad_ref[rows, lanes]
            scores = jnp.where(allowed, dot_of(key, query, ((1,), (1,))) * scale, -1e30)
            weights_soft = jnp.exp(scores - logsum_ref[0, 0, head : head + 1, rows])
            grad_value = dot_of(weights_soft.astype(half_type), grad, ((1,), (0,)))
            grad_weights = dot_of(value_ref[:reach, lanes], grad, ((1,), (1,)))
            leaning = jnp.sum(weights_soft * grad_weights, 0, keepdims=True)
            grad_scores = (weights_soft * (grad_weights - leaning)).astype(half_type)
            query_sum[rows, lanes] = dot_of(grad_scores, key, ((0,), (0,))) * scale
            grad_key = dot_of(grad_scores, query, ((1,), (0,))) * scale
            if block == 1:
                value_sum[:, lanes] = grad_value
                key_sum[:, lanes] = grad_key
            else:
                value_sum[:reach, lanes] = value_sum[:reach, lanes] + grad_value
                key_sum[:reach, lanes] = key_sum[:reach, lanes] + grad_key
    out_ref[0] = turned(query_sum[...], tables_ref, False).astype(half_type)
    out_ref[1] = turned(key_sum[...], tables_ref, False).astype(half_type)
    out_ref[2] = value_sum[...].astype(half_type)


def attention_backward(queries, keys_all, values_all, grad_context, logsum, tables, segments):
    micro_count, row_length = segments.shape
    tokens, width = queries.shape
    pairs = width // LANES
    part, tables_spec, row, column, logsum_spec = attention_specs(row_length, pairs)
    return pl.pallas_call(
        backward_kernel,
        out_shape=jax.ShapeDtypeStruct((3, tokens, width), half_type),
        grid=(micro_count, pairs),
        in_specs=[part(0), part(0), part(0), part(0), tables_spec, row, column, logsum_spec],
        out_specs=pl.BlockSpec((3, row_length, LANES), lambda m, h: (0, m, h)),
        scratch_shapes=[pltpu.VMEM((row_length, LANES), full_type) for _ in range(3)],
        compiler_params=pltpu.CompilerParams(
            dimension_semantics=("arbitrary", "arbitrary"), vmem_limit_bytes=40 * 1024 * 1024
        ),
    )(queries, keys_all, values_all, grad_context, tables, segments[:, None, :], segments[:, :, None], logsum)


def document_kernel(
    starts_ref, total_ref, in_ref, out_ref, other_ref, own_ref, turned_ref, shift_ref, window_ref
):
    micro_count, docs = starts_ref.shape[0], starts_ref.shape[1] - 1
    row_length = in_ref.shape[0] // micro_count
    reach = row_length // 2
    step = 16
    half = other_ref.shape[0]
    places = [(micro, doc) for micro in range(micro_count) for doc in range(docs)]

    def bounds(micro, doc):
        start, end = starts_ref[micro, doc], starts_ref[micro, doc + 1]
        window = jnp.minimum((start // step) * step, row_length - reach)
        base = pl.multiple_of(micro * row_length + window, step)
        return (start - window, end - window, base)

    @pl.when(pl.program_id(0) == 0)
    def _():
        row = lax.broadcasted_iota(jnp.int32, (reach, in_ref.shape[1]), 0)
        for place, (micro, doc) in enumerate(places):
            begin, end, base = bounds(micro, doc)

            @pl.when(end <= reach)
            def _():
                rows = in_ref[pl.ds(base, reach), :].astype(full_type)
                kept = jnp.where((row >= begin) & (row < end), rows, 0.0)
                turned_ref[place] = jnp.transpose(kept).astype(half_type)

            @pl.when(end > reach)
            def _():
                to = lax.broadcasted_iota(jnp.int32, (reach, reach + step), 0)
                source = lax.broadcasted_iota(jnp.int32, (reach, reach + step), 1)
                shift_ref[place] = jnp.where(to + begin == source, 1.0, 0.0).astype(half_type)
                rows = dot_of(shift_ref[place], in_ref[pl.ds(base, reach + step), :], ((1,), (0,)))
                kept = jnp.where(row < end - begin, rows, 0.0)
                turned_ref[place] = jnp.transpose(kept).astype(half_type)

    for place, (micro, doc) in enumerate(places):
        begin, end, base = bounds(micro, doc)

        @pl.when(end <= reach)
        def _():
            window_ref[place] = out_ref[pl.ds(base, reach), :]

        @pl.when(end > reach)
        def _():
            window_ref[place] = dot_of(
                shift_ref[place], out_ref[pl.ds(base, reach + step), :], ((1,), (0,))
            ).astype(half_type)

    total = total_ref[0]
    parts = 2
    rows = half // parts
    for part in range(2 * parts):
        found = None
        for place in range(len(places)):
            block = dot_of(
                turned_ref[place, part * rows : (part + 1) * rows, :], window_ref[place], ((1,), (0,))
            )
            block = (block * total).astype(half_type).astype(full_type)
            found = block * block if found is None else found + block * block
        target = other_ref if part < parts else own_ref
        start = (part % parts) * rows
        target[start : start + rows, :] = found


def document_squares(rot_in, rot_out, segments, total):
    micro_count, row_length = segments.shape
    tokens, width = rot_in.shape
    hidden = rot_out.shape[1]
    tile = 2 * LANES
    slots = jnp.arange(DOCS + 1)
    starts = jnp.sum(segments[:, :, None] < slots[None, None, :], 1).astype(jnp.int32)
    return pl.pallas_call(
        document_kernel,
        out_shape=(jax.ShapeDtypeStruct((width // 2, hidden), full_type),) * 2,
        grid=(hidden // tile,),
        in_specs=[
            pl.BlockSpec(memory_space=pltpu.SMEM),
            pl.BlockSpec(memory_space=pltpu.SMEM),
            pl.BlockSpec((tokens, width), lambda i: (0, 0)),
            pl.BlockSpec((tokens, tile), lambda i: (0, i)),
        ],
        out_specs=(pl.BlockSpec((width // 2, tile), lambda i: (0, i)),) * 2,
        scratch_shapes=[
            pltpu.VMEM((micro_count * DOCS, width, row_length // 2), half_type),
            pltpu.VMEM((micro_count * DOCS, row_length // 2, row_length // 2 + 16), half_type),
            pltpu.VMEM((micro_count * DOCS, row_length // 2, tile), half_type),
        ],
        compiler_params=pltpu.CompilerParams(
            dimension_semantics=("arbitrary",), vmem_limit_bytes=40 * 1024 * 1024
        ),
    )(starts, total.reshape(1), rot_in, rot_out)


AXES = ("dp", "fsdp")


def partner_pairs(count, bit):
    return [(place, place ^ (1 << bit)) for place in range(count)]


class Stream:
    def __init__(self, chunks, order, left, wire, relative=False):
        self.held = chunks.reshape((2,) * len(order) + chunks.shape[1:])
        self.left = list(left)
        self.order = list(order)
        self.wire = wire
        self.relative = relative
        self.sent = self.kept = self.got = None

    def land(self, arrived):
        self.held = self.kept + arrived.astype(full_type)
        self.got = None
        return [self]

    def split(self):
        bit = self.order[0]
        axis = self.left.index(bit)
        mine = 0 if self.relative else (lax.axis_index(AXES) >> bit) & 1
        self.sent = lax.dynamic_index_in_dim(self.held, 1 - mine, axis, keepdims=False).astype(self.wire)
        self.kept = lax.dynamic_index_in_dim(self.held, mine, axis, keepdims=False)
        self.left.pop(axis)

    def send(self, ready):
        self.got = lax.ppermute(ready, AXES, partner_pairs(lax.axis_size(AXES), self.order.pop(0)))


class FirstStep:
    def __init__(self, other, own, rows, wire):
        self.sent, self.kept, self.rows, self.wire = other, own, rows, wire
        self.order = [0]
        self.got = None
        self.streams = None

    def land(self, arrived):
        held = (self.kept + arrived).reshape(-1, self.rows, self.kept.shape[1])
        half = held.shape[2] // 2
        bits = lax.axis_size(AXES).bit_length() - 1
        order_a, order_b = link_orders(bits)
        left = range(bits - 1, 0, -1)
        self.got = None
        self.streams = [
            Stream(held[:, :, :half], order_a[1:], left, self.wire),
            Stream(held[:, :, half:], order_b[1:], left, self.wire),
        ]
        return self.streams

    def split(self):
        pass

    def send(self, ready):
        self.order = []
        self.got = lax.ppermute(ready, AXES, partner_pairs(lax.axis_size(AXES), 0))

    def finished(self):
        return jnp.concatenate([stream.held for stream in self.streams], 1)


def advance(anchor, live):
    flying = [stream for stream in live if stream.got is not None]
    anchor, landed = lax.optimization_barrier((anchor, [stream.got for stream in flying]))
    going = [stream for stream in live if stream.got is None]
    for stream, arrived in zip(flying, landed):
        going.extend(stream.land(arrived))
    going = [stream for stream in going if stream.order]
    for stream in going:
        stream.split()
    anchor, ready = lax.optimization_barrier((anchor, [stream.sent for stream in going]))
    for stream, block in zip(going, ready):
        stream.send(block)
    live[:] = going
    return anchor


def run_all(anchor, live):
    while live:
        anchor = advance(anchor, live)
    return anchor


def pair_first(width, rows, place):
    to = lax.broadcasted_iota(jnp.int32, (width, width), 1)
    source = lax.broadcasted_iota(jnp.int32, (width, width), 0)
    core = jnp.where(to < width // 2, 1 - (place & 1), place & 1)
    inside = to % (width // 2)
    wanted = (inside // rows) * (2 * rows) + core * rows + inside % rows
    return (source == wanted).astype(half_type)


def link_orders(bits):
    near = list(range(1, bits - 2))
    return ([0, bits - 2, bits - 1] + near, [0, bits - 1, bits - 2] + near)


def flipped(folded, place):
    bits = lax.axis_size(AXES).bit_length() - 1
    for axis in range(bits):
        mine = (place >> (bits - 1 - axis)) & 1
        folded = jnp.where(mine == 1, jnp.flip(folded, axis), folded)
    return folded


def by_device(stacked, order, place):
    bits = len(order)
    folded = stacked.reshape((2,) * bits + stacked.shape[1:])
    natural = [order.index(bit) for bit in range(bits - 1, -1, -1)]
    folded = jnp.transpose(folded, natural + list(range(bits, folded.ndim)))
    return flipped(folded, place).reshape(stacked.shape)


def by_partner(ordered, order, place):
    bits = len(order)
    folded = flipped(ordered.reshape((2,) * bits + ordered.shape[1:]), place)
    stacked = [bits - 1 - bit for bit in order]
    folded = jnp.transpose(folded, stacked + list(range(bits, folded.ndim)))
    return folded.reshape(ordered.shape)


def gather_trees(blocks, orders):
    held = [block[None] for block in blocks]
    for step in range(len(orders[0])):
        for m, order in enumerate(orders):
            count = 1 << len(order)
            arrived = lax.ppermute(held[m], AXES, partner_pairs(count, order[-1 - step]))
            held[m] = jnp.concatenate([held[m], arrived], 0)
    return held


def shared_by_all(own, count):
    return lax.all_to_all(
        jnp.broadcast_to(own[None], (count,) + own.shape), AXES, split_axis=0, concat_axis=0, tiled=True
    )


def adam_update(weight, gradient, moment_one, moment_two, rate, step_value):
    next_one = decay_first * moment_one + (1.0 - decay_first) * gradient
    next_two = decay_second * moment_two + (1.0 - decay_second) * gradient * gradient
    fix_one = 1.0 - decay_first**step_value
    fix_two = 1.0 - decay_second**step_value
    update = next_one / fix_one / (jnp.sqrt(next_two / fix_two) + adam_epsilon)
    return [weight - rate * (update + weight_decay * weight), next_one, next_two]


def per_device(
    step_count,
    token_ids,
    segment_ids,
    loss_positions,
    label_ids,
    label_mask,
    embed_in,
    embed_in_first,
    embed_in_second,
    embed_out,
    embed_out_first,
    embed_out_second,
    proj_in,
    proj_in_first,
    proj_in_second,
    proj_up,
    proj_up_first,
    proj_up_second,
    proj_mix,
    proj_mix_first,
    proj_mix_second,
    vector_params,
    vector_first,
    vector_second,
    basis_in,
    basis_out,
):
    micro_count = token_ids.shape[0]
    row_length = token_ids.shape[2]
    pick_count = loss_positions.shape[2]
    tokens = micro_count * row_length
    count = lax.axis_size(AXES)
    total = jnp.maximum(jnp.sum(label_mask.astype(full_type)), 1.0)
    vocab = embed_in.shape[1]
    own_width = embed_in.shape[0]
    width = proj_mix.shape[1]
    hidden = proj_up.shape[1]
    head_width = width // HEADS

    place = lax.axis_index(AXES)
    flat_ids = jnp.transpose(token_ids, (1, 0, 2)).reshape(-1)
    ids_by_run = flat_ids.reshape(count, 1, tokens)
    columns = gather_features(embed_in, ids_by_run)
    arrived = lax.all_to_all(columns, AXES, split_axis=0, concat_axis=0, tiled=True)
    embedded = arrived.reshape(width, tokens).T.astype(full_type)
    places = scatter_places(ids_by_run, own_width, vocab)

    small = vector_params.astype(half_type).reshape(own_width, -1)
    each = small.shape[1]
    small = jnp.pad(small, ((0, 0), (0, -each % LANES)))
    both = jnp.concatenate([proj_in.astype(half_type), proj_up.astype(half_type), small], 1)
    both = lax.all_gather(both, AXES, axis=0, tiled=True)
    weight_in, weight_up = both[:, : 3 * width], both[:, 3 * width : 3 * width + hidden]
    weight_mix = lax.all_gather(proj_mix.astype(half_type), AXES, axis=0, tiled=True)
    vector = both[:, 3 * width + hidden : 3 * width + hidden + each].reshape(-1).astype(full_type)
    pairing = pair_first(width, own_width, place)
    basis_paired = jnp.dot(basis_in, pairing, preferred_element_type=full_type).astype(half_type)
    (
        bias_in,
        bias_up,
        bias_mix,
        shift_first,
        shift_second,
        shift_last,
        gain_first,
        gain_second,
        gain_last,
    ) = split_vector(vector, width, hidden)

    segments = segment_ids[:, 0]
    picks = loss_positions[:, 0] + row_length * jnp.arange(micro_count)[:, None]
    picks = picks.reshape(-1)

    normed, inv_std = normalize(embedded)
    first_in = (normed * gain_first + shift_first).astype(half_type)
    second_in = (normed * gain_second + shift_second).astype(half_type)
    mixed = jnp.dot(first_in, weight_in, preferred_element_type=full_type) + bias_in
    tables = turn_tables(row_length, head_width)
    context, queries, keys_all, values_all, logsum = attention_forward(mixed, tables, segments)
    hidden_pre = jnp.dot(second_in, weight_up, preferred_element_type=full_type) + bias_up
    active = (hidden_pre * (0.5 + 0.5 * lax.erf(hidden_pre * (1.0 / math.sqrt(2.0))))).astype(half_type)
    joined = jnp.concatenate([context, active], 1)
    residual = embedded + jnp.dot(joined, weight_mix, preferred_element_type=full_type) + bias_mix
    normed_last, inv_last = normalize(residual)
    final = normed_last * gain_last + shift_last
    picked = jnp.take(final, picks, axis=0, mode="clip").astype(half_type)

    bits = count.bit_length() - 1
    orders = link_orders(bits)
    picked = picked.reshape(micro_count, pick_count, width)
    gathered = jnp.stack(gather_trees(picked, orders)).reshape(-1, width)
    table_out = embed_out.astype(half_type)
    vocab_rows = embed_out.shape[0]
    vocab_ids = place * vocab_rows + jnp.arange(vocab_rows)
    labels_flat = jnp.stack([by_partner(label_ids[m], orders[m], place) for m in range(micro_count)]).reshape(-1)
    mask_flat = jnp.stack([by_partner(label_mask[m], orders[m], place) for m in range(micro_count)]).reshape(-1)
    mask_flat = mask_flat.astype(full_type)
    logits = jnp.einsum("rd,vd->rv", gathered, table_out, preferred_element_type=full_type)
    matches = labels_flat[:, None] == vocab_ids[None, :]
    label_part = jnp.sum(jnp.where(matches, logits, 0.0), 1)
    local_max = jnp.max(logits, 1)
    local_sum = jnp.sum(jnp.exp(logits - local_max[:, None]), 1)
    parts = jnp.stack([local_max, local_sum, label_part], 0).reshape(3, micro_count, count, pick_count)
    parts = jnp.transpose(parts, (1, 2, 0, 3))
    parts = jnp.stack([by_device(parts[m], orders[m], place) for m in range(micro_count)], 1)
    parts = lax.all_to_all(
        parts.reshape(count, 1, -1), AXES, split_axis=0, concat_axis=0, tiled=True
    ).reshape(count, micro_count, 3, pick_count)
    peak = jnp.max(parts[:, :, 0], 0)
    own_logsum = peak + jnp.log(jnp.sum(parts[:, :, 1] * jnp.exp(parts[:, :, 0] - peak[None]), 0))
    own_mask = lax.dynamic_index_in_dim(label_mask, place, 1, keepdims=False).astype(full_type)
    loss_part = jnp.sum(own_mask * (own_logsum - jnp.sum(parts[:, :, 2], 0))) / total
    logsum_all = shared_by_all(own_logsum.reshape(1, -1), count).reshape(count, micro_count, pick_count)
    logsum_all = jnp.stack([by_partner(logsum_all[:, m], orders[m], place) for m in range(micro_count)]).reshape(-1)
    grad_logits = (
        (jnp.exp(logits - logsum_all[:, None]) - matches.astype(full_type))
        * (mask_flat / total)[:, None]
    ).astype(half_type)
    back = jnp.dot(grad_logits, table_out, preferred_element_type=full_type)
    back = back.reshape(micro_count, count, pick_count, width)
    pick_streams = [
        Stream(back[m], orders[m], orders[m], full_type, relative=True) for m in range(micro_count)
    ]
    live = list(pick_streams)
    grad_logits = advance(grad_logits, live)
    grad_out_table = jnp.einsum("rv,rd->vd", grad_logits, gathered, preferred_element_type=full_type)
    out_squares = jnp.sum(grad_out_table * grad_out_table)
    second_paired, out_squares = advance((second_in, out_squares), live)
    rot_in = jnp.dot(second_paired, basis_paired, preferred_element_type=full_type).astype(half_type)
    first_turned = lax.dot_general(
        pairing, first_in, (((0,), (1,)), ((), ())), preferred_element_type=full_type
    ).astype(half_type)
    rot_in, first_turned = advance((rot_in, first_turned), live)
    run_all(jnp.zeros((), full_type), live)
    grad_picked = jnp.concatenate([stream.held for stream in pick_streams], 0)

    grad_final = jnp.zeros((tokens, width), full_type).at[picks].add(grad_picked)
    grad_residual = norm_back(grad_final * gain_last, normed_last, inv_last)
    grad_branch = grad_residual.astype(half_type)
    grad_mix = jnp.einsum("sa,sb->ab", joined, grad_branch, preferred_element_type=full_type)
    grad_branch, grad_mix = lax.optimization_barrier((grad_branch, grad_mix))
    own_mix = lax.psum_scatter(grad_mix, AXES, scatter_dimension=0, tiled=True)
    grad_joined = jnp.einsum("sb,ab->sa", grad_branch, weight_mix, preferred_element_type=full_type)
    grad_context = grad_joined[:, :width].astype(half_type)
    grad_parts = attention_backward(
        queries, keys_all, values_all, grad_context, logsum, tables, segments
    )
    grad_mixed = jnp.concatenate([grad_parts[0], grad_parts[1], grad_parts[2]], 1)
    in_other = jnp.dot(first_turned[: width // 2], grad_mixed, preferred_element_type=full_type)
    in_own = jnp.dot(first_turned[width // 2 :], grad_mixed, preferred_element_type=full_type)
    in_step = FirstStep(in_other, in_own, own_width, full_type)
    live = [in_step]
    grad_joined = advance(grad_joined, live)
    grad_hidden = (grad_joined[:, width:] * gelu_slope(hidden_pre)).astype(half_type)
    grad_hidden = advance(grad_hidden, live)
    grad_up = jnp.einsum("sa,sb->ab", second_in, grad_hidden, preferred_element_type=full_type)
    grad_second = jnp.einsum("sb,ab->sa", grad_hidden, weight_up, preferred_element_type=full_type)
    grad_up, grad_second, grad_mixed = advance((grad_up, grad_second, grad_mixed), live)
    own_up = lax.psum_scatter(grad_up, AXES, scatter_dimension=0, tiled=True)
    grad_first = jnp.einsum("sb,ab->sa", grad_mixed, weight_in, preferred_element_type=full_type)
    grad_embedded = grad_residual + norm_back(
        grad_first * gain_first + grad_second * gain_second, normed, inv_std
    )
    vector_grad = jnp.concatenate(
        [
            jnp.sum(grad_mixed.astype(full_type), 0),
            jnp.sum(grad_hidden.astype(full_type), 0),
            jnp.sum(grad_residual, 0),
            jnp.sum(grad_first, 0),
            jnp.sum(grad_second, 0),
            jnp.sum(grad_final, 0),
            jnp.sum(grad_first * normed, 0),
            jnp.sum(grad_second * normed, 0),
            jnp.sum(grad_final * normed_last, 0),
        ]
    )
    sending = grad_embedded.astype(half_type).T.reshape(count, own_width, tokens)
    sending, grad_hidden_late, vector_grad = advance((sending, grad_hidden, vector_grad), live)
    returned = lax.all_to_all(sending, AXES, split_axis=0, concat_axis=0, tiled=True)
    vector_parts = lax.all_to_all(
        vector_grad.reshape(count, 1, -1), AXES, split_axis=0, concat_axis=0, tiled=True
    )

    rot_out = jnp.dot(grad_hidden_late, basis_out, preferred_element_type=full_type).astype(half_type)
    rot_out, vector_parts = lax.optimization_barrier((rot_out, vector_parts))
    scale_other, scale_own = document_squares(rot_in, rot_out, segments, total)
    scale_step = FirstStep(scale_other, scale_own, own_width, half_type)
    scale_live = [scale_step]
    returned = advance(returned, live)
    returned = advance(returned, scale_live)
    own_vector = jnp.sum(vector_parts, (0, 1))
    grad_in_table, in_squares = scatter_features(returned, places, vocab)
    in_squares = run_all(in_squares, live)
    own_in = in_step.finished()
    grads = (grad_in_table, grad_out_table, own_in, own_up, own_mix, own_vector)
    squares = jnp.sum(in_squares) + out_squares
    squares = squares + sum((jnp.sum(gradient * gradient) for gradient in grads[2:]))
    both = jnp.sum(shared_by_all(jnp.stack([squares, loss_part])[None], count), (0, 1))
    advance(jnp.zeros((), full_type), scale_live)
    both = advance(both, scale_live)
    grad_norm = jnp.sqrt(both[0])
    loss_value = both[1]
    factor = jnp.minimum(1.0, clip_limit / (grad_norm + 1e-06))
    step_value = step_count[0].astype(full_type)
    weights = (embed_in, embed_out, proj_in, proj_up, proj_mix, vector_params)
    firsts = (
        embed_in_first,
        embed_out_first,
        proj_in_first,
        proj_up_first,
        proj_mix_first,
        vector_first,
    )
    seconds = (
        embed_in_second,
        embed_out_second,
        proj_in_second,
        proj_up_second,
        proj_mix_second,
        vector_second,
    )
    updates = []
    for index, (weight, moment_one, moment_two, rate) in enumerate(zip(weights, firsts, seconds, step_rates)):
        gradient = grads[index]
        if index in (1, 2):
            updates[-1], gradient = advance((updates[-1], gradient), scale_live)
        updates.append(adam_update(weight, gradient * factor, moment_one, moment_two, rate, step_value))
    run_all(loss_value, scale_live)
    eigen_scales = scale_step.finished() / float(micro_count * count * DOCS)
    results = [value for update in updates for value in update]
    return tuple(results) + (loss_value, grad_norm, eigen_scales)


def solution(mesh):
    in_specs = (
        P(),
        P(),
        P(None, ("dp", "fsdp"), None),
        P(None, ("dp", "fsdp"), None),
        P(),
        P(),
        P(("dp", "fsdp"), None),
        P(("dp", "fsdp"), None),
        P(("dp", "fsdp"), None),
        P(("dp", "fsdp"), None),
        P(("dp", "fsdp"), None),
        P(("dp", "fsdp"), None),
        P(("dp", "fsdp"), None),
        P(("dp", "fsdp"), None),
        P(("dp", "fsdp"), None),
        P(("dp", "fsdp"), None),
        P(("dp", "fsdp"), None),
        P(("dp", "fsdp"), None),
        P(("dp", "fsdp"), None),
        P(("dp", "fsdp"), None),
        P(("dp", "fsdp"), None),
        P(("dp", "fsdp")),
        P(("dp", "fsdp")),
        P(("dp", "fsdp")),
        P(),
        P(),
    )
    out_specs = (
        P(("dp", "fsdp"), None),
        P(("dp", "fsdp"), None),
        P(("dp", "fsdp"), None),
        P(("dp", "fsdp"), None),
        P(("dp", "fsdp"), None),
        P(("dp", "fsdp"), None),
        P(("dp", "fsdp"), None),
        P(("dp", "fsdp"), None),
        P(("dp", "fsdp"), None),
        P(("dp", "fsdp"), None),
        P(("dp", "fsdp"), None),
        P(("dp", "fsdp"), None),
        P(("dp", "fsdp"), None),
        P(("dp", "fsdp"), None),
        P(("dp", "fsdp"), None),
        P(("dp", "fsdp")),
        P(("dp", "fsdp")),
        P(("dp", "fsdp")),
        P(),
        P(),
        P(("dp", "fsdp"), None),
    )
    return jax.shard_map(
        per_device, mesh=mesh, in_specs=in_specs, out_specs=out_specs, check_vma=False
    )
```
